32 devices in a mesh: disp: 8 (over y, x, core), col: 4 (over z).
Axes of the slice: x: 2, y: 2, z: 4, core: 2. Of those that a mesh axis runs over, the one named last changes fastest.
Arguments:
- left_feat: bfloat16 [320, 2, 1024], P('disp', None, 'col'), may hold values from -6 to 6
- right_feat: bfloat16 [320, 2, 1024], P('disp', None, 'col'), may hold values from -6 to 6
- conv1_w: bfloat16 [32, 40, 3, 3, 3], replicated, may hold values from -0.25 to 0.25
- conv2_w: bfloat16 [32, 32, 3, 3, 3], replicated, may hold values from -0.3125 to 0.3125
- conv3_w: bfloat16 [32, 32, 3, 3, 3], replicated, may hold values from -0.3125 to 0.3125
- head_w: float32 [32], replicated, may hold values from -120 to 120
Outputs:
- warped: bfloat16 [320, 2, 1024], P('disp', None, 'col')
- disparity: float32 [2, 1024], P(None, 'col')
The draws below stay inside these ranges and needn't reach their ends.
All inputs are finite; a program needn't handle non-finite values.
Results may differ from the reference program's by a relative error of at most 0.015.
The reference program's roundings to bfloat16 on the way count: a program that leaves them out, or rounds other values in their place, can miss the bound.
Values may be sent and summed in bfloat16 or wider, within the bound.
No kernel may reach another device: no remote copies, remote signals or barrier semaphores. Data moves between devices by JAX's collectives and lax.ppermute only.
A program may use at most 64 MiB of HBM per device.

```python
import jax
import jax.numpy as jnp
from jax import lax

C = 320
G = 40
F = 32
H = 2
CG = 8
DISP = 128
W = 1024


def draw_head_w(key, part):
    values = jnp.clip(2.0 * jax.random.normal(key, (F,), jnp.float32), -8.0, 8.0)
    return values


def shard_levels(stream_key, dims, cuts, smallest, high):
    gain, own = 1.0, jax.random.fold_in(stream_key, 6)
    for position, shards_of in cuts:
        draws = jnp.exp(jax.random.uniform(jax.random.fold_in(own, position), (shards_of,), jnp.float32, smallest / len(cuts), high / len(cuts)))
        gain = gain * jnp.repeat(draws, dims[position] // shards_of).reshape([-1 if axis == position else 1 for axis in range(len(dims))])
    return gain


def normal_values(own_key, shape, deviation, bound, shards=(), kind=jnp.bfloat16):
    level = shard_levels(own_key, shape, shards, -0.22, 0.18) if shards else 1.0
    entries = jax.random.normal(own_key, shape, jnp.float32) * deviation * level
    return jnp.minimum(jnp.maximum(entries, -bound), bound).astype(kind)


def setup_inputs(seed: int = 0) -> dict:
    key_of = jax.random.split(jax.random.key(seed), 7)
    return {
        "left_feat": normal_values(key_of[0], (C, H, W), 1.0, 6.0, ((0, 8), (2, 4))),
        "right_feat": normal_values(key_of[1], (C, H, W), 1.0, 6.0, ((0, 8), (2, 4))),
        "conv1_w": normal_values(key_of[2], (F, G, 3, 3, 3), (G * 27 // 2) ** -0.5, 0.25),
        "conv2_w": normal_values(key_of[3], (F, F, 3, 3, 3), (F * 27 // 2) ** -0.5, 0.3125),
        "conv3_w": normal_values(key_of[4], (F, F, 3, 3, 3), (F * 27 // 2) ** -0.5, 0.3125),
        "head_w": draw_head_w(jax.random.fold_in(key_of[6], 71), 0),
    }


masked_value = -1.0e30


def convolve(activity, kernel):
    output = lax.conv_general_dilated(activity[None], kernel, (1, 1, 1), "SAME", dimension_numbers=("NCDHW", "OIDHW", "NCDHW"), preferred_element_type=jnp.float32)
    return jnp.maximum(output[0], 0.0)


def reference(left_feat, right_feat, conv1_w, conv2_w, conv3_w, head_w):
    padded_right = jnp.concatenate([jnp.zeros((C, H, DISP), right_feat.dtype), right_feat], axis=2)

    def correlate(offset):
        shifted = lax.dynamic_slice_in_dim(padded_right, (DISP - offset).astype(jnp.int32), W, 2)
        product = left_feat.astype(jnp.float32) * shifted.astype(jnp.float32)
        return (jnp.sum(product.reshape(G, CG, H, W), axis=1) / CG).astype(jnp.bfloat16)

    volume = jnp.moveaxis(lax.map(correlate, jnp.arange(DISP, dtype=jnp.int32)), 0, 1)
    activity = convolve(volume, conv1_w).astype(jnp.bfloat16)
    activity = convolve(activity, conv2_w).astype(jnp.bfloat16)
    activity = convolve(activity, conv3_w)
    scores = jnp.sum(head_w[:, None, None, None] * activity, axis=0)
    valid_mask = jnp.arange(W)[None, None, :] >= jnp.arange(DISP)[:, None, None]
    scores = jnp.where(valid_mask, scores, masked_value)
    top_score = jnp.max(scores, axis=0)
    weighting = jnp.where(valid_mask, jnp.exp(scores - top_score[None]), 0.0)
    denominator = jnp.sum(weighting, axis=0)
    disp_values = jnp.arange(DISP).astype(jnp.float32)[:, None, None]
    disp_sum = jnp.sum(weighting * disp_values, axis=0)

    def add_term(offset, running):
        shifted = lax.dynamic_slice_in_dim(padded_right, (DISP - offset).astype(jnp.int32), W, 2)
        weight = lax.dynamic_index_in_dim(weighting, offset, 0, keepdims=False)
        return running + weight[None] * shifted.astype(jnp.float32)

    numerator = lax.fori_loop(0, DISP, add_term, jnp.zeros((C, H, W), jnp.float32))
    warped = (numerator / denominator[None]).astype(jnp.bfloat16)
    return (warped, disp_sum / denominator / DISP)
```

```python
import functools

import jax
import jax.numpy as jnp
from jax import lax
from jax.experimental import pallas as pl
from jax.experimental.pallas import tpu as pltpu
from jax.sharding import PartitionSpec as P

DG = 16
CG = 8
LANES = 128
KROWS = 256

masked_value = -1e30


def round_up(value, unit):
    return -(-value // unit) * unit


class Dims:
    def __init__(self, left, conv1, conv2, groups_disp, strips):
        own, self.h, self.strip = left
        self.n = groups_disp
        self.strips = strips
        self.own_rows = own * self.h
        self.rows = self.own_rows * self.n
        self.d = DG * self.n
        self.bw = self.strip // self.n
        self.mw = self.bw + 6
        self.tail = self.d + 2
        self.g = conv1[1]
        self.f = conv2[0]
        self.lo = round_up(self.mw + self.d - 1, 8)
        self.lb = self.lo // LANES * LANES
        self.lw = round_up(self.lo + self.mw, LANES)
        self.hops = []
        left_over = self.tail
        while left_over > 0:
            self.hops.append(min(left_over, self.strip))
            left_over -= self.strip
        per = KROWS // (CG * self.h)
        self.chunks = [min(per, self.g - k) for k in range(0, self.g, per)]
        self.lg = LANES // self.bw
        self.rg = round_up(-(-(self.own_rows + self.h) // self.lg), 8)


def lane_iota(shape):
    return lax.broadcasted_iota(jnp.int32, shape, 1)


def widen(x, lanes):
    have = x.shape[1]
    if have == lanes:
        return x
    return jnp.concatenate([x, jnp.zeros((x.shape[0], lanes - have), x.dtype)], axis=1)


def rolled(x, shift):
    shift %= x.shape[1]
    return x if shift == 0 else pltpu.roll(x, shift, 1)


def edge_kernel(dm, left_ref, right_ref, *outs):
    left = left_ref[...].astype(jnp.float32)
    right = right_ref[...].astype(jnp.float32)
    for k, count in enumerate(dm.hops):
        out = outs[k]
        width = out.shape[1]
        block = rolled(widen(right, max(width, dm.strip)), count - dm.strip)[:, :width]
        lane = lane_iota(block.shape)
        if k == 0:
            edge = rolled(widen(left, max(width, dm.strip)), count + 3 - dm.strip)[:, :width]
            block = jnp.where(lane < count, block, edge)
        out[...] = block.astype(out.dtype)
    out = outs[-1]
    first = right[:, :LANES]
    second = rolled(left[:, :LANES], 3)
    out[...] = jnp.where(lane_iota(first.shape) < 3, first, second).astype(out.dtype)


def pack_kernel(dm, left_ref, right_ref, *refs):
    ups, down_ref, out_ref = refs[: len(dm.hops)], refs[-2], refs[-1]
    left = left_ref[...].astype(jnp.float32)
    right = right_ref[...].astype(jnp.float32)
    down = down_ref[...].astype(jnp.float32)
    ext = round_up(dm.tail + dm.strip + 3, LANES)
    ext = max(ext, dm.lw)
    lane = lane_iota((dm.own_rows, ext))
    row = rolled(widen(right, ext), dm.tail)
    row = jnp.where(lane < dm.tail + dm.strip, row, rolled(widen(down, ext), dm.tail + dm.strip))
    for k, count in enumerate(dm.hops):
        start = dm.tail - sum(dm.hops[: k + 1])
        piece = rolled(widen(ups[k][...].astype(jnp.float32), ext), start)
        row = jnp.where((lane >= start) & (lane < start + count), piece, row)
    lext = max(round_up(dm.strip + 6, LANES), dm.lw)
    lane_l = lane_iota((dm.own_rows, lext))
    lrow = rolled(widen(left, lext), 3)
    edge = rolled(widen(ups[0][...].astype(jnp.float32), max(lext, ups[0].shape[1])), -dm.hops[0])
    lrow = jnp.where(lane_l < 3, edge[:, :lext], lrow)
    lrow = jnp.where(lane_l >= dm.strip + 3, rolled(widen(down, lext), dm.strip), lrow)
    lane_o = lane_iota((dm.own_rows, dm.lw))
    for j in range(dm.n):
        a = rolled(row, -dm.bw * j)[:, : dm.lw]
        b = rolled(lrow, dm.lo - dm.bw * j)[:, : dm.lw]
        out_ref[j] = jnp.where(lane_o < dm.lo, a, b).astype(out_ref.dtype)


def prep_kernel(dm, w1_ref, w2_ref, w3_ref, o1_ref, o2_ref, o3_ref):
    for layer, (w_ref, o_ref) in enumerate(((w1_ref, o1_ref), (w2_ref, o2_ref), (w3_ref, o3_ref))):
        inputs = w_ref.shape[2]
        per_a = dm.h * inputs
        shape = (inputs, 3 * per_a)
        i = lax.broadcasted_iota(jnp.int32, shape, 0)
        col = lane_iota(shape)
        total = None
        for a in range(3):
            for hi in range(dm.h):
                if layer == 0:
                    pos = jnp.zeros(shape, jnp.int32)
                    first = 0
                    for count in dm.chunks:
                        here = first * dm.h + hi * count + (i - first)
                        pos = jnp.where(i >= first, here, pos)
                        first += count
                else:
                    pos = hi * inputs + i
                place = jnp.where(col == a * per_a + pos, 1.0, 0.0).astype(jnp.bfloat16)
                blocks = []
                for e in range(3):
                    for ho in range(dm.h):
                        b = hi - ho + 1
                        if 0 <= b <= 2:
                            blocks.append(w_ref[(a * 3 + b) * 3 + e])
                        else:
                            blocks.append(jnp.zeros((dm.f, inputs), jnp.bfloat16))
                term = jnp.dot(
                    jnp.concatenate(blocks, axis=0), place, preferred_element_type=jnp.float32
                )
                total = term if total is None else total + term
        o_ref[...] = total.astype(o_ref.dtype)


def main_kernel(dm, x_ref, w1_ref, w2_ref, w3_ref, head_ref, out_ref, lt_ref, lhs_ref, pc_ref, a1_ref, a2_ref, a3_ref, ps_ref, s_ref):
    d, mw, h, f = dm.d, dm.mw, dm.h, dm.f
    base = lax.axis_index("col") * dm.strip + lax.axis_index("disp") * dm.bw
    total = dm.strips * dm.strip

    lt_ref[...] = jnp.transpose(x_ref[:, dm.lb : dm.lw].astype(jnp.float32))

    first = 0
    for k, count in enumerate(dm.chunks):
        r = count * h
        q = count * CG * h
        lane = lane_iota((r, q))
        sub = lax.broadcasted_iota(jnp.int32, (r, q), 0)
        keep = (lane % h == sub // count) & (lane // (CG * h) == sub % count)
        for m in range(mw):
            at = dm.lo - dm.lb + m
            line = jnp.broadcast_to(lt_ref[at : at + 1, first : first + q], (r, q))
            lhs_ref[m * r : (m + 1) * r, :q] = jnp.where(keep, line, 0.0).astype(jnp.bfloat16)
        pc_ref[k, : mw * r] = jnp.dot(
            lhs_ref[: mw * r, :q], x_ref[first : first + q, :], preferred_element_type=jnp.float32
        )
        first += q

    lane_d = {}

    def spread(ref, m, v):
        rows = v.shape[0]
        if rows not in lane_d:
            lane_d[rows] = lane_iota((rows, d))
        lane = lane_d[rows]
        at = slice(m * d, (m + 1) * d)
        ref[:rows, at] = jnp.where(lane < d - 1, rolled(v, -1), 0.0).astype(jnp.bfloat16)
        ref[rows : 2 * rows, at] = v.astype(jnp.bfloat16)
        ref[2 * rows :, at] = jnp.where(lane > 0, rolled(v, 1), 0.0).astype(jnp.bfloat16)

    for m in range(mw):
        parts = [pc_ref[k, m * c * h : (m + 1) * c * h] for k, c in enumerate(dm.chunks)]
        block = jnp.concatenate(parts, axis=0)
        spread(a1_ref, m, rolled(block, -m)[:, :d] * (1.0 / CG))

    step = 4 * LANES

    def layer(w_ref, a_ref, columns, emit):
        width = columns * d
        for t in range(0, width, step):
            size = min(step, width - t)
            ps_ref[:, t : t + size] = jnp.dot(
                w_ref[...], a_ref[:, t : t + size], preferred_element_type=jnp.float32
            )
        fh = f * h
        for m in range(1, columns - 1):
            z = ps_ref[:fh, (m - 1) * d : m * d]
            z = z + ps_ref[fh : 2 * fh, m * d : (m + 1) * d]
            z = z + ps_ref[2 * fh :, (m + 1) * d : (m + 2) * d]
            emit(m - 1, jnp.maximum(z, 0.0))

    def inside(column, z):
        if 3 <= column < mw - 3:
            return z
        at = base - 3 + column
        return jnp.where((at >= 0) & (at < total), z, 0.0)

    layer(w1_ref, a1_ref, mw, lambda m, z: spread(a2_ref, m, inside(m + 1, z)))
    layer(w2_ref, a2_ref, mw - 2, lambda m, z: spread(a3_ref, m, inside(m + 2, z)))

    head = head_ref[...]

    def score(m, z):
        z = z * head
        for row in range(h):
            s_ref[row, m : m + 1, :] = jnp.sum(z[row * f : (row + 1) * f], axis=0, keepdims=True)

    layer(w3_ref, a3_ref, mw - 4, score)

    disp = (d - 1) - lane_iota((dm.bw, d))
    column = base + lax.broadcasted_iota(jnp.int32, (dm.bw, d), 0)
    valid = column >= disp
    disp_f = disp.astype(jnp.float32)
    bands, disparity = [], []
    for row in range(h):
        s = jnp.where(valid, s_ref[row], masked_value)
        top = jnp.max(s, axis=1, keepdims=True)
        weighting = jnp.where(valid, jnp.exp(s - top), 0.0)
        denominator = jnp.sum(weighting, axis=1, keepdims=True)
        disp_sum = jnp.sum(weighting * disp_f, axis=1, keepdims=True)
        disparity.append(disp_sum / denominator / d)
        band = widen(weighting / denominator, dm.lw)
        bands.append(pltpu.roll(band, 3, 1, stride=1, stride_axis=0))
    band = jnp.concatenate(bands, axis=0)
    high = band.astype(jnp.bfloat16)
    low = (band - high.astype(jnp.float32)).astype(jnp.bfloat16)
    sums = lax.dot_general(
        x_ref[...],
        jnp.concatenate([high, low], axis=0),
        (((1,), (1,)), ((), ())),
        preferred_element_type=jnp.float32,
    )
    hb = h * dm.bw
    sums = widen(sums, round_up(2 * hb, LANES))
    sums = sums + rolled(sums, -hb)
    row = lax.broadcasted_iota(jnp.int32, sums.shape, 0) % h
    warped = sums
    for k in range(1, h):
        warped = jnp.where(row == k, rolled(sums, -k * dm.bw), warped)
    warped = warped[:, :LANES]

    eye = lane_iota((dm.bw, LANES)) == lax.broadcasted_iota(jnp.int32, (dm.bw, LANES), 0)
    lines = [jnp.sum(jnp.where(eye, v, 0.0), axis=0, keepdims=True) for v in disparity]
    lines.append(jnp.zeros((dm.lg * dm.rg - dm.own_rows - h, LANES), jnp.float32))
    lines = jnp.concatenate(lines, axis=0)
    lane = lane_iota((dm.rg, LANES))
    for j in range(dm.n):
        mine = jnp.concatenate([warped[j * dm.own_rows : (j + 1) * dm.own_rows], lines], axis=0)
        packed = mine[: dm.rg]
        for g in range(1, dm.lg):
            packed = jnp.where(
                (lane >= g * dm.bw) & (lane < (g + 1) * dm.bw),
                rolled(mine[g * dm.rg : (g + 1) * dm.rg], g * dm.bw),
                packed,
            )
        out_ref[j] = packed


def unpack_kernel(dm, y_ref, warped_ref, disparity_ref):
    per = LANES // dm.bw
    lane = lane_iota((dm.rg, LANES))
    tiles = []
    for t in range(dm.n // per):
        groups = []
        for g in range(dm.lg):
            total = None
            for p in range(per):
                piece = rolled(y_ref[t * per + p], (p - g) * dm.bw)
                keep = (lane >= p * dm.bw) & (lane < (p + 1) * dm.bw)
                total = piece if total is None else jnp.where(keep, piece, total)
            groups.append(total)
        tiles.append(jnp.concatenate(groups, axis=0))
    full = jnp.concatenate(tiles, axis=1)
    warped_ref[...] = full[: dm.own_rows].astype(warped_ref.dtype)
    disparity_ref[...] = full[dm.own_rows : dm.own_rows + dm.h]


def shards(left_feat, right_feat, conv1_w, conv2_w, conv3_w, head_w):
    n, strips = lax.axis_size("disp"), lax.axis_size("col")
    dm = Dims(left_feat.shape, conv1_w.shape, conv2_w.shape, n, strips)
    bf, f32 = jnp.bfloat16, jnp.float32
    left = left_feat.reshape(dm.own_rows, dm.strip)
    right = right_feat.reshape(dm.own_rows, dm.strip)

    widths = [round_up(c + (3 if k == 0 else 0), LANES) for k, c in enumerate(dm.hops)]
    edges = pl.pallas_call(
        functools.partial(edge_kernel, dm),
        out_shape=[jax.ShapeDtypeStruct((dm.own_rows, w), bf) for w in widths + [LANES]],
    )(left, right)
    ups = [
        lax.ppermute(e, "col", [(s, s + k + 1) for s in range(strips - k - 1)])
        for k, e in enumerate(edges[:-1])
    ]
    down = lax.ppermute(edges[-1], "col", [(s + 1, s) for s in range(strips - 1)])

    kernels = [w.transpose(2, 3, 4, 0, 1).reshape(27, w.shape[0], w.shape[1]) for w in (conv1_w, conv2_w, conv3_w)]
    m3 = 3 * dm.h * dm.f
    depths = [3 * dm.h * w.shape[2] for w in kernels]
    w1, w2, w3 = pl.pallas_call(
        functools.partial(prep_kernel, dm),
        out_shape=[jax.ShapeDtypeStruct((m3, k), bf) for k in depths],
    )(*kernels)

    send = pl.pallas_call(
        functools.partial(pack_kernel, dm),
        out_shape=jax.ShapeDtypeStruct((n, dm.own_rows, dm.lw), bf),
    )(left, right, *ups, down)
    x = lax.all_to_all(send, "disp", 0, 0).reshape(dm.rows, dm.lw)

    head = jnp.broadcast_to(jnp.tile(head_w, dm.h)[:, None], (dm.h * dm.f, dm.d))
    r_max = max(dm.chunks) * dm.h
    columns = [dm.mw, dm.mw - 2, dm.mw - 4]
    packed = pl.pallas_call(
        functools.partial(main_kernel, dm),
        out_shape=jax.ShapeDtypeStruct((n, dm.rg, LANES), f32),
        scratch_shapes=[
            pltpu.VMEM((dm.lw - dm.lb, dm.rows), f32),
            pltpu.VMEM((dm.mw * r_max, KROWS), bf),
            pltpu.VMEM((len(dm.chunks), dm.mw * r_max, dm.lw), f32),
            pltpu.VMEM((depths[0], columns[0] * dm.d), bf),
            pltpu.VMEM((depths[1], columns[1] * dm.d), bf),
            pltpu.VMEM((depths[2], columns[2] * dm.d), bf),
            pltpu.VMEM((m3, columns[0] * dm.d), f32),
            pltpu.VMEM((dm.h, dm.bw, dm.d), f32),
        ],
    )(x, w1, w2, w3, head)
    y = lax.all_to_all(packed, "disp", 0, 0)
    warped, disparity = pl.pallas_call(
        functools.partial(unpack_kernel, dm),
        out_shape=[
            jax.ShapeDtypeStruct((dm.own_rows, dm.strip), bf),
            jax.ShapeDtypeStruct((dm.h, dm.strip), f32),
        ],
    )(y)
    return (warped.reshape(left_feat.shape), disparity)


def solution(mesh):
    return jax.shard_map(
        shards,
        mesh=mesh,
        in_specs=(P("disp", None, "col"), P("disp", None, "col"), P(), P(), P(), P()),
        out_specs=(P("disp", None, "col"), P(None, "col")),
        check_vma=False,
    )
```

```python
import functools

import jax
import jax.numpy as jnp
from jax import lax
from jax.experimental import pallas as pl
from jax.experimental.pallas import tpu as pltpu
from jax.sharding import PartitionSpec as P

DG = 16
CG = 8
LANES = 128
KROWS = 256
VMEM = pl.BlockSpec(memory_space=pltpu.VMEM)

masked_value = -1e30


def round_up(value, unit):
    return -(-value // unit) * unit


class Dims:
    def __init__(self, left, conv1, conv2, groups_disp, strips):
        own, self.h, self.strip = left
        self.n = groups_disp
        self.strips = strips
        self.own_rows = own * self.h
        self.rows = self.own_rows * self.n
        self.d = DG * self.n
        self.bw = self.strip // self.n
        self.mw = self.bw + 6
        self.tail = self.d + 2
        self.g = conv1[1]
        self.f = conv2[0]
        self.lo = round_up(self.mw + self.d - 1, 8)
        self.lb = self.lo // LANES * LANES
        self.lw = round_up(self.lo + self.mw, LANES)
        self.hops = []
        left_over = self.tail
        while left_over > 0:
            self.hops.append(min(left_over, self.strip))
            left_over -= self.strip
        per = KROWS // (CG * self.h)
        self.chunks = [min(per, self.g - k) for k in range(0, self.g, per)]
        self.lg = LANES // self.bw
        self.rg = round_up(-(-(self.own_rows + self.h) // self.lg), 8)


def lane_iota(shape):
    return lax.broadcasted_iota(jnp.int32, shape, 1)


def widen(x, lanes):
    have = x.shape[1]
    if have == lanes:
        return x
    return jnp.concatenate([x, jnp.zeros((x.shape[0], lanes - have), x.dtype)], axis=1)


def rolled(x, shift):
    shift %= x.shape[1]
    return x if shift == 0 else pltpu.roll(x, shift, 1)


def flat(ref):
    return ref[...].astype(jnp.float32).reshape(-1, ref.shape[-1])


def edge_kernel(dm, left_ref, right_ref, *outs):
    left, right = flat(left_ref), flat(right_ref)
    width = outs[0].shape[1]
    count = dm.hops[0]
    lane = lane_iota((dm.own_rows, width))
    last = rolled(widen(right, width), count - dm.strip)
    edge = rolled(widen(left, width), count + 3 - dm.strip)
    up = jnp.where(lane < count, last, edge)
    down = jnp.where(lane < 3, widen(right, width), rolled(widen(left, width), 3))
    even = lax.axis_index("col") % 2 == 0
    outs[0][...] = jnp.where(even, up, down).astype(outs[0].dtype)
    outs[1][...] = jnp.where(even, down, up).astype(outs[1].dtype)
    for out, count in zip(outs[2:], dm.hops[1:]):
        out[...] = rolled(right, count - dm.strip)[:, : out.shape[1]].astype(out.dtype)


def pack_kernel(dm, left_ref, right_ref, pair0_ref, pair1_ref, *refs):
    out_ref = refs[-1]
    left, right = flat(left_ref), flat(right_ref)
    pair0, pair1 = flat(pair0_ref), flat(pair1_ref)
    even = lax.axis_index("col") % 2 == 0
    up = jnp.where(even, pair1, pair0)
    down = jnp.where(even, pair0, pair1)[:, :LANES]
    ext = max(round_up(dm.tail + dm.strip + 3, LANES), dm.lw, up.shape[1])
    lane = lane_iota((dm.own_rows, ext))
    row = rolled(widen(right, ext), dm.tail)
    row = jnp.where(lane < dm.tail + dm.strip, row, rolled(widen(down, ext), dm.tail + dm.strip))
    pieces = [up] + [flat(ref) for ref in refs[:-1]]
    for k, count in enumerate(dm.hops):
        start = dm.tail - sum(dm.hops[: k + 1])
        piece = rolled(widen(pieces[k], ext), start)
        row = jnp.where((lane >= start) & (lane < start + count), piece, row)
    lext = max(round_up(dm.strip + 6, LANES), dm.lw, up.shape[1])
    lane_l = lane_iota((dm.own_rows, lext))
    lrow = rolled(widen(left, lext), 3)
    lrow = jnp.where(lane_l < 3, rolled(widen(up, lext), -dm.hops[0]), lrow)
    lrow = jnp.where(lane_l >= dm.strip + 3, rolled(widen(down, lext), dm.strip), lrow)
    lane_o = lane_iota((dm.own_rows, dm.lw))
    for j in range(dm.n):
        a = rolled(row, -dm.bw * j)[:, : dm.lw]
        b = rolled(lrow, dm.lo - dm.bw * j)[:, : dm.lw]
        out_ref[j] = jnp.where(lane_o < dm.lo, a, b).astype(out_ref.dtype)


def prep_kernel(dm, w1_ref, w2_ref, w3_ref, head_ref, o1_ref, o2_ref, o3_ref, column_ref):
    for layer, (w_ref, o_ref) in enumerate(((w1_ref, o1_ref), (w2_ref, o2_ref), (w3_ref, o3_ref))):
        inputs = w_ref.shape[2]
        per_a = dm.h * inputs
        shape = (inputs, 3 * per_a)
        i = lax.broadcasted_iota(jnp.int32, shape, 0)
        col = lane_iota(shape)
        total = None
        for a in range(3):
            for hi in range(dm.h):
                if layer == 0:
                    pos = jnp.zeros(shape, jnp.int32)
                    first = 0
                    for count in dm.chunks:
                        here = first * dm.h + hi * count + (i - first)
                        pos = jnp.where(i >= first, here, pos)
                        first += count
                else:
                    pos = hi * inputs + i
                place = jnp.where(col == a * per_a + pos, 1.0, 0.0).astype(jnp.bfloat16)
                blocks = []
                for e in range(3):
                    for ho in range(dm.h):
                        b = hi - ho + 1
                        if 0 <= b <= 2:
                            blocks.append(w_ref[(a * 3 + b) * 3 + e])
                        else:
                            blocks.append(jnp.zeros((dm.f, inputs), jnp.bfloat16))
                term = jnp.dot(
                    jnp.concatenate(blocks, axis=0), place, preferred_element_type=jnp.float32
                )
                total = term if total is None else total + term
        o_ref[...] = total.astype(o_ref.dtype)
    square = (dm.f, dm.f)
    eye = lane_iota(square) == lax.broadcasted_iota(jnp.int32, square, 0)
    column = jnp.sum(jnp.where(eye, head_ref[...], 0.0), axis=1, keepdims=True)
    column = jnp.broadcast_to(column, (dm.f, dm.d))
    column_ref[...] = jnp.concatenate([column] * dm.h, axis=0)


def main_kernel(dm, x_ref, w1_ref, w2_ref, w3_ref, head_ref, out_ref, lt_ref, lhs_ref, pc_ref, a1_ref, a2_ref, a3_ref, ps_ref, s_ref):
    d, mw, h, f = dm.d, dm.mw, dm.h, dm.f
    base = lax.axis_index("col") * dm.strip + lax.axis_index("disp") * dm.bw
    total = dm.strips * dm.strip

    lt_ref[...] = jnp.transpose(x_ref[:, dm.lb : dm.lw].astype(jnp.float32))

    first = 0
    for k, count in enumerate(dm.chunks):
        r = count * h
        q = count * CG * h
        lane = lane_iota((r, q))
        sub = lax.broadcasted_iota(jnp.int32, (r, q), 0)
        keep = (lane % h == sub // count) & (lane // (CG * h) == sub % count)
        for m in range(mw):
            at = dm.lo - dm.lb + m
            line = jnp.broadcast_to(lt_ref[at : at + 1, first : first + q], (r, q))
            lhs_ref[m * r : (m + 1) * r, :q] = jnp.where(keep, line, 0.0).astype(jnp.bfloat16)
        pc_ref[k, : mw * r] = jnp.dot(
            lhs_ref[: mw * r, :q], x_ref[first : first + q, :], preferred_element_type=jnp.float32
        )
        first += q

    lane_d = {}

    def spread(ref, m, v):
        rows = v.shape[0]
        if rows not in lane_d:
            lane_d[rows] = lane_iota((rows, d))
        lane = lane_d[rows]
        at = slice(m * d, (m + 1) * d)
        ref[:rows, at] = jnp.where(lane < d - 1, rolled(v, -1), 0.0).astype(jnp.bfloat16)
        ref[rows : 2 * rows, at] = v.astype(jnp.bfloat16)
        ref[2 * rows :, at] = jnp.where(lane > 0, rolled(v, 1), 0.0).astype(jnp.bfloat16)

    for m in range(mw):
        parts = [pc_ref[k, m * c * h : (m + 1) * c * h] for k, c in enumerate(dm.chunks)]
        block = jnp.concatenate(parts, axis=0)
        spread(a1_ref, m, rolled(block, -m)[:, :d] * (1.0 / CG))

    step = 4 * LANES

    def layer(w_ref, a_ref, columns, emit):
        width = columns * d
        for t in range(0, width, step):
            size = min(step, width - t)
            ps_ref[:, t : t + size] = jnp.dot(
                w_ref[...], a_ref[:, t : t + size], preferred_element_type=jnp.float32
            )
        fh = f * h
        for m in range(1, columns - 1):
            z = ps_ref[:fh, (m - 1) * d : m * d]
            z = z + ps_ref[fh : 2 * fh, m * d : (m + 1) * d]
            z = z + ps_ref[2 * fh :, (m + 1) * d : (m + 2) * d]
            emit(m - 1, jnp.maximum(z, 0.0))

    def inside(column, z):
        if 3 <= column < mw - 3:
            return z
        at = base - 3 + column
        return jnp.where((at >= 0) & (at < total), z, 0.0)

    layer(w1_ref, a1_ref, mw, lambda m, z: spread(a2_ref, m, inside(m + 1, z)))
    layer(w2_ref, a2_ref, mw - 2, lambda m, z: spread(a3_ref, m, inside(m + 2, z)))

    head = head_ref[...]

    def score(m, z):
        z = z * head
        for row in range(h):
            s_ref[row, m : m + 1, :] = jnp.sum(z[row * f : (row + 1) * f], axis=0, keepdims=True)

    layer(w3_ref, a3_ref, mw - 4, score)

    disp = (d - 1) - lane_iota((dm.bw, d))
    column = base + lax.broadcasted_iota(jnp.int32, (dm.bw, d), 0)
    valid = column >= disp
    disp_f = disp.astype(jnp.float32)
    bands, disparity = [], []
    for row in range(h):
        s = jnp.where(valid, s_ref[row], masked_value)
        top = jnp.max(s, axis=1, keepdims=True)
        weighting = jnp.where(valid, jnp.exp(s - top), 0.0)
        denominator = jnp.sum(weighting, axis=1, keepdims=True)
        disp_sum = jnp.sum(weighting * disp_f, axis=1, keepdims=True)
        disparity.append(disp_sum / denominator / d)
        band = widen(weighting / denominator, dm.lw)
        bands.append(pltpu.roll(band, 3, 1, stride=1, stride_axis=0))
    band = jnp.concatenate(bands, axis=0)
    high = band.astype(jnp.bfloat16)
    low = (band - high.astype(jnp.float32)).astype(jnp.bfloat16)
    sums = lax.dot_general(
        x_ref[...],
        jnp.concatenate([high, low], axis=0),
        (((1,), (1,)), ((), ())),
        preferred_element_type=jnp.float32,
    )
    hb = h * dm.bw
    sums = widen(sums, round_up(2 * hb, LANES))
    sums = sums + rolled(sums, -hb)
    row = lax.broadcasted_iota(jnp.int32, sums.shape, 0) % h
    warped = sums
    for k in range(1, h):
        warped = jnp.where(row == k, rolled(sums, -k * dm.bw), warped)
    warped = warped[:, :LANES]

    eye = lane_iota((dm.bw, LANES)) == lax.broadcasted_iota(jnp.int32, (dm.bw, LANES), 0)
    lines = [jnp.sum(jnp.where(eye, v, 0.0), axis=0, keepdims=True) for v in disparity]
    lines.append(jnp.zeros((dm.lg * dm.rg - dm.own_rows - h, LANES), jnp.float32))
    lines = jnp.concatenate(lines, axis=0)
    lane = lane_iota((dm.rg, LANES))
    for j in range(dm.n):
        mine = jnp.concatenate([warped[j * dm.own_rows : (j + 1) * dm.own_rows], lines], axis=0)
        packed = mine[: dm.rg]
        for g in range(1, dm.lg):
            packed = jnp.where(
                (lane >= g * dm.bw) & (lane < (g + 1) * dm.bw),
                rolled(mine[g * dm.rg : (g + 1) * dm.rg], g * dm.bw),
                packed,
            )
        out_ref[j] = packed


def unpack_kernel(dm, y_ref, warped_ref, disparity_ref):
    per = LANES // dm.bw
    lane = lane_iota((dm.rg, LANES))
    tiles = []
    for t in range(dm.n // per):
        groups = []
        for g in range(dm.lg):
            total = None
            for p in range(per):
                piece = rolled(y_ref[t * per + p], (p - g) * dm.bw)
                keep = (lane >= p * dm.bw) & (lane < (p + 1) * dm.bw)
                total = piece if total is None else jnp.where(keep, piece, total)
            groups.append(total)
        tiles.append(jnp.concatenate(groups, axis=0))
    full = jnp.concatenate(tiles, axis=1)
    warped_ref[...] = full[: dm.own_rows].reshape(warped_ref.shape).astype(warped_ref.dtype)
    disparity_ref[...] = full[dm.own_rows : dm.own_rows + dm.h]


def shards(left_feat, right_feat, conv1_w, conv2_w, conv3_w, head_w):
    n, strips = lax.axis_size("disp"), lax.axis_size("col")
    dm = Dims(left_feat.shape, conv1_w.shape, conv2_w.shape, n, strips)
    bf, f32 = jnp.bfloat16, jnp.float32

    def call(kernel, out_shape, operands, mib=8, **options):
        return pl.pallas_call(
            functools.partial(kernel, dm),
            out_shape=out_shape,
            in_specs=[VMEM] * len(operands),
            out_specs=jax.tree.map(lambda _: VMEM, out_shape),
            compiler_params=pltpu.CompilerParams(vmem_limit_bytes=mib << 20),
            **options,
        )(*operands)

    wide = max(round_up(dm.hops[0] + 3, LANES), dm.strip)
    widths = [wide, wide] + [round_up(c, LANES) for c in dm.hops[1:]]
    edges = call(
        edge_kernel,
        [jax.ShapeDtypeStruct((dm.own_rows, w), bf) for w in widths],
        [left_feat, right_feat],
    )
    arrived = []
    for first in range(2):
        pairs = [(s, s + 1) for s in range(first, strips - 1, 2)]
        pairs += [(b, a) for a, b in pairs]
        arrived.append(lax.ppermute(edges[first], "col", pairs))
    for k, e in enumerate(edges[2:], 2):
        arrived.append(lax.ppermute(e, "col", [(s, s + k) for s in range(strips - k)]))

    kernels = [w.transpose(2, 3, 4, 0, 1).reshape(27, w.shape[0], w.shape[1]) for w in (conv1_w, conv2_w, conv3_w)]
    m3 = 3 * dm.h * dm.f
    depths = [3 * dm.h * w.shape[2] for w in kernels]
    w1, w2, w3, head = call(
        prep_kernel,
        [jax.ShapeDtypeStruct((m3, k), bf) for k in depths]
        + [jax.ShapeDtypeStruct((dm.h * dm.f, dm.d), f32)],
        kernels + [head_w[None]],
    )

    send = call(
        pack_kernel,
        jax.ShapeDtypeStruct((n, dm.own_rows, dm.lw), bf),
        [left_feat, right_feat] + arrived,
    )
    x = lax.all_to_all(send, "disp", 0, 0).reshape(dm.rows, dm.lw)

    r_max = max(dm.chunks) * dm.h
    columns = [dm.mw, dm.mw - 2, dm.mw - 4]
    packed = call(
        main_kernel,
        jax.ShapeDtypeStruct((n, dm.rg, LANES), f32),
        [x, w1, w2, w3, head],
        mib=32,
        scratch_shapes=[
            pltpu.VMEM((dm.lw - dm.lb, dm.rows), f32),
            pltpu.VMEM((dm.mw * r_max, KROWS), bf),
            pltpu.VMEM((len(dm.chunks), dm.mw * r_max, dm.lw), f32),
            pltpu.VMEM((depths[0], columns[0] * dm.d), bf),
            pltpu.VMEM((depths[1], columns[1] * dm.d), bf),
            pltpu.VMEM((depths[2], columns[2] * dm.d), bf),
            pltpu.VMEM((m3, columns[0] * dm.d), f32),
            pltpu.VMEM((dm.h, dm.bw, dm.d), f32),
        ],
    )
    y = lax.all_to_all(packed, "disp", 0, 0)
    return tuple(
        call(
            unpack_kernel,
            [
                jax.ShapeDtypeStruct(left_feat.shape, bf),
                jax.ShapeDtypeStruct((dm.h, dm.strip), f32),
            ],
            [y],
        )
    )


def solution(mesh):
    return jax.shard_map(
        shards,
        mesh=mesh,
        in_specs=(P("disp", None, "col"), P("disp", None, "col"), P(), P(), P(), P()),
        out_specs=(P("disp", None, "col"), P(None, "col")),
        check_vma=False,
    )
```

```python
import functools

import jax
import jax.numpy as jnp
from jax import lax
from jax.experimental import pallas as pl
from jax.experimental.pallas import tpu as pltpu
from jax.sharding import PartitionSpec as P

DG = 16
CG = 8
LANES = 128
KROWS = 256
VMEM = pl.BlockSpec(memory_space=pltpu.VMEM)

masked_value = -1e30


def round_up(value, unit):
    return -(-value // unit) * unit


class Dims:
    def __init__(self, left, conv1, conv2, groups_disp, strips):
        own, self.h, self.strip = left
        self.n = groups_disp
        self.strips = strips
        self.own_rows = own * self.h
        self.rows = self.own_rows * self.n
        self.d = DG * self.n
        self.bw = self.strip // self.n
        self.mw = self.bw + 6
        self.tail = self.d + 2
        self.g = conv1[1]
        self.f = conv2[0]
        self.lo = round_up(self.mw + self.d - 1, 8)
        self.lb = self.lo // LANES * LANES
        self.lw = round_up(self.lo + self.mw, LANES)
        self.hops = []
        left_over = self.tail
        while left_over > 0:
            self.hops.append(min(left_over, self.strip))
            left_over -= self.strip
        per = KROWS // (CG * self.h)
        self.chunks = [min(per, self.g - k) for k in range(0, self.g, per)]
        self.chips = self.n // 2
        self.lo2 = round_up(self.mw + self.bw + self.d - 1, 8)
        self.lw2 = round_up(self.lo2 + self.mw + self.bw, LANES)
        self.lg = LANES // self.bw
        self.rg = round_up(-(-(self.own_rows + self.h) // self.lg), 8)


def lane_iota(shape):
    return lax.broadcasted_iota(jnp.int32, shape, 1)


def widen(x, lanes):
    have = x.shape[1]
    if have == lanes:
        return x
    return jnp.concatenate([x, jnp.zeros((x.shape[0], lanes - have), x.dtype)], axis=1)


def rolled(x, shift):
    shift %= x.shape[1]
    return x if shift == 0 else pltpu.roll(x, shift, 1)


def flat(ref):
    return ref[...].astype(jnp.float32).reshape(-1, ref.shape[-1])


def copied_in(sources, targets, sems):
    copies = [
        pltpu.make_async_copy(source, target, sems.at[k])
        for k, (source, target) in enumerate(zip(sources, targets))
    ]
    for copy in copies:
        copy.start()
    return [copy.wait for copy in copies]


def edge_kernel(dm, left_hbm, right_hbm, *refs):
    *outs, flat_left_ref, flat_right_ref, left_ref, right_ref, sems = refs
    for wait in copied_in((left_hbm, right_hbm), (left_ref, right_ref), sems):
        wait()
    left, right = flat(left_ref), flat(right_ref)
    flat_left_ref[...] = left.astype(flat_left_ref.dtype)
    flat_right_ref[...] = right.astype(flat_right_ref.dtype)
    width = outs[0].shape[1]
    count = dm.hops[0]
    lane = lane_iota((dm.own_rows, width))
    last = rolled(widen(right, width), count - dm.strip)
    edge = rolled(widen(left, width), count + 3 - dm.strip)
    up = jnp.where(lane < count, last, edge)
    down = jnp.where(lane < 3, widen(right, width), rolled(widen(left, width), 3))
    even = lax.axis_index("col") % 2 == 0
    outs[0][...] = jnp.where(even, up, down).astype(outs[0].dtype)
    outs[1][...] = jnp.where(even, down, up).astype(outs[1].dtype)
    for out, count in zip(outs[2:], dm.hops[1:]):
        out[...] = rolled(right, count - dm.strip)[:, : out.shape[1]].astype(out.dtype)


def pack_kernel(dm, left_ref, right_ref, pair0_ref, pair1_ref, *refs):
    more, outs, windows_ref = refs[: len(dm.hops) - 1], refs[len(dm.hops) - 1 : -1], refs[-1]
    left, right = flat(left_ref), flat(right_ref)
    pair0, pair1 = flat(pair0_ref), flat(pair1_ref)
    even = lax.axis_index("col") % 2 == 0
    up = jnp.where(even, pair1, pair0)
    down = jnp.where(even, pair0, pair1)[:, :LANES]
    ext = max(round_up(dm.tail + dm.strip + 3, LANES), dm.lw2, up.shape[1])
    lane = lane_iota((dm.own_rows, ext))
    row = rolled(widen(right, ext), dm.tail)
    row = jnp.where(lane < dm.tail + dm.strip, row, rolled(widen(down, ext), dm.tail + dm.strip))
    pieces = [up] + [flat(ref) for ref in more]
    for k, count in enumerate(dm.hops):
        start = dm.tail - sum(dm.hops[: k + 1])
        piece = rolled(widen(pieces[k], ext), start)
        row = jnp.where((lane >= start) & (lane < start + count), piece, row)
    lext = max(round_up(dm.strip + 6, LANES), dm.lw2, up.shape[1])
    lane_l = lane_iota((dm.own_rows, lext))
    lrow = rolled(widen(left, lext), 3)
    lrow = jnp.where(lane_l < 3, rolled(widen(up, lext), -dm.hops[0]), lrow)
    lrow = jnp.where(lane_l >= dm.strip + 3, rolled(widen(down, lext), dm.strip), lrow)
    lane_o = lane_iota((dm.own_rows, dm.lw2))
    for q in range(dm.chips):
        a = rolled(row, -2 * dm.bw * q)[:, : dm.lw2]
        b = rolled(lrow, dm.lo2 - 2 * dm.bw * q)[:, : dm.lw2]
        windows_ref[q] = jnp.where(lane_o < dm.lo2, a, b).astype(windows_ref.dtype)
    chip = lax.axis_index("disp") // 2
    for m, out in enumerate(outs):
        out[...] = windows_ref[chip ^ m]


def split_kernel(dm, *refs):
    *windows, keep_ref, give_ref = refs
    first_core = lax.axis_index("disp") % 2 == 0
    for m, ref in enumerate(windows):
        x = flat(ref)
        lane = lane_iota((dm.own_rows, dm.lw))
        parts = []
        for core in range(2):
            a = rolled(x, -core * dm.bw)[:, : dm.lw]
            b = rolled(x, dm.lo - dm.lo2 - core * dm.bw)[:, : dm.lw]
            parts.append(jnp.where(lane < dm.lo, a, b))
        keep_ref[m] = jnp.where(first_core, parts[0], parts[1]).astype(keep_ref.dtype)
        give_ref[m] = jnp.where(first_core, parts[1], parts[0]).astype(give_ref.dtype)


def prep_kernel(dm, *refs):
    outs, targets, sems = refs[4:8], refs[8:12], refs[12]
    waits = copied_in(refs[:4], targets, sems)
    w1_ref, w2_ref, w3_ref, head_ref = targets
    o1_ref, o2_ref, o3_ref, column_ref = outs
    chip = lax.axis_index("disp") // 2
    for layer, (w_ref, o_ref) in enumerate(((w1_ref, o1_ref), (w2_ref, o2_ref), (w3_ref, o3_ref))):
        inputs = w_ref.shape[2]
        per_a = dm.h * inputs
        waits[layer]()
        shape = (inputs, 3 * per_a)
        i = lax.broadcasted_iota(jnp.int32, shape, 0)
        if layer == 0:
            per_chip = inputs // dm.chips
            i = ((i // per_chip) ^ chip) * per_chip + i % per_chip
        col = lane_iota(shape)
        total = None
        for a in range(3):
            for hi in range(dm.h):
                if layer == 0:
                    pos = jnp.zeros(shape, jnp.int32)
                    first = 0
                    for count in dm.chunks:
                        here = first * dm.h + hi * count + (i - first)
                        pos = jnp.where(i >= first, here, pos)
                        first += count
                else:
                    pos = hi * inputs + i
                place = jnp.where(col == a * per_a + pos, 1.0, 0.0).astype(jnp.bfloat16)
                blocks = []
                for e in range(3):
                    for ho in range(dm.h):
                        b = hi - ho + 1
                        if 0 <= b <= 2:
                            blocks.append(w_ref[(a * 3 + b) * 3 + e])
                        else:
                            blocks.append(jnp.zeros((dm.f, inputs), jnp.bfloat16))
                term = jnp.dot(
                    jnp.concatenate(blocks, axis=0), place, preferred_element_type=jnp.float32
                )
                total = term if total is None else total + term
        o_ref[...] = total.astype(o_ref.dtype)
    waits[3]()
    square = (dm.f, dm.f)
    eye = lane_iota(square) == lax.broadcasted_iota(jnp.int32, square, 0)
    column = jnp.sum(jnp.where(eye, head_ref[...], 0.0), axis=1, keepdims=True)
    column = jnp.broadcast_to(column, (dm.f, dm.d))
    column_ref[...] = jnp.concatenate([column] * dm.h, axis=0)


def main_kernel(dm, keep_ref, got_ref, w1_ref, w2_ref, w3_ref, head_ref, out_ref, x_ref, lt_ref, lhs_ref, pc_ref, a1_ref, a2_ref, a3_ref, ps_ref, s_ref):
    d, mw, h, f = dm.d, dm.mw, dm.h, dm.f
    base = lax.axis_index("col") * dm.strip + lax.axis_index("disp") * dm.bw
    total = dm.strips * dm.strip

    chip, core = lax.axis_index("disp") // 2, lax.axis_index("disp") % 2
    for m in range(dm.chips):
        kept, got = flat(keep_ref.at[m]), flat(got_ref.at[m])
        both = [jnp.where(core == 0, kept, got), jnp.where(core == 0, got, kept)]
        rows = 2 * dm.own_rows
        x_ref[m * rows : (m + 1) * rows] = jnp.concatenate(both, axis=0).astype(x_ref.dtype)

    lt_ref[...] = jnp.transpose(x_ref[:, dm.lb : dm.lw].astype(jnp.float32))

    first = 0
    for k, count in enumerate(dm.chunks):
        r = count * h
        q = count * CG * h
        lane = lane_iota((r, q))
        sub = lax.broadcasted_iota(jnp.int32, (r, q), 0)
        keep = (lane % h == sub // count) & (lane // (CG * h) == sub % count)
        for m in range(mw):
            at = dm.lo - dm.lb + m
            line = jnp.broadcast_to(lt_ref[at : at + 1, first : first + q], (r, q))
            lhs_ref[m * r : (m + 1) * r, :q] = jnp.where(keep, line, 0.0).astype(jnp.bfloat16)
        pc_ref[k, : mw * r] = jnp.dot(
            lhs_ref[: mw * r, :q], x_ref[first : first + q, :], preferred_element_type=jnp.float32
        )
        first += q

    lane_d = {}

    def spread(ref, m, v):
        rows = v.shape[0]
        if rows not in lane_d:
            lane_d[rows] = lane_iota((rows, d))
        lane = lane_d[rows]
        at = slice(m * d, (m + 1) * d)
        ref[:rows, at] = jnp.where(lane < d - 1, rolled(v, -1), 0.0).astype(jnp.bfloat16)
        ref[rows : 2 * rows, at] = v.astype(jnp.bfloat16)
        ref[2 * rows :, at] = jnp.where(lane > 0, rolled(v, 1), 0.0).astype(jnp.bfloat16)

    for m in range(mw):
        parts = [pc_ref[k, m * c * h : (m + 1) * c * h] for k, c in enumerate(dm.chunks)]
        block = jnp.concatenate(parts, axis=0)
        spread(a1_ref, m, rolled(block, -m)[:, :d] * (1.0 / CG))

    step = 4 * LANES

    def layer(w_ref, a_ref, columns, emit):
        width = columns * d
        for t in range(0, width, step):
            size = min(step, width - t)
            ps_ref[:, t : t + size] = jnp.dot(
                w_ref[...], a_ref[:, t : t + size], preferred_element_type=jnp.float32
            )
        fh = f * h
        for m in range(1, columns - 1):
            z = ps_ref[:fh, (m - 1) * d : m * d]
            z = z + ps_ref[fh : 2 * fh, m * d : (m + 1) * d]
            z = z + ps_ref[2 * fh :, (m + 1) * d : (m + 2) * d]
            emit(m - 1, jnp.maximum(z, 0.0))

    def inside(column, z):
        if 3 <= column < mw - 3:
            return z
        at = base - 3 + column
        return jnp.where((at >= 0) & (at < total), z, 0.0)

    layer(w1_ref, a1_ref, mw, lambda m, z: spread(a2_ref, m, inside(m + 1, z)))
    layer(w2_ref, a2_ref, mw - 2, lambda m, z: spread(a3_ref, m, inside(m + 2, z)))

    head = head_ref[...]

    def score(m, z):
        z = z * head
        for row in range(h):
            s_ref[row, m : m + 1, :] = jnp.sum(z[row * f : (row + 1) * f], axis=0, keepdims=True)

    layer(w3_ref, a3_ref, mw - 4, score)

    disp = (d - 1) - lane_iota((dm.bw, d))
    column = base + lax.broadcasted_iota(jnp.int32, (dm.bw, d), 0)
    valid = column >= disp
    disp_f = disp.astype(jnp.float32)
    bands, disparity = [], []
    for row in range(h):
        s = jnp.where(valid, s_ref[row], masked_value)
        top = jnp.max(s, axis=1, keepdims=True)
        weighting = jnp.where(valid, jnp.exp(s - top), 0.0)
        denominator = jnp.sum(weighting, axis=1, keepdims=True)
        disp_sum = jnp.sum(weighting * disp_f, axis=1, keepdims=True)
        disparity.append(disp_sum / denominator / d)
        band = widen(weighting / denominator, dm.lw)
        bands.append(pltpu.roll(band, 3, 1, stride=1, stride_axis=0))
    band = jnp.concatenate(bands, axis=0)
    high = band.astype(jnp.bfloat16)
    low = (band - high.astype(jnp.float32)).astype(jnp.bfloat16)
    sums = lax.dot_general(
        x_ref[...],
        jnp.concatenate([high, low], axis=0),
        (((1,), (1,)), ((), ())),
        preferred_element_type=jnp.float32,
    )
    hb = h * dm.bw
    sums = widen(sums, round_up(2 * hb, LANES))
    sums = sums + rolled(sums, -hb)
    row = lax.broadcasted_iota(jnp.int32, sums.shape, 0) % h
    warped = sums
    for k in range(1, h):
        warped = jnp.where(row == k, rolled(sums, -k * dm.bw), warped)
    warped = warped[:, :LANES]

    eye = lane_iota((dm.bw, LANES)) == lax.broadcasted_iota(jnp.int32, (dm.bw, LANES), 0)
    lines = [jnp.sum(jnp.where(eye, v, 0.0), axis=0, keepdims=True) for v in disparity]
    lines.append(jnp.zeros((dm.lg * dm.rg - dm.own_rows - h, LANES), jnp.float32))
    lines = jnp.concatenate(lines, axis=0)
    lane = lane_iota((dm.rg, LANES))
    for j in range(dm.n):
        mine = jnp.concatenate([warped[j * dm.own_rows : (j + 1) * dm.own_rows], lines], axis=0)
        packed = mine[: dm.rg]
        for g in range(1, dm.lg):
            packed = jnp.where(
                (lane >= g * dm.bw) & (lane < (g + 1) * dm.bw),
                rolled(mine[g * dm.rg : (g + 1) * dm.rg], g * dm.bw),
                packed,
            )
        out_ref[(j // 2 ^ chip) * 2 + j % 2] = packed


def unpack_kernel(dm, y_ref, warped_ref, disparity_ref):
    per = LANES // dm.bw
    lane = lane_iota((dm.rg, LANES))
    tiles = []
    for t in range(dm.n // per):
        groups = []
        for g in range(dm.lg):
            total = None
            for p in range(per):
                piece = rolled(y_ref[t * per + p], (p - g) * dm.bw)
                keep = (lane >= p * dm.bw) & (lane < (p + 1) * dm.bw)
                total = piece if total is None else jnp.where(keep, piece, total)
            groups.append(total)
        tiles.append(jnp.concatenate(groups, axis=0))
    full = jnp.concatenate(tiles, axis=1)
    warped_ref[...] = full[: dm.own_rows].reshape(warped_ref.shape).astype(warped_ref.dtype)
    disparity_ref[...] = full[dm.own_rows : dm.own_rows + dm.h]


def shards(left_feat, right_feat, conv1_w, conv2_w, conv3_w, head_w):
    n, strips = lax.axis_size("disp"), lax.axis_size("col")
    dm = Dims(left_feat.shape, conv1_w.shape, conv2_w.shape, n, strips)
    bf, f32 = jnp.bfloat16, jnp.float32

    def call(kernel, out_shape, operands, mib=8, in_hbm=False, **options):
        spec = VMEM
        if in_hbm:
            spec = pl.BlockSpec(memory_space=pltpu.HBM)
            operands = [pltpu.with_memory_space_constraint(v, pltpu.HBM) for v in operands]
        return pl.pallas_call(
            functools.partial(kernel, dm),
            out_shape=out_shape,
            in_specs=[spec] * len(operands),
            out_specs=jax.tree.map(lambda _: VMEM, out_shape),
            compiler_params=pltpu.CompilerParams(vmem_limit_bytes=mib << 20),
            **options,
        )(*operands)

    wide = max(round_up(dm.hops[0] + 3, LANES), dm.strip)
    widths = [wide, wide] + [round_up(c, LANES) for c in dm.hops[1:]]
    *edges, left, right = call(
        edge_kernel,
        [jax.ShapeDtypeStruct((dm.own_rows, w), bf) for w in widths + [dm.strip] * 2],
        [left_feat, right_feat],
        in_hbm=True,
        scratch_shapes=[
            pltpu.VMEM(left_feat.shape, bf),
            pltpu.VMEM(left_feat.shape, bf),
            pltpu.SemaphoreType.DMA((2,)),
        ],
    )
    arrived = []
    for first in range(2):
        pairs = [(s, s + 1) for s in range(first, strips - 1, 2)]
        pairs += [(b, a) for a, b in pairs]
        arrived.append(lax.ppermute(edges[first], "col", pairs))
    for k, e in enumerate(edges[2:], 2):
        arrived.append(lax.ppermute(e, "col", [(s, s + k) for s in range(strips - k)]))

    kernels = [w.transpose(2, 3, 4, 0, 1).reshape(27, w.shape[0], w.shape[1]) for w in (conv1_w, conv2_w, conv3_w)]
    arrived, kernels = lax.optimization_barrier((arrived, kernels))
    m3 = 3 * dm.h * dm.f
    depths = [3 * dm.h * w.shape[2] for w in kernels]
    w1, w2, w3, head = call(
        prep_kernel,
        [jax.ShapeDtypeStruct((m3, k), bf) for k in depths]
        + [jax.ShapeDtypeStruct((dm.h * dm.f, dm.d), f32)],
        kernels + [head_w[None]],
        in_hbm=True,
        scratch_shapes=[pltpu.VMEM(w.shape, bf) for w in kernels]
        + [pltpu.VMEM((1, dm.f), f32), pltpu.SemaphoreType.DMA((4,))],
    )

    own_window, *windows = call(
        pack_kernel,
        [jax.ShapeDtypeStruct((dm.own_rows, dm.lw2), bf)] * dm.chips,
        [left, right] + arrived,
        scratch_shapes=[pltpu.VMEM((dm.chips, dm.own_rows, dm.lw2), bf)],
    )
    windows = [own_window] + [
        lax.ppermute(v, "disp", [(i, i ^ (2 * m)) for i in range(n)])
        for m, v in enumerate(windows, 1)
    ]
    windows, (w1, w2, w3, head) = lax.optimization_barrier((windows, (w1, w2, w3, head)))
    half = jax.ShapeDtypeStruct((dm.chips, dm.own_rows, dm.lw), bf)
    keep, give = call(split_kernel, [half, half], windows)
    got = lax.ppermute(give, "disp", [(i, i ^ 1) for i in range(n)])

    r_max = max(dm.chunks) * dm.h
    columns = [dm.mw, dm.mw - 2, dm.mw - 4]
    packed = call(
        main_kernel,
        jax.ShapeDtypeStruct((n, dm.rg, LANES), f32),
        [keep, got, w1, w2, w3, head],
        mib=32,
        scratch_shapes=[
            pltpu.VMEM((dm.rows, dm.lw), bf),
            pltpu.VMEM((dm.lw - dm.lb, dm.rows), f32),
            pltpu.VMEM((dm.mw * r_max, KROWS), bf),
            pltpu.VMEM((len(dm.chunks), dm.mw * r_max, dm.lw), f32),
            pltpu.VMEM((depths[0], columns[0] * dm.d), bf),
            pltpu.VMEM((depths[1], columns[1] * dm.d), bf),
            pltpu.VMEM((depths[2], columns[2] * dm.d), bf),
            pltpu.VMEM((m3, columns[0] * dm.d), f32),
            pltpu.VMEM((dm.h, dm.bw, dm.d), f32),
        ],
    )
    y = lax.all_to_all(packed, "disp", 0, 0)
    return tuple(
        call(
            unpack_kernel,
            [
                jax.ShapeDtypeStruct(left_feat.shape, bf),
                jax.ShapeDtypeStruct((dm.h, dm.strip), f32),
            ],
            [y],
        )
    )


def solution(mesh):
    return jax.shard_map(
        shards,
        mesh=mesh,
        in_specs=(P("disp", None, "col"), P("disp", None, "col"), P(), P(), P(), P()),
        out_specs=(P("disp", None, "col"), P(None, "col")),
        check_vma=False,
    )
```

```python
import functools

import jax
import jax.numpy as jnp
from jax import lax
from jax.experimental import pallas as pl
from jax.experimental.pallas import tpu as pltpu
from jax.sharding import PartitionSpec as P

DG = 16
CG = 8
LANES = 128
KROWS = 256
TILE = 4
TERMS = 3
VMEM = pl.BlockSpec(memory_space=pltpu.VMEM)

masked_value = -1e30


def round_up(value, unit):
    return -(-value // unit) * unit


class Dims:
    def __init__(self, left, conv1, conv2, groups_disp, strips):
        own, self.h, self.strip = left
        self.n = groups_disp
        self.strips = strips
        self.own_rows = own * self.h
        self.rows = self.own_rows * self.n
        self.d = DG * self.n
        self.bw = self.strip // self.n
        self.mw = self.bw + 6
        self.tail = self.d + 2
        self.g = conv1[1]
        self.f = conv2[0]
        self.lo = round_up(self.mw + self.d - 1, 8)
        self.lb = self.lo // LANES * LANES
        self.lw = round_up(self.lo + self.mw, LANES)
        self.hops = []
        left_over = self.tail
        while left_over > 0:
            self.hops.append(min(left_over, self.strip))
            left_over -= self.strip
        per = KROWS // (CG * self.h)
        self.chunks = [min(per, self.g - k) for k in range(0, self.g, per)]
        self.chips = self.n // 2
        self.lo2 = round_up(self.mw + self.bw + self.d - 1, 8)
        self.lw2 = round_up(self.lo2 + self.mw + self.bw, LANES)
        self.lg = LANES // self.bw
        self.rg = round_up(-(-(self.own_rows + TERMS * self.h) // self.lg), 8)


def lane_iota(shape):
    return lax.broadcasted_iota(jnp.int32, shape, 1)


def widen(x, lanes):
    have = x.shape[1]
    if have == lanes:
        return x
    return jnp.concatenate([x, jnp.zeros((x.shape[0], lanes - have), x.dtype)], axis=1)


def rolled(x, shift):
    shift %= x.shape[1]
    return x if shift == 0 else pltpu.roll(x, shift, 1)


def flat(ref):
    return ref[...].astype(jnp.float32).reshape(-1, ref.shape[-1])


def copied_in(sources, targets, sems):
    copies = [
        pltpu.make_async_copy(source, target, sems.at[k])
        for k, (source, target) in enumerate(zip(sources, targets))
    ]
    for copy in copies:
        copy.start()
    return [copy.wait for copy in copies]


def edge_kernel(dm, left_hbm, right_hbm, *refs):
    *outs, flat_left_ref, flat_right_ref, left_ref, right_ref, sems = refs
    for wait in copied_in((left_hbm, right_hbm), (left_ref, right_ref), sems):
        wait()
    left, right = flat(left_ref), flat(right_ref)
    flat_left_ref[...] = left.astype(flat_left_ref.dtype)
    flat_right_ref[...] = right.astype(flat_right_ref.dtype)
    width = outs[0].shape[1]
    count = dm.hops[0]
    lane = lane_iota((dm.own_rows, width))
    last = rolled(widen(right, width), count - dm.strip)
    edge = rolled(widen(left, width), count + 3 - dm.strip)
    up = jnp.where(lane < count, last, edge)
    down = jnp.where(lane < 3, widen(right, width), rolled(widen(left, width), 3))
    even = lax.axis_index("col") % 2 == 0
    outs[0][...] = jnp.where(even, up, down).astype(outs[0].dtype)
    outs[1][...] = jnp.where(even, down, up).astype(outs[1].dtype)
    for out, count in zip(outs[2:], dm.hops[1:]):
        out[...] = rolled(right, count - dm.strip)[:, : out.shape[1]].astype(out.dtype)


def pack_kernel(dm, left_ref, right_ref, pair0_ref, pair1_ref, *refs):
    more, outs, windows_ref = refs[: len(dm.hops) - 1], refs[len(dm.hops) - 1 : -1], refs[-1]
    left, right = flat(left_ref), flat(right_ref)
    pair0, pair1 = flat(pair0_ref), flat(pair1_ref)
    even = lax.axis_index("col") % 2 == 0
    up = jnp.where(even, pair1, pair0)
    down = jnp.where(even, pair0, pair1)[:, :LANES]
    ext = max(round_up(dm.tail + dm.strip + 3, LANES), dm.lw2, up.shape[1])
    lane = lane_iota((dm.own_rows, ext))
    row = rolled(widen(right, ext), dm.tail)
    row = jnp.where(lane < dm.tail + dm.strip, row, rolled(widen(down, ext), dm.tail + dm.strip))
    pieces = [up] + [flat(ref) for ref in more]
    for k, count in enumerate(dm.hops):
        start = dm.tail - sum(dm.hops[: k + 1])
        piece = rolled(widen(pieces[k], ext), start)
        row = jnp.where((lane >= start) & (lane < start + count), piece, row)
    lext = max(round_up(dm.strip + 6, LANES), dm.lw2, up.shape[1])
    lane_l = lane_iota((dm.own_rows, lext))
    lrow = rolled(widen(left, lext), 3)
    lrow = jnp.where(lane_l < 3, rolled(widen(up, lext), -dm.hops[0]), lrow)
    lrow = jnp.where(lane_l >= dm.strip + 3, rolled(widen(down, lext), dm.strip), lrow)
    lane_o = lane_iota((dm.own_rows, dm.lw2))
    for q in range(dm.chips):
        a = rolled(row, -2 * dm.bw * q)[:, : dm.lw2]
        b = rolled(lrow, dm.lo2 - 2 * dm.bw * q)[:, : dm.lw2]
        windows_ref[q] = jnp.where(lane_o < dm.lo2, a, b).astype(windows_ref.dtype)
    chip = lax.axis_index("disp") // 2
    for m, out in enumerate(outs):
        out[...] = windows_ref[chip ^ m]


def split_kernel(dm, *refs):
    *windows, keep_ref, give_ref = refs
    first_core = lax.axis_index("disp") % 2 == 0
    for m, ref in enumerate(windows):
        x = flat(ref)
        lane = lane_iota((dm.own_rows, dm.lw))
        parts = []
        for core in range(2):
            a = rolled(x, -core * dm.bw)[:, : dm.lw]
            b = rolled(x, dm.lo - dm.lo2 - core * dm.bw)[:, : dm.lw]
            parts.append(jnp.where(lane < dm.lo, a, b))
        keep_ref[m] = jnp.where(first_core, parts[0], parts[1]).astype(keep_ref.dtype)
        give_ref[m] = jnp.where(first_core, parts[1], parts[0]).astype(give_ref.dtype)


def prep_kernel(dm, *refs):
    outs, targets, sems = refs[4:8], refs[8:12], refs[12]
    waits = copied_in(refs[:4], targets, sems)
    w1_ref, w2_ref, w3_ref, head_ref = targets
    o1_ref, o2_ref, o3_ref, column_ref = outs
    chip = lax.axis_index("disp") // 2
    for layer, (w_ref, o_ref) in enumerate(((w1_ref, o1_ref), (w2_ref, o2_ref), (w3_ref, o3_ref))):
        inputs = w_ref.shape[2]
        per_a = dm.h * inputs
        waits[layer]()
        shape = (inputs, 3 * per_a)
        i = lax.broadcasted_iota(jnp.int32, shape, 0)
        if layer == 0:
            per_chip = inputs // dm.chips
            i = ((i // per_chip) ^ chip) * per_chip + i % per_chip
        col = lane_iota(shape)
        total = None
        for a in range(3):
            for hi in range(dm.h):
                if layer == 0:
                    pos = jnp.zeros(shape, jnp.int32)
                    first = 0
                    for count in dm.chunks:
                        here = first * dm.h + hi * count + (i - first)
                        pos = jnp.where(i >= first, here, pos)
                        first += count
                else:
                    pos = hi * inputs + i
                place = jnp.where(col == a * per_a + pos, 1.0, 0.0).astype(jnp.bfloat16)
                blocks = []
                for e in range(3):
                    for ho in range(dm.h):
                        b = hi - ho + 1
                        if 0 <= b <= 2:
                            blocks.append(w_ref[(a * 3 + b) * 3 + e])
                        else:
                            blocks.append(jnp.zeros((dm.f, inputs), jnp.bfloat16))
                term = jnp.dot(
                    jnp.concatenate(blocks, axis=0), place, preferred_element_type=jnp.float32
                )
                total = term if total is None else total + term
        o_ref[...] = total.astype(o_ref.dtype)
    waits[3]()
    square = (dm.f, dm.f)
    eye = lane_iota(square) == lax.broadcasted_iota(jnp.int32, square, 0)
    column = jnp.sum(jnp.where(eye, head_ref[...], 0.0), axis=1, keepdims=True)
    column = jnp.broadcast_to(column, (dm.f, dm.d))
    column_ref[...] = jnp.concatenate([column] * dm.h, axis=0)


def main_kernel(dm, keep_ref, got_ref, w1_ref, w2_ref, w3_ref, head_ref, out_ref, x_ref, lt_ref, lhs_ref, pc_ref, a1_ref, a2_ref, a3_ref, p1_ref, p2_ref, p3_ref, s_ref):
    d, mw, h, f, bf = dm.d, dm.mw, dm.h, dm.f, jnp.bfloat16
    chip, core = lax.axis_index("disp") // 2, lax.axis_index("disp") % 2
    base = lax.axis_index("col") * dm.strip + lax.axis_index("disp") * dm.bw
    total = dm.strips * dm.strip

    for m in range(dm.chips):
        kept, got = flat(keep_ref.at[m]), flat(got_ref.at[m])
        both = [jnp.where(core == 0, kept, got), jnp.where(core == 0, got, kept)]
        rows = 2 * dm.own_rows
        both = jnp.concatenate(both, axis=0)
        x_ref[m * rows : (m + 1) * rows] = both.astype(bf)
        lt_ref[:, m * rows : (m + 1) * rows] = jnp.transpose(both[:, dm.lb :]) * (1.0 / CG)

    keeps = []
    for count in dm.chunks:
        r, q = count * h, count * CG * h
        lane = lane_iota((r, q))
        sub = lax.broadcasted_iota(jnp.int32, (r, q), 0)
        keeps.append((lane % h == sub // count) & (lane // (CG * h) == sub % count))

    def correlate(m0, m1):
        first = 0
        for k, count in enumerate(dm.chunks):
            r, q = count * h, count * CG * h
            for m in range(m0, m1):
                at = dm.lo - dm.lb + m
                line = jnp.broadcast_to(lt_ref[at : at + 1, first : first + q], (r, q))
                lhs_ref[k, m * r : (m + 1) * r, :q] = jnp.where(keeps[k], line, 0.0).astype(bf)
            pc_ref[k, m0 * r : m1 * r] = jnp.dot(
                lhs_ref[k, m0 * r : m1 * r, :q],
                x_ref[first : first + q, :],
                preferred_element_type=jnp.float32,
            )
            first += q

    lanes = {}

    def spread(ref, m, v):
        rows = v.shape[0]
        if rows not in lanes:
            lanes[rows] = lane_iota((rows, d))
        lane = lanes[rows]
        at = slice(m * d, (m + 1) * d)
        zero = jnp.zeros_like(v)
        ref[:rows, at] = jnp.where(lane < d - 1, rolled(v, -1), zero)
        ref[rows : 2 * rows, at] = v
        ref[2 * rows :, at] = jnp.where(lane > 0, rolled(v, 1), zero)

    def volume(m0, m1):
        for m in range(m0, m1):
            parts = [pc_ref[k, m * c * h : (m + 1) * c * h].astype(bf) for k, c in enumerate(dm.chunks)]
            spread(a1_ref, m, rolled(jnp.concatenate(parts, axis=0), -m)[:, :d])

    def product(w_ref, a_ref, p_ref):
        def run(m0, m1):
            at = slice(m0 * d, m1 * d)
            p_ref[:, at] = jnp.dot(w_ref[...], a_ref[:, at], preferred_element_type=jnp.float32)

        return run

    def taken(p_ref, emit):
        fh = f * h

        def run(m0, m1):
            for m in range(m0, m1):
                z = p_ref[:fh, m * d : (m + 1) * d]
                z = z + p_ref[fh : 2 * fh, (m + 1) * d : (m + 2) * d]
                z = z + p_ref[2 * fh :, (m + 2) * d : (m + 3) * d]
                emit(m, jnp.maximum(z, 0.0))

        return run

    def activity(a_ref, margin):
        def emit(m, z):
            column = m + margin
            if not 3 <= column < mw - 3:
                at = base - 3 + column
                z = jnp.where((at >= 0) & (at < total), z, 0.0)
            spread(a_ref, m, z.astype(bf))

        return emit

    head = head_ref[...]

    def score(m, z):
        z = z * head
        for row in range(h):
            s_ref[row, m : m + 1, :] = jnp.sum(z[row * f : (row + 1) * f], axis=0, keepdims=True)

    stages = [
        (correlate, mw, 0),
        (volume, mw, 0),
        (product(w1_ref, a1_ref, p1_ref), mw, 0),
        (taken(p1_ref, activity(a2_ref, 1)), mw - 2, 2),
        (product(w2_ref, a2_ref, p2_ref), mw - 2, 0),
        (taken(p2_ref, activity(a3_ref, 2)), mw - 4, 2),
        (product(w3_ref, a3_ref, p3_ref), mw - 4, 0),
        (taken(p3_ref, score), mw - 6, 2),
    ]
    done = [0] * len(stages)
    while done[-1] < stages[-1][1]:
        before = list(done)
        for k in reversed(range(len(stages))):
            run, count, beyond = stages[k]
            ready = count if k == 0 else min(count, before[k - 1] - beyond)
            last = ready == count
            size = ready - done[k] if last else (ready - done[k]) // TILE * TILE
            size = min(size, TILE)
            if size > 0:
                run(done[k], done[k] + size)
                done[k] += size

    disp = (d - 1) - lane_iota((dm.bw, d))
    column = base + lax.broadcasted_iota(jnp.int32, (dm.bw, d), 0)
    valid = column >= disp
    disp_f = disp.astype(jnp.float32)
    bands, disparity = [], []
    for row in range(h):
        s = jnp.where(valid, s_ref[row], masked_value)
        top = jnp.max(s, axis=1, keepdims=True)
        weighting = jnp.where(valid, jnp.exp(s - top), 0.0)
        denominator = jnp.sum(weighting, axis=1, keepdims=True)
        disp_sum = jnp.sum(weighting * disp_f, axis=1, keepdims=True)
        disparity.append(disp_sum / denominator / d)
        band = widen(weighting / denominator, dm.lw)
        band = pltpu.roll(band, 3, 1, stride=1, stride_axis=0)
        bands += [band] * dm.lg
    band = jnp.concatenate(bands, axis=0)
    high = band.astype(bf)
    low = (band - high.astype(jnp.float32)).astype(bf)
    sums = None
    for part in (high, low):
        term = lax.dot_general(
            x_ref[...], part, (((1,), (1,)), ((), ())), preferred_element_type=jnp.float32
        )
        sums = term if sums is None else sums + term
    row = lax.broadcasted_iota(jnp.int32, (dm.rows, LANES), 0) % h
    warped = sums[:, :LANES]
    for k in range(1, h):
        warped = jnp.where(row == k, sums[:, k * LANES : (k + 1) * LANES], warped)

    eye = lane_iota((dm.bw, LANES)) % dm.bw == lax.broadcasted_iota(jnp.int32, (dm.bw, LANES), 0)
    rest = [jnp.sum(jnp.where(eye, v, 0.0), axis=0, keepdims=True) for v in disparity]
    lines = []
    for _ in range(TERMS):
        terms = [v.astype(bf).astype(jnp.float32) for v in rest]
        rest = [v - t for v, t in zip(rest, terms)]
        lines += terms
    lines.append(jnp.zeros((dm.lg * dm.rg - dm.own_rows - len(lines), LANES), jnp.float32))
    lines = jnp.concatenate(lines, axis=0)
    group = lane_iota((dm.rg, LANES)) // dm.bw
    for j in range(dm.n):
        mine = jnp.concatenate([warped[j * dm.own_rows : (j + 1) * dm.own_rows], lines], axis=0)
        packed = mine[: dm.rg]
        for g in range(1, dm.lg):
            packed = jnp.where(group == g, mine[g * dm.rg : (g + 1) * dm.rg], packed)
        out_ref[(j // 2 ^ chip) * 2 + j % 2] = packed.astype(out_ref.dtype)


def unpack_kernel(dm, y_ref, warped_ref, disparity_ref):
    per = LANES // dm.bw
    lane = lane_iota((dm.rg, LANES))
    tiles = []
    for t in range(dm.n // per):
        groups = []
        for g in range(dm.lg):
            total = None
            for p in range(per):
                piece = rolled(flat(y_ref.at[t * per + p]), (p - g) * dm.bw)
                keep = (lane >= p * dm.bw) & (lane < (p + 1) * dm.bw)
                total = piece if total is None else jnp.where(keep, piece, total)
            groups.append(total)
        tiles.append(jnp.concatenate(groups, axis=0))
    full = jnp.concatenate(tiles, axis=1)
    warped_ref[...] = full[: dm.own_rows].reshape(warped_ref.shape).astype(warped_ref.dtype)
    total = None
    for k in reversed(range(TERMS)):
        at = dm.own_rows + k * dm.h
        term = full[at : at + dm.h]
        total = term if total is None else term + total
    disparity_ref[...] = total


def shards(left_feat, right_feat, conv1_w, conv2_w, conv3_w, head_w):
    n, strips = lax.axis_size("disp"), lax.axis_size("col")
    dm = Dims(left_feat.shape, conv1_w.shape, conv2_w.shape, n, strips)
    bf, f32 = jnp.bfloat16, jnp.float32

    def call(kernel, out_shape, operands, mib=8, in_hbm=False, **options):
        spec = VMEM
        if in_hbm:
            spec = pl.BlockSpec(memory_space=pltpu.HBM)
            operands = [pltpu.with_memory_space_constraint(v, pltpu.HBM) for v in operands]
        return pl.pallas_call(
            functools.partial(kernel, dm),
            out_shape=out_shape,
            in_specs=[spec] * len(operands),
            out_specs=jax.tree.map(lambda _: VMEM, out_shape),
            compiler_params=pltpu.CompilerParams(vmem_limit_bytes=mib << 20),
            **options,
        )(*operands)

    wide = max(round_up(dm.hops[0] + 3, LANES), dm.strip)
    widths = [wide, wide] + [round_up(c, LANES) for c in dm.hops[1:]]
    *edges, left, right = call(
        edge_kernel,
        [jax.ShapeDtypeStruct((dm.own_rows, w), bf) for w in widths + [dm.strip] * 2],
        [left_feat, right_feat],
        in_hbm=True,
        scratch_shapes=[
            pltpu.VMEM(left_feat.shape, bf),
            pltpu.VMEM(left_feat.shape, bf),
            pltpu.SemaphoreType.DMA((2,)),
        ],
    )
    arrived = []
    for first in range(2):
        pairs = [(s, s + 1) for s in range(first, strips - 1, 2)]
        pairs += [(b, a) for a, b in pairs]
        arrived.append(lax.ppermute(edges[first], "col", pairs))
    for k, e in enumerate(edges[2:], 2):
        arrived.append(lax.ppermute(e, "col", [(s, s + k) for s in range(strips - k)]))

    kernels = [w.transpose(2, 3, 4, 0, 1).reshape(27, w.shape[0], w.shape[1]) for w in (conv1_w, conv2_w, conv3_w)]
    arrived, kernels = lax.optimization_barrier((arrived, kernels))
    m3 = 3 * dm.h * dm.f
    depths = [3 * dm.h * w.shape[2] for w in kernels]
    w1, w2, w3, head = call(
        prep_kernel,
        [jax.ShapeDtypeStruct((m3, k), bf) for k in depths]
        + [jax.ShapeDtypeStruct((dm.h * dm.f, dm.d), f32)],
        kernels + [head_w[None]],
        in_hbm=True,
        scratch_shapes=[pltpu.VMEM(w.shape, bf) for w in kernels]
        + [pltpu.VMEM((1, dm.f), f32), pltpu.SemaphoreType.DMA((4,))],
    )

    own_window, *windows = call(
        pack_kernel,
        [jax.ShapeDtypeStruct((dm.own_rows, dm.lw2), bf)] * dm.chips,
        [left, right] + arrived,
        scratch_shapes=[pltpu.VMEM((dm.chips, dm.own_rows, dm.lw2), bf)],
    )
    windows = [own_window] + [
        lax.ppermute(v, "disp", [(i, i ^ (2 * m)) for i in range(n)])
        for m, v in enumerate(windows, 1)
    ]
    windows, (w1, w2, w3, head) = lax.optimization_barrier((windows, (w1, w2, w3, head)))
    half = jax.ShapeDtypeStruct((dm.chips, dm.own_rows, dm.lw), bf)
    keep, give = call(split_kernel, [half, half], windows)
    got = lax.ppermute(give, "disp", [(i, i ^ 1) for i in range(n)])

    r_max = max(dm.chunks) * dm.h
    columns = [dm.mw, dm.mw - 2, dm.mw - 4]
    packed = call(
        main_kernel,
        jax.ShapeDtypeStruct((n, dm.rg, LANES), bf),
        [keep, got, w1, w2, w3, head],
        mib=32,
        scratch_shapes=[
            pltpu.VMEM((dm.rows, dm.lw), bf),
            pltpu.VMEM((dm.lw - dm.lb, dm.rows), f32),
            pltpu.VMEM((len(dm.chunks), dm.mw * r_max, KROWS), bf),
            pltpu.VMEM((len(dm.chunks), dm.mw * r_max, dm.lw), f32),
            *[pltpu.VMEM((k, c * dm.d), bf) for k, c in zip(depths, columns)],
            *[pltpu.VMEM((m3, c * dm.d), f32) for c in columns],
            pltpu.VMEM((dm.h, dm.bw, dm.d), f32),
        ],
    )
    y = lax.all_to_all(packed, "disp", 0, 0)
    return tuple(
        call(
            unpack_kernel,
            [
                jax.ShapeDtypeStruct(left_feat.shape, bf),
                jax.ShapeDtypeStruct((dm.h, dm.strip), f32),
            ],
            [y],
        )
    )


def solution(mesh):
    return jax.shard_map(
        shards,
        mesh=mesh,
        in_specs=(P("disp", None, "col"), P("disp", None, "col"), P(), P(), P(), P()),
        out_specs=(P("disp", None, "col"), P(None, "col")),
        check_vma=False,
    )
```

```python
import functools

import jax
import jax.numpy as jnp
from jax import lax
from jax.experimental import pallas as pl
from jax.experimental.pallas import tpu as pltpu
from jax.sharding import PartitionSpec as P

DG = 16
CG = 8
LANES = 128
KROWS = 256
TILE = 8
TERMS = 3
VMEM = pl.BlockSpec(memory_space=pltpu.VMEM)

masked_value = -1e30


def round_up(value, unit):
    return -(-value // unit) * unit


class Dims:
    def __init__(self, left, conv1, conv2, groups_disp, strips):
        own, self.h, self.strip = left
        self.n = groups_disp
        self.strips = strips
        self.own_rows = own * self.h
        self.rows = self.own_rows * self.n
        self.d = DG * self.n
        self.bw = self.strip // self.n
        self.mw = self.bw + 6
        self.tail = self.d + 2
        self.g = conv1[1]
        self.f = conv2[0]
        self.lo = round_up(self.mw + self.d - 1, 8)
        self.lb = self.lo // LANES * LANES
        self.lw = round_up(self.lo + self.mw, LANES)
        self.hops = []
        left_over = self.tail
        while left_over > 0:
            self.hops.append(min(left_over, self.strip))
            left_over -= self.strip
        self.chips = self.n // 2
        self.lo2 = round_up(self.mw + self.bw + self.d - 1, 8)
        self.lw2 = round_up(self.lo2 + self.mw + self.bw, LANES)
        per = KROWS // (CG * self.h)
        self.kept = self.g // 2
        self.full = self.kept // per * per
        rest = 2 * (self.kept - self.full)
        self.split = own % CG == 0 and self.full > 0 and rest <= per and rest * self.h % 16 == 0
        if self.split:
            self.chunks = [per] * (2 * self.full // per) + ([rest] if rest else [])
            self.early = self.full // per
        else:
            self.chunks = [min(per, self.g - k) for k in range(0, self.g, per)]
            self.early = 0
        self.early_rows = sum(self.chunks[: self.early]) * self.h
        self.lg = LANES // self.bw
        self.rg = round_up(-(-(self.own_rows + TERMS * self.h) // self.lg), 8)


def lane_iota(shape):
    return lax.broadcasted_iota(jnp.int32, shape, 1)


def widen(x, lanes):
    have = x.shape[1]
    if have == lanes:
        return x
    return jnp.concatenate([x, jnp.zeros((x.shape[0], lanes - have), x.dtype)], axis=1)


def rolled(x, shift):
    shift %= x.shape[1]
    return x if shift == 0 else pltpu.roll(x, shift, 1)


def flat(ref):
    return ref[...].astype(jnp.float32).reshape(-1, ref.shape[-1])


def copied_in(sources, targets, sems):
    copies = [
        pltpu.make_async_copy(source, target, sems.at[k])
        for k, (source, target) in enumerate(zip(sources, targets))
    ]
    for copy in copies:
        copy.start()
    return [copy.wait for copy in copies]


def edge_kernel(dm, left_hbm, right_hbm, *refs):
    *outs, flat_left_ref, flat_right_ref, left_ref, right_ref, sems = refs
    for wait in copied_in((left_hbm, right_hbm), (left_ref, right_ref), sems):
        wait()
    left, right = flat(left_ref), flat(right_ref)
    flat_left_ref[...] = left.astype(flat_left_ref.dtype)
    flat_right_ref[...] = right.astype(flat_right_ref.dtype)
    width = outs[0].shape[1]
    count = dm.hops[0]
    lane = lane_iota((dm.own_rows, width))
    last = rolled(widen(right, width), count - dm.strip)
    edge = rolled(widen(left, width), count + 3 - dm.strip)
    up = jnp.where(lane < count, last, edge)
    down = jnp.where(lane < 3, widen(right, width), rolled(widen(left, width), 3))
    even = lax.axis_index("col") % 2 == 0
    outs[0][...] = jnp.where(even, up, down).astype(outs[0].dtype)
    outs[1][...] = jnp.where(even, down, up).astype(outs[1].dtype)
    for out, count in zip(outs[2:], dm.hops[1:]):
        out[...] = rolled(right, count - dm.strip)[:, : out.shape[1]].astype(out.dtype)


def pack_kernel(dm, left_ref, right_ref, pair0_ref, pair1_ref, *refs):
    more, outs, windows_ref = refs[: len(dm.hops) - 1], refs[len(dm.hops) - 1 : -1], refs[-1]
    left, right = flat(left_ref), flat(right_ref)
    pair0, pair1 = flat(pair0_ref), flat(pair1_ref)
    even = lax.axis_index("col") % 2 == 0
    up = jnp.where(even, pair1, pair0)
    down = jnp.where(even, pair0, pair1)[:, :LANES]
    ext = max(round_up(dm.tail + dm.strip + 3, LANES), dm.lw2, up.shape[1])
    lane = lane_iota((dm.own_rows, ext))
    row = rolled(widen(right, ext), dm.tail)
    row = jnp.where(lane < dm.tail + dm.strip, row, rolled(widen(down, ext), dm.tail + dm.strip))
    pieces = [up] + [flat(ref) for ref in more]
    for k, count in enumerate(dm.hops):
        start = dm.tail - sum(dm.hops[: k + 1])
        piece = rolled(widen(pieces[k], ext), start)
        row = jnp.where((lane >= start) & (lane < start + count), piece, row)
    lext = max(round_up(dm.strip + 6, LANES), dm.lw2, up.shape[1])
    lane_l = lane_iota((dm.own_rows, lext))
    lrow = rolled(widen(left, lext), 3)
    lrow = jnp.where(lane_l < 3, rolled(widen(up, lext), -dm.hops[0]), lrow)
    lrow = jnp.where(lane_l >= dm.strip + 3, rolled(widen(down, lext), dm.strip), lrow)
    lane_o = lane_iota((dm.own_rows, dm.lw2))
    for q in range(dm.chips):
        a = rolled(row, -2 * dm.bw * q)[:, : dm.lw2]
        b = rolled(lrow, dm.lo2 - 2 * dm.bw * q)[:, : dm.lw2]
        windows_ref[q] = jnp.where(lane_o < dm.lo2, a, b).astype(windows_ref.dtype)
    chip = lax.axis_index("disp") // 2
    for m, out in enumerate(outs):
        out[...] = windows_ref[chip ^ m]


def split_kernel(dm, *refs):
    *windows, keep_ref, give_ref = refs
    first_core = lax.axis_index("disp") % 2 == 0
    for m, ref in enumerate(windows):
        x = flat(ref)
        lane = lane_iota((dm.own_rows, dm.lw))
        parts = []
        for core in range(2):
            a = rolled(x, -core * dm.bw)[:, : dm.lw]
            b = rolled(x, dm.lo - dm.lo2 - core * dm.bw)[:, : dm.lw]
            parts.append(jnp.where(lane < dm.lo, a, b))
        keep_ref[m] = jnp.where(first_core, parts[0], parts[1]).astype(keep_ref.dtype)
        give_ref[m] = jnp.where(first_core, parts[1], parts[0]).astype(give_ref.dtype)


def prep_kernel(dm, *refs):
    outs, targets, sems = refs[4:8], refs[8:12], refs[12]
    waits = copied_in(refs[:4], targets, sems)
    w1_ref, w2_ref, w3_ref, head_ref = targets
    o1_ref, o2_ref, o3_ref, column_ref = outs
    chip, core = lax.axis_index("disp") // 2, lax.axis_index("disp") % 2
    for layer, (w_ref, o_ref) in enumerate(((w1_ref, o1_ref), (w2_ref, o2_ref), (w3_ref, o3_ref))):
        inputs = w_ref.shape[2]
        per_a = dm.h * inputs
        waits[layer]()
        shape = (inputs, 3 * per_a)
        i = lax.broadcasted_iota(jnp.int32, shape, 0)
        if layer == 0 and dm.split:
            per_device = inputs // dm.n
            device = i // per_device
            side = (device % 2) ^ core
            i = ((device // 2) ^ chip) * per_device + i % per_device
            rest = 2 * dm.full + side * (dm.kept - dm.full) + i - dm.full
            i = jnp.where(i < dm.full, side * dm.full + i, rest)
        elif layer == 0:
            per_chip = inputs // dm.chips
            i = ((i // per_chip) ^ chip) * per_chip + i % per_chip
        col = lane_iota(shape)
        total = None
        for a in range(3):
            for hi in range(dm.h):
                if layer == 0:
                    pos = jnp.zeros(shape, jnp.int32)
                    first = 0
                    for count in dm.chunks:
                        here = first * dm.h + hi * count + (i - first)
                        pos = jnp.where(i >= first, here, pos)
                        first += count
                else:
                    pos = hi * inputs + i
                place = jnp.where(col == a * per_a + pos, 1.0, 0.0).astype(jnp.bfloat16)
                blocks = []
                for e in range(3):
                    for ho in range(dm.h):
                        b = hi - ho + 1
                        if 0 <= b <= 2:
                            blocks.append(w_ref[(a * 3 + b) * 3 + e])
                        else:
                            blocks.append(jnp.zeros((dm.f, inputs), jnp.bfloat16))
                term = jnp.dot(
                    jnp.concatenate(blocks, axis=0), place, preferred_element_type=jnp.float32
                )
                total = term if total is None else total + term
        o_ref[...] = total.astype(o_ref.dtype)
    waits[3]()
    square = (dm.f, dm.f)
    eye = lane_iota(square) == lax.broadcasted_iota(jnp.int32, square, 0)
    column = jnp.sum(jnp.where(eye, head_ref[...], 0.0), axis=1, keepdims=True)
    column = jnp.broadcast_to(column, (dm.f, dm.d))
    column_ref[...] = jnp.concatenate([column] * dm.h, axis=0)


def correlator(dm, chunks, x_of, lt_ref, lhs_ref, pc_ref):
    keeps = []
    for count in chunks:
        r, q = count * dm.h, count * CG * dm.h
        lane = lane_iota((r, q))
        sub = lax.broadcasted_iota(jnp.int32, (r, q), 0)
        keeps.append((lane % dm.h == sub // count) & (lane // (CG * dm.h) == sub % count))

    def run(m0, m1):
        first = 0
        for k, count in enumerate(chunks):
            r, q = count * dm.h, count * CG * dm.h
            for m in range(m0, m1):
                at = dm.lo - dm.lb + m
                line = jnp.broadcast_to(lt_ref[at : at + 1, first : first + q], (r, q))
                line = jnp.where(keeps[k], line, 0.0).astype(jnp.bfloat16)
                lhs_ref[k, m * r : (m + 1) * r, :q] = line
            pc_ref[k, m0 * r : m1 * r] = jnp.dot(
                lhs_ref[k, m0 * r : m1 * r, :q], x_of(k), preferred_element_type=jnp.float32
            )
            first += q

    return run


def shifts(v, lanes):
    if v.shape not in lanes:
        lanes[v.shape] = lane_iota(v.shape)
    lane, zero = lanes[v.shape], jnp.zeros_like(v)
    last = v.shape[1] - 1
    return (
        jnp.where(lane < last, rolled(v, -1), zero),
        v,
        jnp.where(lane > 0, rolled(v, 1), zero),
    )


def column_of(dm, chunks, pc_ref, m):
    parts = []
    for k, count in enumerate(chunks):
        r = count * dm.h
        parts.append(pc_ref[k, m * r : (m + 1) * r].astype(jnp.bfloat16))
    return rolled(jnp.concatenate(parts, axis=0), -m)[:, : dm.d]


def left_columns(dm, x):
    return jnp.transpose(x[:, dm.lb :].astype(jnp.float32)) * (1.0 / CG)


def pipeline(stages):
    done = [0] * len(stages)
    while done[-1] < stages[-1][1]:
        before = list(done)
        for k in reversed(range(len(stages))):
            run, count, beyond = stages[k]
            ready = count if k == 0 else min(count, before[k - 1] - beyond)
            size = ready - done[k] if ready == count else (ready - done[k]) // TILE * TILE
            size = min(size, TILE)
            if size > 0:
                run(done[k], done[k] + size)
                done[k] += size


def early_kernel(dm, keep_ref, part_ref, lt_ref, lhs_ref, pc_ref):
    chunks = dm.chunks[: dm.early]
    x = keep_ref[...].reshape(-1, dm.lw)
    rows = KROWS * dm.early
    lt_ref[...] = left_columns(dm, x[:rows])
    lanes = {}

    def volume(m0, m1):
        for m in range(m0, m1):
            for a, v in enumerate(shifts(column_of(dm, chunks, pc_ref, m), lanes)):
                part_ref[a, :, m * dm.d : (m + 1) * dm.d] = v

    x_of = lambda k: x[k * KROWS : (k + 1) * KROWS]
    pipeline([(correlator(dm, chunks, x_of, lt_ref, lhs_ref, pc_ref), dm.mw, 0), (volume, dm.mw, 0)])


def main_kernel(dm, keep_ref, got_ref, *refs):
    part_ref, refs = (refs[0], refs[1:]) if dm.split else (None, refs)
    w1_ref, w2_ref, w3_ref, head_ref, out_ref, x_ref, lt_ref, lhs_ref, pc_ref = refs[:9]
    a1_ref, a2_ref, a3_ref, p1_ref, p2_ref, p3_ref, s_ref = refs[9:]
    d, mw, h, f, bf = dm.d, dm.mw, dm.h, dm.f, jnp.bfloat16
    chip, core = lax.axis_index("disp") // 2, lax.axis_index("disp") % 2
    base = lax.axis_index("col") * dm.strip + lax.axis_index("disp") * dm.bw
    total = dm.strips * dm.strip
    chunks = dm.chunks[dm.early :]

    if dm.split:
        half, early = dm.rows // 2, KROWS * dm.early
        x_ref[:half] = keep_ref[...].reshape(half, dm.lw)
        x_ref[half:] = got_ref[...].reshape(half, dm.lw)
        sources = [x_ref[half + k * KROWS : half + (k + 1) * KROWS] for k in range(dm.early)]
        if early < half:
            rest = [keep_ref[...].reshape(half, dm.lw)[early:], got_ref[...].reshape(half, dm.lw)[early:]]
            sources.append(jnp.concatenate(rest, axis=0))
        at = 0
        for x in sources:
            lt_ref[:, at : at + x.shape[0]] = left_columns(dm, x)
            at += x.shape[0]
        x_of = lambda k: sources[k]
    else:
        rows = 2 * dm.own_rows
        for m in range(dm.chips):
            kept, got = flat(keep_ref.at[m]), flat(got_ref.at[m])
            both = [jnp.where(core == 0, kept, got), jnp.where(core == 0, got, kept)]
            both = jnp.concatenate(both, axis=0)
            x_ref[m * rows : (m + 1) * rows] = both.astype(bf)
            lt_ref[:, m * rows : (m + 1) * rows] = left_columns(dm, both)
        x_of = lambda k: x_ref[k * KROWS : k * KROWS + chunks[k] * CG * h]

    lanes = {}

    def spread(ref, m, v, first=0):
        rows = first + v.shape[0]
        for a, shifted in enumerate(shifts(v, lanes)):
            ref[a * rows + first : (a + 1) * rows, m * d : (m + 1) * d] = shifted

    def volume(m0, m1):
        for m in range(m0, m1):
            spread(a1_ref, m, column_of(dm, chunks, pc_ref, m), dm.early_rows)
            if dm.split:
                at = slice(m * d, (m + 1) * d)
                for a in range(3):
                    first = a * h * dm.g
                    a1_ref[first : first + dm.early_rows, at] = part_ref[a, :, at]

    def product(w_ref, a_ref, p_ref):
        def run(m0, m1):
            at = slice(m0 * d, m1 * d)
            p_ref[:, at] = jnp.dot(w_ref[...], a_ref[:, at], preferred_element_type=jnp.float32)

        return run

    def taken(p_ref, emit):
        fh = f * h

        def run(m0, m1):
            for m in range(m0, m1):
                z = p_ref[:fh, m * d : (m + 1) * d]
                z = z + p_ref[fh : 2 * fh, (m + 1) * d : (m + 2) * d]
                z = z + p_ref[2 * fh :, (m + 2) * d : (m + 3) * d]
                emit(m, jnp.maximum(z, 0.0))

        return run

    def activity(a_ref, margin):
        def emit(m, z):
            column = m + margin
            if not 3 <= column < mw - 3:
                at = base - 3 + column
                z = jnp.where((at >= 0) & (at < total), z, 0.0)
            spread(a_ref, m, z.astype(bf))

        return emit

    head = head_ref[...]

    def score(m, z):
        z = z * head
        for row in range(h):
            s_ref[row, m : m + 1, :] = jnp.sum(z[row * f : (row + 1) * f], axis=0, keepdims=True)

    stages = [
        (correlator(dm, chunks, x_of, lt_ref, lhs_ref, pc_ref), mw, 0),
        (volume, mw, 0),
        (product(w1_ref, a1_ref, p1_ref), mw, 0),
        (taken(p1_ref, activity(a2_ref, 1)), mw - 2, 2),
        (product(w2_ref, a2_ref, p2_ref), mw - 2, 0),
        (taken(p2_ref, activity(a3_ref, 2)), mw - 4, 2),
        (product(w3_ref, a3_ref, p3_ref), mw - 4, 0),
        (taken(p3_ref, score), mw - 6, 2),
    ]
    pipeline(stages)

    disp = (d - 1) - lane_iota((dm.bw, d))
    column = base + lax.broadcasted_iota(jnp.int32, (dm.bw, d), 0)
    valid = column >= disp
    disp_f = disp.astype(jnp.float32)
    bands, disparity = [], []
    for row in range(h):
        s = jnp.where(valid, s_ref[row], masked_value)
        top = jnp.max(s, axis=1, keepdims=True)
        weighting = jnp.where(valid, jnp.exp(s - top), 0.0)
        denominator = jnp.sum(weighting, axis=1, keepdims=True)
        disp_sum = jnp.sum(weighting * disp_f, axis=1, keepdims=True)
        disparity.append(disp_sum / denominator / d)
        band = widen(weighting / denominator, dm.lw)
        band = pltpu.roll(band, 3, 1, stride=1, stride_axis=0)
        bands += [band] * dm.lg
    band = jnp.concatenate(bands, axis=0)
    sums = lax.dot_general(
        x_ref[...], band.astype(bf), (((1,), (1,)), ((), ())), preferred_element_type=jnp.float32
    )
    row = lax.broadcasted_iota(jnp.int32, (dm.rows, LANES), 0) % h
    warped = sums[:, :LANES]
    for k in range(1, h):
        warped = jnp.where(row == k, sums[:, k * LANES : (k + 1) * LANES], warped)

    eye = lane_iota((dm.bw, LANES)) % dm.bw == lax.broadcasted_iota(jnp.int32, (dm.bw, LANES), 0)
    rest = [jnp.sum(jnp.where(eye, v, 0.0), axis=0, keepdims=True) for v in disparity]
    lines = []
    for _ in range(TERMS):
        terms = [v.astype(bf).astype(jnp.float32) for v in rest]
        rest = [v - t for v, t in zip(rest, terms)]
        lines += terms
    lines.append(jnp.zeros((dm.lg * dm.rg - dm.own_rows - len(lines), LANES), jnp.float32))
    lines = jnp.concatenate(lines, axis=0)
    group = lane_iota((dm.rg, LANES)) // dm.bw
    for j in range(dm.n):
        mine = jnp.concatenate([warped[j * dm.own_rows : (j + 1) * dm.own_rows], lines], axis=0)
        packed = mine[: dm.rg]
        for g in range(1, dm.lg):
            packed = jnp.where(group == g, mine[g * dm.rg : (g + 1) * dm.rg], packed)
        if dm.split:
            target = (j % dm.chips ^ chip) * 2 + (j // dm.chips ^ core)
        else:
            target = (j // 2 ^ chip) * 2 + j % 2
        out_ref[target] = packed.astype(out_ref.dtype)


def unpack_kernel(dm, y_ref, warped_ref, disparity_ref):
    per = LANES // dm.bw
    lane = lane_iota((dm.rg, LANES))
    tiles = []
    for t in range(dm.n // per):
        groups = []
        for g in range(dm.lg):
            total = None
            for p in range(per):
                piece = rolled(flat(y_ref.at[t * per + p]), (p - g) * dm.bw)
                keep = (lane >= p * dm.bw) & (lane < (p + 1) * dm.bw)
                total = piece if total is None else jnp.where(keep, piece, total)
            groups.append(total)
        tiles.append(jnp.concatenate(groups, axis=0))
    full = jnp.concatenate(tiles, axis=1)
    warped_ref[...] = full[: dm.own_rows].reshape(warped_ref.shape).astype(warped_ref.dtype)
    total = None
    for k in reversed(range(TERMS)):
        at = dm.own_rows + k * dm.h
        term = full[at : at + dm.h]
        total = term if total is None else term + total
    disparity_ref[...] = total


def shards(left_feat, right_feat, conv1_w, conv2_w, conv3_w, head_w):
    n, strips = lax.axis_size("disp"), lax.axis_size("col")
    dm = Dims(left_feat.shape, conv1_w.shape, conv2_w.shape, n, strips)
    bf, f32 = jnp.bfloat16, jnp.float32

    def call(kernel, out_shape, operands, mib=8, in_hbm=False, **options):
        spec = VMEM
        if in_hbm:
            spec = pl.BlockSpec(memory_space=pltpu.HBM)
            operands = [pltpu.with_memory_space_constraint(v, pltpu.HBM) for v in operands]
        return pl.pallas_call(
            functools.partial(kernel, dm),
            out_shape=out_shape,
            in_specs=[spec] * len(operands),
            out_specs=jax.tree.map(lambda _: VMEM, out_shape),
            compiler_params=pltpu.CompilerParams(vmem_limit_bytes=mib << 20),
            **options,
        )(*operands)

    wide = max(round_up(dm.hops[0] + 3, LANES), dm.strip)
    widths = [wide, wide] + [round_up(c, LANES) for c in dm.hops[1:]]
    *edges, left, right = call(
        edge_kernel,
        [jax.ShapeDtypeStruct((dm.own_rows, w), bf) for w in widths + [dm.strip] * 2],
        [left_feat, right_feat],
        in_hbm=True,
        scratch_shapes=[
            pltpu.VMEM(left_feat.shape, bf),
            pltpu.VMEM(left_feat.shape, bf),
            pltpu.SemaphoreType.DMA((2,)),
        ],
    )
    arrived = []
    for first in range(2):
        pairs = [(s, s + 1) for s in range(first, strips - 1, 2)]
        pairs += [(b, a) for a, b in pairs]
        arrived.append(lax.ppermute(edges[first], "col", pairs))
    for k, e in enumerate(edges[2:], 2):
        arrived.append(lax.ppermute(e, "col", [(s, s + k) for s in range(strips - k)]))

    kernels = [w.transpose(2, 3, 4, 0, 1).reshape(27, w.shape[0], w.shape[1]) for w in (conv1_w, conv2_w, conv3_w)]
    arrived, kernels = lax.optimization_barrier((arrived, kernels))
    m3 = 3 * dm.h * dm.f
    depths = [3 * dm.h * w.shape[2] for w in kernels]
    w1, w2, w3, head = call(
        prep_kernel,
        [jax.ShapeDtypeStruct((m3, k), bf) for k in depths]
        + [jax.ShapeDtypeStruct((dm.h * dm.f, dm.d), f32)],
        kernels + [head_w[None]],
        in_hbm=True,
        scratch_shapes=[pltpu.VMEM(w.shape, bf) for w in kernels]
        + [pltpu.VMEM((1, dm.f), f32), pltpu.SemaphoreType.DMA((4,))],
    )

    own_window, *windows = call(
        pack_kernel,
        [jax.ShapeDtypeStruct((dm.own_rows, dm.lw2), bf)] * dm.chips,
        [left, right] + arrived,
        scratch_shapes=[pltpu.VMEM((dm.chips, dm.own_rows, dm.lw2), bf)],
    )
    windows = [own_window] + [
        lax.ppermute(v, "disp", [(i, i ^ (2 * m)) for i in range(n)])
        for m, v in enumerate(windows, 1)
    ]
    windows, (w1, w2, w3, head) = lax.optimization_barrier((windows, (w1, w2, w3, head)))
    half = jax.ShapeDtypeStruct((dm.chips, dm.own_rows, dm.lw), bf)
    keep, give = call(split_kernel, [half, half], windows)
    got = lax.ppermute(give, "disp", [(i, i ^ 1) for i in range(n)])

    def stage(chunks):
        r = max(chunks) * dm.h
        return [
            pltpu.VMEM((dm.lw - dm.lb, sum(chunks) * CG * dm.h), f32),
            pltpu.VMEM((len(chunks), dm.mw * r, KROWS), bf),
            pltpu.VMEM((len(chunks), dm.mw * r, dm.lw), f32),
        ]

    columns = [dm.mw, dm.mw - 2, dm.mw - 4]
    operands = [keep, got]
    if dm.split:
        operands.append(
            call(
                early_kernel,
                jax.ShapeDtypeStruct((3, dm.early_rows, dm.mw * dm.d), bf),
                [keep],
                mib=16,
                scratch_shapes=stage(dm.chunks[: dm.early]),
            )
        )
    packed = call(
        main_kernel,
        jax.ShapeDtypeStruct((n, dm.rg, LANES), bf),
        operands + [w1, w2, w3, head],
        mib=32,
        scratch_shapes=[
            pltpu.VMEM((dm.rows, dm.lw), bf),
            *stage(dm.chunks[dm.early :]),
            *[pltpu.VMEM((k, c * dm.d), bf) for k, c in zip(depths, columns)],
            *[pltpu.VMEM((m3, c * dm.d), f32) for c in columns],
            pltpu.VMEM((dm.h, dm.bw, dm.d), f32),
        ],
    )
    y = lax.all_to_all(packed, "disp", 0, 0)
    return tuple(
        call(
            unpack_kernel,
            [
                jax.ShapeDtypeStruct(left_feat.shape, bf),
                jax.ShapeDtypeStruct((dm.h, dm.strip), f32),
            ],
            [y],
        )
    )


def solution(mesh):
    return jax.shard_map(
        shards,
        mesh=mesh,
        in_specs=(P("disp", None, "col"), P("disp", None, "col"), P(), P(), P(), P()),
        out_specs=(P("disp", None, "col"), P(None, "col")),
        check_vma=False,
    )
```

```python
import functools

import jax
import jax.numpy as jnp
from jax import lax
from jax.experimental import pallas as pl
from jax.experimental.pallas import tpu as pltpu
from jax.sharding import PartitionSpec as P


DG = 16
CG = 8
LANES = 128
KROWS = 256
TILE = 8
TERMS = 3
VMEM = pl.BlockSpec(memory_space=pltpu.VMEM)

masked_value = -1e30


def round_up(value, unit):
    return -(-value // unit) * unit


class Dims:
    def __init__(self, left, conv1, conv2, groups_disp, strips):
        own, self.h, self.strip = left
        self.n = groups_disp
        self.strips = strips
        self.own_rows = own * self.h
        self.rows = self.own_rows * self.n
        self.d = DG * self.n
        self.bw = self.strip // self.n
        self.mw = self.bw + 6
        self.tail = self.d + 2
        self.g = conv1[1]
        self.f = conv2[0]
        self.lo = round_up(self.mw + self.d - 1, 8)
        self.lb = self.lo // LANES * LANES
        self.lw = round_up(self.lo + self.mw, LANES)
        self.hops = []
        left_over = self.tail
        while left_over > 0:
            self.hops.append(min(left_over, self.strip))
            left_over -= self.strip
        self.chips = self.n // 2
        self.lo2 = round_up(self.mw + self.bw + self.d - 1, 8)
        self.lw2 = round_up(self.lo2 + self.mw + self.bw, LANES)
        per = KROWS // (CG * self.h)
        self.kept = self.g // 2
        self.full = self.kept // per * per
        rest = 2 * (self.kept - self.full)
        self.split = own % CG == 0 and self.full > 0 and rest <= per and rest * self.h % 16 == 0
        if self.split:
            self.chunks = [per] * (2 * self.full // per) + ([rest] if rest else [])
            self.early = self.full // per
        else:
            self.chunks = [min(per, self.g - k) for k in range(0, self.g, per)]
            self.early = 0
        self.early_rows = sum(self.chunks[: self.early]) * self.h
        self.lg = LANES // self.bw
        self.rg = round_up(-(-(self.own_rows + TERMS * self.h) // self.lg), 8)


def lane_iota(shape):
    return lax.broadcasted_iota(jnp.int32, shape, 1)


def widen(x, lanes):
    have = x.shape[1]
    if have == lanes:
        return x
    return jnp.concatenate([x, jnp.zeros((x.shape[0], lanes - have), x.dtype)], axis=1)


def rolled(x, shift):
    shift %= x.shape[1]
    return x if shift == 0 else pltpu.roll(x, shift, 1)


def flat(ref):
    return ref[...].astype(jnp.float32).reshape(-1, ref.shape[-1])


def copied_in(sources, targets, sems):
    copies = [
        pltpu.make_async_copy(source, target, sems.at[k])
        for k, (source, target) in enumerate(zip(sources, targets))
    ]
    for copy in copies:
        copy.start()
    return [copy.wait for copy in copies]


def edge_kernel(dm, left_hbm, right_hbm, *refs):
    *outs, flat_left_ref, flat_right_ref, left_ref, right_ref, sems = refs
    for wait in copied_in((left_hbm, right_hbm), (left_ref, right_ref), sems):
        wait()
    left, right = flat(left_ref), flat(right_ref)
    flat_left_ref[...] = left.astype(flat_left_ref.dtype)
    flat_right_ref[...] = right.astype(flat_right_ref.dtype)
    width = outs[0].shape[1]
    count = dm.hops[0]
    lane = lane_iota((dm.own_rows, width))
    last = rolled(widen(right, width), count - dm.strip)
    edge = rolled(widen(left, width), count + 3 - dm.strip)
    up = jnp.where(lane < count, last, edge)
    down = jnp.where(lane < 3, widen(right, width), rolled(widen(left, width), 3))
    even = lax.axis_index("col") % 2 == 0
    outs[0][...] = jnp.where(even, up, down).astype(outs[0].dtype)
    outs[1][...] = jnp.where(even, down, up).astype(outs[1].dtype)
    for out, count in zip(outs[2:], dm.hops[1:]):
        out[...] = rolled(right, count - dm.strip)[:, : out.shape[1]].astype(out.dtype)


def pack_kernel(dm, left_ref, right_ref, pair0_ref, pair1_ref, *refs):
    more, outs, windows_ref = refs[: len(dm.hops) - 1], refs[len(dm.hops) - 1 : -1], refs[-1]
    left, right = flat(left_ref), flat(right_ref)
    pair0, pair1 = flat(pair0_ref), flat(pair1_ref)
    even = lax.axis_index("col") % 2 == 0
    up = jnp.where(even, pair1, pair0)
    down = jnp.where(even, pair0, pair1)[:, :LANES]
    ext = max(round_up(dm.tail + dm.strip + 3, LANES), dm.lw2, up.shape[1])
    lane = lane_iota((dm.own_rows, ext))
    row = rolled(widen(right, ext), dm.tail)
    row = jnp.where(lane < dm.tail + dm.strip, row, rolled(widen(down, ext), dm.tail + dm.strip))
    pieces = [up] + [flat(ref) for ref in more]
    for k, count in enumerate(dm.hops):
        start = dm.tail - sum(dm.hops[: k + 1])
        piece = rolled(widen(pieces[k], ext), start)
        row = jnp.where((lane >= start) & (lane < start + count), piece, row)
    lext = max(round_up(dm.strip + 6, LANES), dm.lw2, up.shape[1])
    lane_l = lane_iota((dm.own_rows, lext))
    lrow = rolled(widen(left, lext), 3)
    lrow = jnp.where(lane_l < 3, rolled(widen(up, lext), -dm.hops[0]), lrow)
    lrow = jnp.where(lane_l >= dm.strip + 3, rolled(widen(down, lext), dm.strip), lrow)
    lane_o = lane_iota((dm.own_rows, dm.lw2))
    for q in range(dm.chips):
        a = rolled(row, -2 * dm.bw * q)[:, : dm.lw2]
        b = rolled(lrow, dm.lo2 - 2 * dm.bw * q)[:, : dm.lw2]
        windows_ref[q] = jnp.where(lane_o < dm.lo2, a, b).astype(windows_ref.dtype)
    chip = lax.axis_index("disp") // 2
    for m, out in enumerate(outs):
        out[...] = windows_ref[chip ^ m]


def split_kernel(dm, *refs):
    *windows, keep_ref, give_ref = refs
    first_core = lax.axis_index("disp") % 2 == 0
    for m, ref in enumerate(windows):
        x = flat(ref)
        lane = lane_iota((dm.own_rows, dm.lw))
        parts = []
        for core in range(2):
            a = rolled(x, -core * dm.bw)[:, : dm.lw]
            b = rolled(x, dm.lo - dm.lo2 - core * dm.bw)[:, : dm.lw]
            parts.append(jnp.where(lane < dm.lo, a, b))
        keep_ref[m] = jnp.where(first_core, parts[0], parts[1]).astype(keep_ref.dtype)
        give_ref[m] = jnp.where(first_core, parts[1], parts[0]).astype(give_ref.dtype)


def prep_kernel(dm, *refs):
    outs, targets, sems = refs[4:8], refs[8:12], refs[12]
    waits = copied_in(refs[:4], targets, sems)
    w1_ref, w2_ref, w3_ref, head_ref = targets
    o1_ref, o2_ref, o3_ref, column_ref = outs
    chip, core = lax.axis_index("disp") // 2, lax.axis_index("disp") % 2
    for layer, (w_ref, o_ref) in enumerate(((w1_ref, o1_ref), (w2_ref, o2_ref), (w3_ref, o3_ref))):
        inputs = w_ref.shape[2]
        per_a = dm.h * inputs
        waits[layer]()
        shape = (inputs, 3 * per_a)
        i = lax.broadcasted_iota(jnp.int32, shape, 0)
        if layer == 0 and dm.split:
            per_device = inputs // dm.n
            device = i // per_device
            side = (device % 2) ^ core
            i = ((device // 2) ^ chip) * per_device + i % per_device
            rest = 2 * dm.full + side * (dm.kept - dm.full) + i - dm.full
            i = jnp.where(i < dm.full, side * dm.full + i, rest)
        elif layer == 0:
            per_chip = inputs // dm.chips
            i = ((i // per_chip) ^ chip) * per_chip + i % per_chip
        col = lane_iota(shape)
        total = None
        for a in range(3):
            for hi in range(dm.h):
                if layer == 0:
                    pos = jnp.zeros(shape, jnp.int32)
                    first = 0
                    for count in dm.chunks:
                        here = first * dm.h + hi * count + (i - first)
                        pos = jnp.where(i >= first, here, pos)
                        first += count
                else:
                    pos = hi * inputs + i
                place = jnp.where(col == a * per_a + pos, 1.0, 0.0).astype(jnp.bfloat16)
                blocks = []
                for e in range(3):
                    for ho in range(dm.h):
                        b = hi - ho + 1
                        if 0 <= b <= 2:
                            blocks.append(w_ref[(a * 3 + b) * 3 + e])
                        else:
                            blocks.append(jnp.zeros((dm.f, inputs), jnp.bfloat16))
                term = jnp.dot(
                    jnp.concatenate(blocks, axis=0), place, preferred_element_type=jnp.float32
                )
                total = term if total is None else total + term
        o_ref[...] = total.astype(o_ref.dtype)
    waits[3]()
    square = (dm.f, dm.f)
    eye = lane_iota(square) == lax.broadcasted_iota(jnp.int32, square, 0)
    column = jnp.sum(jnp.where(eye, head_ref[...], 0.0), axis=1, keepdims=True)
    column = jnp.broadcast_to(column, (dm.f, dm.d))
    column_ref[...] = jnp.concatenate([column] * dm.h, axis=0)


def correlator(dm, chunks, x_of, lt_ref, lhs_ref, pc_ref):
    keeps = []
    for count in chunks:
        r, q = count * dm.h, count * CG * dm.h
        lane = lane_iota((r, q))
        sub = lax.broadcasted_iota(jnp.int32, (r, q), 0)
        keeps.append((lane % dm.h == sub // count) & (lane // (CG * dm.h) == sub % count))

    def run(m0, m1):
        first = 0
        for k, count in enumerate(chunks):
            r, q = count * dm.h, count * CG * dm.h
            for m in range(m0, m1):
                at = dm.lo - dm.lb + m
                line = jnp.broadcast_to(lt_ref[at : at + 1, first : first + q], (r, q))
                line = jnp.where(keeps[k], line, 0.0).astype(jnp.bfloat16)
                lhs_ref[k, m * r : (m + 1) * r, :q] = line
            pc_ref[k, m0 * r : m1 * r] = jnp.dot(
                lhs_ref[k, m0 * r : m1 * r, :q], x_of(k), preferred_element_type=jnp.float32
            )
            first += q

    return run


def shifts(v, lanes):
    if v.shape not in lanes:
        lanes[v.shape] = lane_iota(v.shape)
    lane, zero = lanes[v.shape], jnp.zeros_like(v)
    last = v.shape[1] - 1
    return (
        jnp.where(lane < last, rolled(v, -1), zero),
        v,
        jnp.where(lane > 0, rolled(v, 1), zero),
    )


def column_of(dm, chunks, pc_ref, m):
    parts = []
    for k, count in enumerate(chunks):
        r = count * dm.h
        parts.append(pc_ref[k, m * r : (m + 1) * r].astype(jnp.bfloat16))
    return rolled(jnp.concatenate(parts, axis=0), -m)[:, : dm.d]


def left_columns(dm, x):
    return jnp.transpose(x[:, dm.lb :].astype(jnp.float32)) * (1.0 / CG)


def pipeline(stages):
    done = [0] * len(stages)
    while done[-1] < stages[-1][1]:
        before = list(done)
        for k in reversed(range(len(stages))):
            run, count, beyond = stages[k]
            ready = count if k == 0 else min(count, before[k - 1] - beyond)
            size = ready - done[k] if ready == count else (ready - done[k]) // TILE * TILE
            size = min(size, TILE)
            if size > 0:
                run(done[k], done[k] + size)
                done[k] += size


def early_kernel(dm, keep_ref, part_ref, lt_ref, lhs_ref, pc_ref):
    chunks = dm.chunks[: dm.early]
    x = keep_ref[...].reshape(-1, dm.lw)
    rows = KROWS * dm.early
    lt_ref[...] = left_columns(dm, x[:rows])
    lanes = {}

    def volume(m0, m1):
        for m in range(m0, m1):
            for a, v in enumerate(shifts(column_of(dm, chunks, pc_ref, m), lanes)):
                part_ref[a, :, m * dm.d : (m + 1) * dm.d] = v

    x_of = lambda k: x[k * KROWS : (k + 1) * KROWS]
    pipeline([(correlator(dm, chunks, x_of, lt_ref, lhs_ref, pc_ref), dm.mw, 0), (volume, dm.mw, 0)])


def main_kernel(dm, keep_ref, got_ref, *refs):
    part_ref, refs = (refs[0], refs[1:]) if dm.split else (None, refs)
    w1_ref, w2_ref, w3_ref, head_ref, out_ref, x_ref, lt_ref, lhs_ref, pc_ref = refs[:9]
    a1_ref, a2_ref, a3_ref, p1_ref, p2_ref, p3_ref, s_ref = refs[9:]
    d, mw, h, f, bf = dm.d, dm.mw, dm.h, dm.f, jnp.bfloat16
    chip, core = lax.axis_index("disp") // 2, lax.axis_index("disp") % 2
    base = lax.axis_index("col") * dm.strip + lax.axis_index("disp") * dm.bw
    total = dm.strips * dm.strip
    chunks = dm.chunks[dm.early :]

    if dm.split:
        half, early = dm.rows // 2, KROWS * dm.early
        x_ref[:half] = keep_ref[...].reshape(half, dm.lw)
        x_ref[half:] = got_ref[...].reshape(half, dm.lw)
        sources = [x_ref[half + k * KROWS : half + (k + 1) * KROWS] for k in range(dm.early)]
        if early < half:
            rest = [keep_ref[...].reshape(half, dm.lw)[early:], got_ref[...].reshape(half, dm.lw)[early:]]
            sources.append(jnp.concatenate(rest, axis=0))
        at = 0
        for x in sources:
            lt_ref[:, at : at + x.shape[0]] = left_columns(dm, x)
            at += x.shape[0]
        x_of = lambda k: sources[k]
    else:
        rows = 2 * dm.own_rows
        for m in range(dm.chips):
            kept, got = flat(keep_ref.at[m]), flat(got_ref.at[m])
            both = [jnp.where(core == 0, kept, got), jnp.where(core == 0, got, kept)]
            both = jnp.concatenate(both, axis=0)
            x_ref[m * rows : (m + 1) * rows] = both.astype(bf)
            lt_ref[:, m * rows : (m + 1) * rows] = left_columns(dm, both)
        x_of = lambda k: x_ref[k * KROWS : k * KROWS + chunks[k] * CG * h]

    lanes = {}

    def spread(ref, m, v, first=0):
        rows = first + v.shape[0]
        for a, shifted in enumerate(shifts(v, lanes)):
            ref[a * rows + first : (a + 1) * rows, m * d : (m + 1) * d] = shifted

    def volume(m0, m1):
        for m in range(m0, m1):
            spread(a1_ref, m, column_of(dm, chunks, pc_ref, m), dm.early_rows)
            if dm.split:
                at = slice(m * d, (m + 1) * d)
                for a in range(3):
                    first = a * h * dm.g
                    a1_ref[first : first + dm.early_rows, at] = part_ref[a, :, at]

    def product(w_ref, a_ref, p_ref):
        def run(m0, m1):
            at = slice(m0 * d, m1 * d)
            p_ref[:, at] = jnp.dot(w_ref[...], a_ref[:, at], preferred_element_type=jnp.float32)

        return run

    def taken(p_ref, emit):
        fh = f * h

        def run(m0, m1):
            for m in range(m0, m1):
                z = p_ref[:fh, m * d : (m + 1) * d]
                z = z + p_ref[fh : 2 * fh, (m + 1) * d : (m + 2) * d]
                z = z + p_ref[2 * fh :, (m + 2) * d : (m + 3) * d]
                emit(m, jnp.maximum(z, 0.0))

        return run

    def activity(a_ref, margin):
        def emit(m, z):
            column = m + margin
            if not 3 <= column < mw - 3:
                at = base - 3 + column
                z = jnp.where((at >= 0) & (at < total), z, 0.0)
            spread(a_ref, m, z.astype(bf))

        return emit

    head = head_ref[...]

    def score(m, z):
        z = z * head
        for row in range(h):
            s_ref[row, m : m + 1, :] = jnp.sum(z[row * f : (row + 1) * f], axis=0, keepdims=True)

    stages = [
        (correlator(dm, chunks, x_of, lt_ref, lhs_ref, pc_ref), mw, 0),
        (volume, mw, 0),
        (product(w1_ref, a1_ref, p1_ref), mw, 0),
        (taken(p1_ref, activity(a2_ref, 1)), mw - 2, 2),
        (product(w2_ref, a2_ref, p2_ref), mw - 2, 0),
        (taken(p2_ref, activity(a3_ref, 2)), mw - 4, 2),
        (product(w3_ref, a3_ref, p3_ref), mw - 4, 0),
        (taken(p3_ref, score), mw - 6, 2),
    ]
    pipeline(stages)

    disp = (d - 1) - lane_iota((dm.bw, d))
    column = base + lax.broadcasted_iota(jnp.int32, (dm.bw, d), 0)
    valid = column >= disp
    disp_f = disp.astype(jnp.float32)
    bands, disparity = [], []
    for row in range(h):
        s = jnp.where(valid, s_ref[row], masked_value)
        top = jnp.max(s, axis=1, keepdims=True)
        weighting = jnp.where(valid, jnp.exp(s - top), 0.0)
        denominator = jnp.sum(weighting, axis=1, keepdims=True)
        disp_sum = jnp.sum(weighting * disp_f, axis=1, keepdims=True)
        disparity.append(disp_sum / denominator / d)
        band = widen(weighting / denominator, dm.lw)
        band = pltpu.roll(band, 3, 1, stride=1, stride_axis=0)
        bands += [band] * dm.lg
    band = jnp.concatenate(bands, axis=0)
    sums = lax.dot_general(
        x_ref[...], band.astype(bf), (((1,), (1,)), ((), ())), preferred_element_type=jnp.float32
    )
    row = lax.broadcasted_iota(jnp.int32, (dm.rows, LANES), 0) % h
    warped = sums[:, :LANES]
    for k in range(1, h):
        warped = jnp.where(row == k, sums[:, k * LANES : (k + 1) * LANES], warped)

    eye = lane_iota((dm.bw, LANES)) % dm.bw == lax.broadcasted_iota(jnp.int32, (dm.bw, LANES), 0)
    rest = [jnp.sum(jnp.where(eye, v, 0.0), axis=0, keepdims=True) for v in disparity]
    lines = []
    for _ in range(TERMS):
        terms = [v.astype(bf).astype(jnp.float32) for v in rest]
        rest = [v - t for v, t in zip(rest, terms)]
        lines += terms
    lines.append(jnp.zeros((dm.lg * dm.rg - dm.own_rows - len(lines), LANES), jnp.float32))
    lines = jnp.concatenate(lines, axis=0)
    group = lane_iota((dm.rg, LANES)) // dm.bw
    for j in range(dm.n):
        mine = jnp.concatenate([warped[j * dm.own_rows : (j + 1) * dm.own_rows], lines], axis=0)
        packed = mine[: dm.rg]
        for g in range(1, dm.lg):
            packed = jnp.where(group == g, mine[g * dm.rg : (g + 1) * dm.rg], packed)
        if dm.split:
            target = (j % dm.chips ^ chip) * 2 + (j // dm.chips ^ core)
        else:
            target = (j // 2 ^ chip) * 2 + j % 2
        out_ref[target] = packed.astype(out_ref.dtype)


def unpack_kernel(dm, y_ref, warped_ref, disparity_ref):
    per = LANES // dm.bw
    lane = lane_iota((dm.rg, LANES))
    tiles = []
    for t in range(dm.n // per):
        groups = []
        for g in range(dm.lg):
            total = None
            for p in range(per):
                piece = rolled(flat(y_ref.at[t * per + p]), (p - g) * dm.bw)
                keep = (lane >= p * dm.bw) & (lane < (p + 1) * dm.bw)
                total = piece if total is None else jnp.where(keep, piece, total)
            groups.append(total)
        tiles.append(jnp.concatenate(groups, axis=0))
    full = jnp.concatenate(tiles, axis=1)
    warped_ref[...] = full[: dm.own_rows].reshape(warped_ref.shape).astype(warped_ref.dtype)
    total = None
    for k in reversed(range(TERMS)):
        at = dm.own_rows + k * dm.h
        term = full[at : at + dm.h]
        total = term if total is None else term + total
    disparity_ref[...] = total


def shards(left_feat, right_feat, conv1_w, conv2_w, conv3_w, head_w):
    n, strips = lax.axis_size("disp"), lax.axis_size("col")
    dm = Dims(left_feat.shape, conv1_w.shape, conv2_w.shape, n, strips)
    bf, f32 = jnp.bfloat16, jnp.float32

    def call(kernel, out_shape, operands, mib=8, in_hbm=False, **options):
        spec = VMEM
        if in_hbm:
            spec = pl.BlockSpec(memory_space=pltpu.HBM)
            operands = [pltpu.with_memory_space_constraint(v, pltpu.HBM) for v in operands]
        return pl.pallas_call(
            functools.partial(kernel, dm),
            out_shape=out_shape,
            in_specs=[spec] * len(operands),
            out_specs=jax.tree.map(lambda _: VMEM, out_shape),
            compiler_params=pltpu.CompilerParams(vmem_limit_bytes=mib << 20),
            **options,
        )(*operands)

    wide = max(round_up(dm.hops[0] + 3, LANES), dm.strip)
    widths = [wide, wide] + [round_up(c, LANES) for c in dm.hops[1:]]
    *edges, left, right = call(
        edge_kernel,
        [jax.ShapeDtypeStruct((dm.own_rows, w), bf) for w in widths + [dm.strip] * 2],
        [left_feat, right_feat],
        in_hbm=True,
        scratch_shapes=[
            pltpu.VMEM(left_feat.shape, bf),
            pltpu.VMEM(left_feat.shape, bf),
            pltpu.SemaphoreType.DMA((2,)),
        ],
    )
    arrived = []
    for first in range(2):
        pairs = [(s, s + 1) for s in range(first, strips - 1, 2)]
        pairs += [(b, a) for a, b in pairs]
        arrived.append(lax.ppermute(edges[first], "col", pairs))
    for k, e in enumerate(edges[2:], 2):
        arrived.append(lax.ppermute(e, "col", [(s, s + k) for s in range(strips - k)]))

    kernels = [w.transpose(2, 3, 4, 0, 1).reshape(27, w.shape[0], w.shape[1]) for w in (conv1_w, conv2_w, conv3_w)]
    arrived, kernels = lax.optimization_barrier((arrived, kernels))
    m3 = 3 * dm.h * dm.f
    depths = [3 * dm.h * w.shape[2] for w in kernels]
    w1, w2, w3, head = call(
        prep_kernel,
        [jax.ShapeDtypeStruct((m3, k), bf) for k in depths]
        + [jax.ShapeDtypeStruct((dm.h * dm.f, dm.d), f32)],
        kernels + [head_w[None]],
        in_hbm=True,
        scratch_shapes=[pltpu.VMEM(w.shape, bf) for w in kernels]
        + [pltpu.VMEM((1, dm.f), f32), pltpu.SemaphoreType.DMA((4,))],
    )

    own_window, *sent = call(
        pack_kernel,
        [jax.ShapeDtypeStruct((dm.own_rows, dm.lw2), bf)] * dm.chips,
        [left, right] + arrived,
        scratch_shapes=[pltpu.VMEM((dm.chips, dm.own_rows, dm.lw2), bf)],
    )
    windows = [own_window]
    for m in range(1, dm.chips):
        pairs = [(i, i ^ (2 * m)) for i in range(n)]
        windows.append(lax.ppermute(sent[m - 1], "disp", pairs))
    windows, (w1, w2, w3, head) = lax.optimization_barrier((windows, (w1, w2, w3, head)))
    half = jax.ShapeDtypeStruct((dm.chips, dm.own_rows, dm.lw), bf)
    keep, give = call(split_kernel, [half, half], windows)
    got = lax.ppermute(give, "disp", [(i, i ^ 1) for i in range(n)])

    def stage(chunks):
        r = max(chunks) * dm.h
        return [
            pltpu.VMEM((dm.lw - dm.lb, sum(chunks) * CG * dm.h), f32),
            pltpu.VMEM((len(chunks), dm.mw * r, KROWS), bf),
            pltpu.VMEM((len(chunks), dm.mw * r, dm.lw), f32),
        ]

    columns = [dm.mw, dm.mw - 2, dm.mw - 4]
    operands = [keep, got]
    if dm.split:
        operands.append(
            call(
                early_kernel,
                jax.ShapeDtypeStruct((3, dm.early_rows, dm.mw * dm.d), bf),
                [keep],
                mib=16,
                scratch_shapes=stage(dm.chunks[: dm.early]),
            )
        )
    packed = call(
        main_kernel,
        jax.ShapeDtypeStruct((n, dm.rg, LANES), bf),
        operands + [w1, w2, w3, head],
        mib=32,
        scratch_shapes=[
            pltpu.VMEM((dm.rows, dm.lw), bf),
            *stage(dm.chunks[dm.early :]),
            *[pltpu.VMEM((k, c * dm.d), bf) for k, c in zip(depths, columns)],
            *[pltpu.VMEM((m3, c * dm.d), f32) for c in columns],
            pltpu.VMEM((dm.h, dm.bw, dm.d), f32),
        ],
    )
    y = lax.all_to_all(packed, "disp", 0, 0)
    return tuple(
        call(
            unpack_kernel,
            [
                jax.ShapeDtypeStruct(left_feat.shape, bf),
                jax.ShapeDtypeStruct((dm.h, dm.strip), f32),
            ],
            [y],
        )
    )


def solution(mesh):
    return jax.shard_map(
        shards,
        mesh=mesh,
        in_specs=(P("disp", None, "col"), P("disp", None, "col"), P(), P(), P(), P()),
        out_specs=(P("disp", None, "col"), P(None, "col")),
        check_vma=False,
    )
```

```python
import functools

import jax
import jax.numpy as jnp
from jax import lax
from jax.experimental import pallas as pl
from jax.experimental.pallas import tpu as pltpu
from jax.sharding import PartitionSpec as P


DG = 16
CG = 8
LANES = 128
KROWS = 256
TILE = 8
TERMS = 3
VMEM = pl.BlockSpec(memory_space=pltpu.VMEM)

masked_value = -1e30


def round_up(value, unit):
    return -(-value // unit) * unit


class Dims:
    def __init__(self, left, conv1, conv2, groups_disp, strips):
        own, self.h, self.strip = left
        self.n = groups_disp
        self.strips = strips
        self.own_rows = own * self.h
        self.rows = self.own_rows * self.n
        self.d = DG * self.n
        self.bw = self.strip // self.n
        self.mw = self.bw + 6
        self.tail = self.d + 2
        self.g = conv1[1]
        self.f = conv2[0]
        self.lo = round_up(self.mw + self.d - 1, 8)
        self.lb = self.lo // LANES * LANES
        self.lw = round_up(self.lo + self.mw, LANES)
        self.hops = []
        left_over = self.tail
        while left_over > 0:
            self.hops.append(min(left_over, self.strip))
            left_over -= self.strip
        self.chips = self.n // 2
        self.lo2 = round_up(self.mw + self.bw + self.d - 1, 8)
        self.lw2 = round_up(self.lo2 + self.mw + self.bw, LANES)
        per = KROWS // (CG * self.h)
        self.kept = self.g // 2
        self.full = self.kept // per * per
        rest = 2 * (self.kept - self.full)
        self.split = own % CG == 0 and self.full > 0 and rest <= per and rest * self.h % 16 == 0
        if self.split:
            self.chunks = [per] * (2 * self.full // per) + ([rest] if rest else [])
            self.early = self.full // per
        else:
            self.chunks = [min(per, self.g - k) for k in range(0, self.g, per)]
            self.early = 0
        self.early_rows = sum(self.chunks[: self.early]) * self.h
        self.lg = LANES // self.bw
        self.rg = round_up(-(-(self.own_rows + TERMS * self.h) // self.lg), 8)


def lane_iota(shape):
    return lax.broadcasted_iota(jnp.int32, shape, 1)


def widen(x, lanes):
    have = x.shape[1]
    if have == lanes:
        return x
    return jnp.concatenate([x, jnp.zeros((x.shape[0], lanes - have), x.dtype)], axis=1)


def rolled(x, shift):
    shift %= x.shape[1]
    return x if shift == 0 else pltpu.roll(x, shift, 1)


def flat(ref):
    return ref[...].astype(jnp.float32).reshape(-1, ref.shape[-1])


def copied_in(sources, targets, sems):
    copies = [
        pltpu.make_async_copy(source, target, sems.at[k])
        for k, (source, target) in enumerate(zip(sources, targets))
    ]
    for copy in copies:
        copy.start()
    return [copy.wait for copy in copies]


def edge_kernel(dm, left_hbm, right_hbm, *refs):
    *outs, flat_left_ref, flat_right_ref, left_ref, right_ref, sems = refs
    for wait in copied_in((left_hbm, right_hbm), (left_ref, right_ref), sems):
        wait()
    left, right = flat(left_ref), flat(right_ref)
    flat_left_ref[...] = left.astype(flat_left_ref.dtype)
    flat_right_ref[...] = right.astype(flat_right_ref.dtype)
    width = outs[0].shape[1]
    count = dm.hops[0]
    lane = lane_iota((dm.own_rows, width))
    last = rolled(widen(right, width), count - dm.strip)
    edge = rolled(widen(left, width), count + 3 - dm.strip)
    up = jnp.where(lane < count, last, edge)
    down = jnp.where(lane < 3, widen(right, width), rolled(widen(left, width), 3))
    even = lax.axis_index("col") % 2 == 0
    outs[0][...] = jnp.where(even, up, down).astype(outs[0].dtype)
    outs[1][...] = jnp.where(even, down, up).astype(outs[1].dtype)
    for out, count in zip(outs[2:], dm.hops[1:]):
        out[...] = rolled(right, count - dm.strip)[:, : out.shape[1]].astype(out.dtype)


def pack_kernel(dm, left_ref, right_ref, pair0_ref, pair1_ref, *refs):
    more, outs, windows_ref = refs[: len(dm.hops) - 1], refs[len(dm.hops) - 1 : -1], refs[-1]
    left, right = flat(left_ref), flat(right_ref)
    pair0, pair1 = flat(pair0_ref), flat(pair1_ref)
    even = lax.axis_index("col") % 2 == 0
    up = jnp.where(even, pair1, pair0)
    down = jnp.where(even, pair0, pair1)[:, :LANES]
    ext = max(round_up(dm.tail + dm.strip + 3, LANES), dm.lw2, up.shape[1])
    lane = lane_iota((dm.own_rows, ext))
    row = rolled(widen(right, ext), dm.tail)
    row = jnp.where(lane < dm.tail + dm.strip, row, rolled(widen(down, ext), dm.tail + dm.strip))
    pieces = [up] + [flat(ref) for ref in more]
    for k, count in enumerate(dm.hops):
        start = dm.tail - sum(dm.hops[: k + 1])
        piece = rolled(widen(pieces[k], ext), start)
        row = jnp.where((lane >= start) & (lane < start + count), piece, row)
    lext = max(round_up(dm.strip + 6, LANES), dm.lw2, up.shape[1])
    lane_l = lane_iota((dm.own_rows, lext))
    lrow = rolled(widen(left, lext), 3)
    lrow = jnp.where(lane_l < 3, rolled(widen(up, lext), -dm.hops[0]), lrow)
    lrow = jnp.where(lane_l >= dm.strip + 3, rolled(widen(down, lext), dm.strip), lrow)
    lane_o = lane_iota((dm.own_rows, dm.lw2))
    for q in range(dm.chips):
        a = rolled(row, -2 * dm.bw * q)[:, : dm.lw2]
        b = rolled(lrow, dm.lo2 - 2 * dm.bw * q)[:, : dm.lw2]
        windows_ref[q] = jnp.where(lane_o < dm.lo2, a, b).astype(windows_ref.dtype)
    chip = lax.axis_index("disp") // 2
    for m, out in enumerate(outs):
        out[...] = windows_ref[chip ^ m]


def split_kernel(dm, *refs):
    *windows, keep_ref, give_ref = refs
    first_core = lax.axis_index("disp") % 2 == 0
    for m, ref in enumerate(windows):
        x = flat(ref)
        lane = lane_iota((dm.own_rows, dm.lw))
        parts = []
        for core in range(2):
            a = rolled(x, -core * dm.bw)[:, : dm.lw]
            b = rolled(x, dm.lo - dm.lo2 - core * dm.bw)[:, : dm.lw]
            parts.append(jnp.where(lane < dm.lo, a, b))
        keep_ref[m] = jnp.where(first_core, parts[0], parts[1]).astype(keep_ref.dtype)
        give_ref[m] = jnp.where(first_core, parts[1], parts[0]).astype(give_ref.dtype)


def prep_kernel(dm, *refs):
    outs, targets, sems = refs[4:8], refs[8:12], refs[12]
    waits = copied_in(refs[:4], targets, sems)
    w1_ref, w2_ref, w3_ref, head_ref = targets
    o1_ref, o2_ref, o3_ref, column_ref = outs
    chip, core = lax.axis_index("disp") // 2, lax.axis_index("disp") % 2
    for layer, (w_ref, o_ref) in enumerate(((w1_ref, o1_ref), (w2_ref, o2_ref), (w3_ref, o3_ref))):
        inputs = w_ref.shape[2]
        per_a = dm.h * inputs
        waits[layer]()
        shape = (inputs, 3 * per_a)
        i = lax.broadcasted_iota(jnp.int32, shape, 0)
        if layer == 0 and dm.split:
            per_device = inputs // dm.n
            device = i // per_device
            side = (device % 2) ^ core
            i = ((device // 2) ^ chip) * per_device + i % per_device
            rest = 2 * dm.full + side * (dm.kept - dm.full) + i - dm.full
            i = jnp.where(i < dm.full, side * dm.full + i, rest)
        elif layer == 0:
            per_chip = inputs // dm.chips
            i = ((i // per_chip) ^ chip) * per_chip + i % per_chip
        col = lane_iota(shape)
        total = None
        for a in range(3):
            for hi in range(dm.h):
                if layer == 0:
                    pos = jnp.zeros(shape, jnp.int32)
                    first = 0
                    for count in dm.chunks:
                        here = first * dm.h + hi * count + (i - first)
                        pos = jnp.where(i >= first, here, pos)
                        first += count
                else:
                    pos = hi * inputs + i
                place = jnp.where(col == a * per_a + pos, 1.0, 0.0).astype(jnp.bfloat16)
                blocks = []
                for e in range(3):
                    for ho in range(dm.h):
                        b = hi - ho + 1
                        if 0 <= b <= 2:
                            blocks.append(w_ref[(a * 3 + b) * 3 + e])
                        else:
                            blocks.append(jnp.zeros((dm.f, inputs), jnp.bfloat16))
                term = jnp.dot(
                    jnp.concatenate(blocks, axis=0), place, preferred_element_type=jnp.float32
                )
                total = term if total is None else total + term
        o_ref[...] = total.astype(o_ref.dtype)
    waits[3]()
    square = (dm.f, dm.f)
    eye = lane_iota(square) == lax.broadcasted_iota(jnp.int32, square, 0)
    column = jnp.sum(jnp.where(eye, head_ref[...], 0.0), axis=1, keepdims=True)
    column = jnp.broadcast_to(column, (dm.f, dm.d))
    column_ref[...] = jnp.concatenate([column] * dm.h, axis=0)


def correlator(dm, chunks, x_of, lt_ref, lhs_ref, pc_ref):
    keeps = []
    for count in chunks:
        r, q = count * dm.h, count * CG * dm.h
        lane = lane_iota((r, q))
        sub = lax.broadcasted_iota(jnp.int32, (r, q), 0)
        keeps.append((lane % dm.h == sub // count) & (lane // (CG * dm.h) == sub % count))

    def run(m0, m1):
        first = 0
        for k, count in enumerate(chunks):
            r, q = count * dm.h, count * CG * dm.h
            for m in range(m0, m1):
                at = dm.lo - dm.lb + m
                line = jnp.broadcast_to(lt_ref[at : at + 1, first : first + q], (r, q))
                line = jnp.where(keeps[k], line, 0.0).astype(jnp.bfloat16)
                lhs_ref[k, m * r : (m + 1) * r, :q] = line
            pc_ref[k, m0 * r : m1 * r] = jnp.dot(
                lhs_ref[k, m0 * r : m1 * r, :q], x_of(k), preferred_element_type=jnp.float32
            )
            first += q

    return run


def shifts(v, lanes):
    if v.shape not in lanes:
        lanes[v.shape] = lane_iota(v.shape)
    lane, zero = lanes[v.shape], jnp.zeros_like(v)
    last = v.shape[1] - 1
    return (
        jnp.where(lane < last, rolled(v, -1), zero),
        v,
        jnp.where(lane > 0, rolled(v, 1), zero),
    )


def column_of(dm, chunks, pc_ref, m):
    parts = []
    for k, count in enumerate(chunks):
        r = count * dm.h
        parts.append(pc_ref[k, m * r : (m + 1) * r].astype(jnp.bfloat16))
    return rolled(jnp.concatenate(parts, axis=0), -m)[:, : dm.d]


def left_columns(dm, x):
    return jnp.transpose(x[:, dm.lb :].astype(jnp.float32)) * (1.0 / CG)


def pipeline(stages):
    done = [0] * len(stages)
    while done[-1] < stages[-1][1]:
        before = list(done)
        for k in reversed(range(len(stages))):
            run, count, beyond = stages[k]
            ready = count if k == 0 else min(count, before[k - 1] - beyond)
            size = ready - done[k] if ready == count else (ready - done[k]) // TILE * TILE
            size = min(size, TILE)
            if size > 0:
                run(done[k], done[k] + size)
                done[k] += size


def early_kernel(dm, keep_ref, part_ref, lt_ref, lhs_ref, pc_ref):
    chunks = dm.chunks[: dm.early]
    x = keep_ref[...].reshape(-1, dm.lw)
    rows = KROWS * dm.early
    lt_ref[...] = left_columns(dm, x[:rows])
    lanes = {}

    def volume(m0, m1):
        for m in range(m0, m1):
            for a, v in enumerate(shifts(column_of(dm, chunks, pc_ref, m), lanes)):
                part_ref[a, :, m * dm.d : (m + 1) * dm.d] = v

    x_of = lambda k: x[k * KROWS : (k + 1) * KROWS]
    pipeline([(correlator(dm, chunks, x_of, lt_ref, lhs_ref, pc_ref), dm.mw, 0), (volume, dm.mw, 0)])


def main_kernel(dm, keep_ref, got_ref, *refs):
    part_ref, refs = (refs[0], refs[1:]) if dm.split else (None, refs)
    w1_ref, w2_ref, w3_ref, head_ref, same_ref, other_ref, x_ref, lt_ref, lhs_ref, pc_ref = refs[:10]
    a1_ref, a2_ref, a3_ref, p1_ref, p2_ref, p3_ref, s_ref = refs[10:]
    d, mw, h, f, bf = dm.d, dm.mw, dm.h, dm.f, jnp.bfloat16
    core = lax.axis_index("disp") % 2
    base = lax.axis_index("col") * dm.strip + lax.axis_index("disp") * dm.bw
    total = dm.strips * dm.strip
    chunks = dm.chunks[dm.early :]

    if dm.split:
        half, early = dm.rows // 2, KROWS * dm.early
        x_ref[:half] = keep_ref[...].reshape(half, dm.lw)
        x_ref[half:] = got_ref[...].reshape(half, dm.lw)
        sources = [x_ref[half + k * KROWS : half + (k + 1) * KROWS] for k in range(dm.early)]
        if early < half:
            rest = [keep_ref[...].reshape(half, dm.lw)[early:], got_ref[...].reshape(half, dm.lw)[early:]]
            sources.append(jnp.concatenate(rest, axis=0))
        at = 0
        for x in sources:
            lt_ref[:, at : at + x.shape[0]] = left_columns(dm, x)
            at += x.shape[0]
        x_of = lambda k: sources[k]
    else:
        rows = 2 * dm.own_rows
        for m in range(dm.chips):
            kept, got = flat(keep_ref.at[m]), flat(got_ref.at[m])
            both = [jnp.where(core == 0, kept, got), jnp.where(core == 0, got, kept)]
            both = jnp.concatenate(both, axis=0)
            x_ref[m * rows : (m + 1) * rows] = both.astype(bf)
            lt_ref[:, m * rows : (m + 1) * rows] = left_columns(dm, both)
        x_of = lambda k: x_ref[k * KROWS : k * KROWS + chunks[k] * CG * h]

    lanes = {}

    def spread(ref, m, v, first=0):
        rows = first + v.shape[0]
        for a, shifted in enumerate(shifts(v, lanes)):
            ref[a * rows + first : (a + 1) * rows, m * d : (m + 1) * d] = shifted

    def volume(m0, m1):
        for m in range(m0, m1):
            spread(a1_ref, m, column_of(dm, chunks, pc_ref, m), dm.early_rows)
            if dm.split:
                at = slice(m * d, (m + 1) * d)
                for a in range(3):
                    first = a * h * dm.g
                    a1_ref[first : first + dm.early_rows, at] = part_ref[a, :, at]

    def product(w_ref, a_ref, p_ref):
        def run(m0, m1):
            at = slice(m0 * d, m1 * d)
            p_ref[:, at] = jnp.dot(w_ref[...], a_ref[:, at], preferred_element_type=jnp.float32)

        return run

    def taken(p_ref, emit):
        fh = f * h

        def run(m0, m1):
            for m in range(m0, m1):
                z = p_ref[:fh, m * d : (m + 1) * d]
                z = z + p_ref[fh : 2 * fh, (m + 1) * d : (m + 2) * d]
                z = z + p_ref[2 * fh :, (m + 2) * d : (m + 3) * d]
                emit(m, jnp.maximum(z, 0.0))

        return run

    def activity(a_ref, margin):
        def emit(m, z):
            column = m + margin
            if not 3 <= column < mw - 3:
                at = base - 3 + column
                z = jnp.where((at >= 0) & (at < total), z, 0.0)
            spread(a_ref, m, z.astype(bf))

        return emit

    head = head_ref[...]

    def score(m, z):
        z = z * head
        for row in range(h):
            s_ref[row, m : m + 1, :] = jnp.sum(z[row * f : (row + 1) * f], axis=0, keepdims=True)

    stages = [
        (correlator(dm, chunks, x_of, lt_ref, lhs_ref, pc_ref), mw, 0),
        (volume, mw, 0),
        (product(w1_ref, a1_ref, p1_ref), mw, 0),
        (taken(p1_ref, activity(a2_ref, 1)), mw - 2, 2),
        (product(w2_ref, a2_ref, p2_ref), mw - 2, 0),
        (taken(p2_ref, activity(a3_ref, 2)), mw - 4, 2),
        (product(w3_ref, a3_ref, p3_ref), mw - 4, 0),
        (taken(p3_ref, score), mw - 6, 2),
    ]
    pipeline(stages)

    disp = (d - 1) - lane_iota((dm.bw, d))
    column = base + lax.broadcasted_iota(jnp.int32, (dm.bw, d), 0)
    valid = column >= disp
    disp_f = disp.astype(jnp.float32)
    bands, disparity = [], []
    for row in range(h):
        s = jnp.where(valid, s_ref[row], masked_value)
        top = jnp.max(s, axis=1, keepdims=True)
        weighting = jnp.where(valid, jnp.exp(s - top), 0.0)
        denominator = jnp.sum(weighting, axis=1, keepdims=True)
        disp_sum = jnp.sum(weighting * disp_f, axis=1, keepdims=True)
        disparity.append(disp_sum / denominator / d)
        band = widen(weighting / denominator, dm.lw)
        band = pltpu.roll(band, 3, 1, stride=1, stride_axis=0)
        bands += [band] * dm.lg
    band = jnp.concatenate(bands, axis=0)
    sums = lax.dot_general(
        x_ref[...], band.astype(bf), (((1,), (1,)), ((), ())), preferred_element_type=jnp.float32
    )
    row = lax.broadcasted_iota(jnp.int32, (dm.rows, LANES), 0) % h
    warped = sums[:, :LANES]
    for k in range(1, h):
        warped = jnp.where(row == k, sums[:, k * LANES : (k + 1) * LANES], warped)

    eye = lane_iota((dm.bw, LANES)) % dm.bw == lax.broadcasted_iota(jnp.int32, (dm.bw, LANES), 0)
    rest = [jnp.sum(jnp.where(eye, v, 0.0), axis=0, keepdims=True) for v in disparity]
    lines = []
    for _ in range(TERMS):
        terms = [v.astype(bf).astype(jnp.float32) for v in rest]
        rest = [v - t for v, t in zip(rest, terms)]
        lines += terms
    lines.append(jnp.zeros((dm.lg * dm.rg - dm.own_rows - len(lines), LANES), jnp.float32))
    lines = jnp.concatenate(lines, axis=0)
    group = lane_iota((dm.rg, LANES)) // dm.bw
    blocks = []
    for j in range(dm.n):
        mine = jnp.concatenate([warped[j * dm.own_rows : (j + 1) * dm.own_rows], lines], axis=0)
        packed = mine[: dm.rg]
        for g in range(1, dm.lg):
            packed = jnp.where(group == g, mine[g * dm.rg : (g + 1) * dm.rg], packed)
        blocks.append(packed)
    for m in range(dm.chips):
        if dm.split:
            same, other = blocks[m], blocks[dm.chips + m]
        else:
            pair = blocks[2 * m : 2 * m + 2]
            same = jnp.where(core == 0, pair[0], pair[1])
            other = jnp.where(core == 0, pair[1], pair[0])
        same_ref[m] = same.astype(same_ref.dtype)
        other_ref[m] = other.astype(other_ref.dtype)


def join_kernel(dm, same_ref, theirs_ref, *outs):
    for m, out in enumerate(outs, 1):
        out[0] = same_ref[m]
        out[1] = theirs_ref[m]


def unpack_kernel(dm, same_ref, theirs_ref, *refs):
    *others, warped_ref, disparity_ref, y_ref = refs
    chip, core = lax.axis_index("disp") // 2, lax.axis_index("disp") % 2
    y_ref[chip * 2 + core] = same_ref[0].astype(jnp.float32)
    y_ref[chip * 2 + 1 - core] = theirs_ref[0].astype(jnp.float32)
    for m, ref in enumerate(others, 1):
        y_ref[(chip ^ m) * 2 + core] = ref[0].astype(jnp.float32)
        y_ref[(chip ^ m) * 2 + 1 - core] = ref[1].astype(jnp.float32)
    per = LANES // dm.bw
    lane = lane_iota((dm.rg, LANES))
    tiles = []
    for t in range(dm.n // per):
        groups = []
        for g in range(dm.lg):
            total = None
            for p in range(per):
                piece = rolled(y_ref[t * per + p], (p - g) * dm.bw)
                keep = (lane >= p * dm.bw) & (lane < (p + 1) * dm.bw)
                total = piece if total is None else jnp.where(keep, piece, total)
            groups.append(total)
        tiles.append(jnp.concatenate(groups, axis=0))
    full = jnp.concatenate(tiles, axis=1)
    warped_ref[...] = full[: dm.own_rows].reshape(warped_ref.shape).astype(warped_ref.dtype)
    total = None
    for k in reversed(range(TERMS)):
        at = dm.own_rows + k * dm.h
        term = full[at : at + dm.h]
        total = term if total is None else term + total
    disparity_ref[...] = total


def shards(left_feat, right_feat, conv1_w, conv2_w, conv3_w, head_w):
    n, strips = lax.axis_size("disp"), lax.axis_size("col")
    dm = Dims(left_feat.shape, conv1_w.shape, conv2_w.shape, n, strips)
    bf, f32 = jnp.bfloat16, jnp.float32

    def call(kernel, out_shape, operands, mib=8, in_hbm=False, **options):
        spec = VMEM
        if in_hbm:
            spec = pl.BlockSpec(memory_space=pltpu.HBM)
            operands = [pltpu.with_memory_space_constraint(v, pltpu.HBM) for v in operands]
        return pl.pallas_call(
            functools.partial(kernel, dm),
            out_shape=out_shape,
            in_specs=[spec] * len(operands),
            out_specs=jax.tree.map(lambda _: VMEM, out_shape),
            compiler_params=pltpu.CompilerParams(vmem_limit_bytes=mib << 20),
            **options,
        )(*operands)

    wide = max(round_up(dm.hops[0] + 3, LANES), dm.strip)
    widths = [wide, wide] + [round_up(c, LANES) for c in dm.hops[1:]]
    *edges, left, right = call(
        edge_kernel,
        [jax.ShapeDtypeStruct((dm.own_rows, w), bf) for w in widths + [dm.strip] * 2],
        [left_feat, right_feat],
        in_hbm=True,
        scratch_shapes=[
            pltpu.VMEM(left_feat.shape, bf),
            pltpu.VMEM(left_feat.shape, bf),
            pltpu.SemaphoreType.DMA((2,)),
        ],
    )
    arrived = []
    for first in range(2):
        pairs = [(s, s + 1) for s in range(first, strips - 1, 2)]
        pairs += [(b, a) for a, b in pairs]
        arrived.append(lax.ppermute(edges[first], "col", pairs))
    for k, e in enumerate(edges[2:], 2):
        arrived.append(lax.ppermute(e, "col", [(s, s + k) for s in range(strips - k)]))

    kernels = [w.transpose(2, 3, 4, 0, 1).reshape(27, w.shape[0], w.shape[1]) for w in (conv1_w, conv2_w, conv3_w)]
    arrived, kernels = lax.optimization_barrier((arrived, kernels))
    m3 = 3 * dm.h * dm.f
    depths = [3 * dm.h * w.shape[2] for w in kernels]
    w1, w2, w3, head = call(
        prep_kernel,
        [jax.ShapeDtypeStruct((m3, k), bf) for k in depths]
        + [jax.ShapeDtypeStruct((dm.h * dm.f, dm.d), f32)],
        kernels + [head_w[None]],
        in_hbm=True,
        scratch_shapes=[pltpu.VMEM(w.shape, bf) for w in kernels]
        + [pltpu.VMEM((1, dm.f), f32), pltpu.SemaphoreType.DMA((4,))],
    )

    own_window, *sent = call(
        pack_kernel,
        [jax.ShapeDtypeStruct((dm.own_rows, dm.lw2), bf)] * dm.chips,
        [left, right] + arrived,
        scratch_shapes=[pltpu.VMEM((dm.chips, dm.own_rows, dm.lw2), bf)],
    )
    windows = [own_window]
    for m in range(1, dm.chips):
        pairs = [(i, i ^ (2 * m)) for i in range(n)]
        windows.append(lax.ppermute(sent[m - 1], "disp", pairs))
    windows, (w1, w2, w3, head) = lax.optimization_barrier((windows, (w1, w2, w3, head)))
    half = jax.ShapeDtypeStruct((dm.chips, dm.own_rows, dm.lw), bf)
    keep, give = call(split_kernel, [half, half], windows)
    got = lax.ppermute(give, "disp", [(i, i ^ 1) for i in range(n)])

    def stage(chunks):
        r = max(chunks) * dm.h
        return [
            pltpu.VMEM((dm.lw - dm.lb, sum(chunks) * CG * dm.h), f32),
            pltpu.VMEM((len(chunks), dm.mw * r, KROWS), bf),
            pltpu.VMEM((len(chunks), dm.mw * r, dm.lw), f32),
        ]

    columns = [dm.mw, dm.mw - 2, dm.mw - 4]
    operands = [keep, got]
    if dm.split:
        operands.append(
            call(
                early_kernel,
                jax.ShapeDtypeStruct((3, dm.early_rows, dm.mw * dm.d), bf),
                [keep],
                mib=16,
                scratch_shapes=stage(dm.chunks[: dm.early]),
            )
        )
    blocks = jax.ShapeDtypeStruct((dm.chips, dm.rg, LANES), bf)
    same, other = call(
        main_kernel,
        [blocks, blocks],
        operands + [w1, w2, w3, head],
        mib=32,
        scratch_shapes=[
            pltpu.VMEM((dm.rows, dm.lw), bf),
            *stage(dm.chunks[dm.early :]),
            *[pltpu.VMEM((k, c * dm.d), bf) for k, c in zip(depths, columns)],
            *[pltpu.VMEM((m3, c * dm.d), f32) for c in columns],
            pltpu.VMEM((dm.h, dm.bw, dm.d), f32),
        ],
    )
    theirs = lax.ppermute(other, "disp", [(i, i ^ 1) for i in range(n)])
    joined = call(
        join_kernel,
        [jax.ShapeDtypeStruct((2, dm.rg, LANES), bf)] * (dm.chips - 1),
        [same, theirs],
    )
    back = []
    for m in range(1, dm.chips):
        pairs = [(i, i ^ (2 * m)) for i in range(n)]
        back.append(lax.ppermute(joined[m - 1], "disp", pairs))
    return tuple(
        call(
            unpack_kernel,
            [
                jax.ShapeDtypeStruct(left_feat.shape, bf),
                jax.ShapeDtypeStruct((dm.h, dm.strip), f32),
            ],
            [same, theirs] + back,
            scratch_shapes=[pltpu.VMEM((n, dm.rg, LANES), f32)],
        )
    )


def solution(mesh):
    return jax.shard_map(
        shards,
        mesh=mesh,
        in_specs=(P("disp", None, "col"), P("disp", None, "col"), P(), P(), P(), P()),
        out_specs=(P("disp", None, "col"), P(None, "col")),
        check_vma=False,
    )
```

```python
import functools

import jax
import jax.numpy as jnp
from jax import lax
from jax.experimental import pallas as pl
from jax.experimental.pallas import tpu as pltpu
from jax.sharding import PartitionSpec as P


DG = 16
CG = 8
LANES = 128
KROWS = 256
TILE = 8
TERMS = 3
VMEM = pl.BlockSpec(memory_space=pltpu.VMEM)

masked_value = -1e30


def round_up(value, unit):
    return -(-value // unit) * unit


class Dims:
    def __init__(self, left, conv1, conv2, groups_disp, strips):
        own, self.h, self.strip = left
        self.n = groups_disp
        self.strips = strips
        self.own_rows = own * self.h
        self.rows = self.own_rows * self.n
        self.d = DG * self.n
        self.bw = self.strip // self.n
        self.mw = self.bw + 6
        self.tail = self.d + 2
        self.g = conv1[1]
        self.f = conv2[0]
        self.lo = round_up(self.mw + self.d - 1, 8)
        self.lb = self.lo // LANES * LANES
        self.lw = round_up(self.lo + self.mw, LANES)
        self.hops = []
        left_over = self.tail
        while left_over > 0:
            self.hops.append(min(left_over, self.strip))
            left_over -= self.strip
        self.chips = self.n // 2
        self.lo2 = round_up(self.mw + self.bw + self.d - 1, 8)
        self.lw2 = round_up(self.lo2 + self.mw + self.bw, LANES)
        per = KROWS // (CG * self.h)
        self.kept = self.g // 2
        self.full = self.kept // per * per
        rest = 2 * (self.kept - self.full)
        self.split = own % CG == 0 and self.full > 0 and rest <= per and rest * self.h % 16 == 0
        if self.split:
            self.chunks = [per] * (2 * self.full // per) + ([rest] if rest else [])
            self.early = self.full // per
        else:
            self.chunks = [min(per, self.g - k) for k in range(0, self.g, per)]
            self.early = 0
        self.early_rows = sum(self.chunks[: self.early]) * self.h
        self.lg = LANES // self.bw
        self.rg = round_up(-(-(self.own_rows + TERMS * self.h) // self.lg), 8)


def lane_iota(shape):
    return lax.broadcasted_iota(jnp.int32, shape, 1)


def widen(x, lanes):
    have = x.shape[1]
    if have == lanes:
        return x
    return jnp.concatenate([x, jnp.zeros((x.shape[0], lanes - have), x.dtype)], axis=1)


def rolled(x, shift):
    shift %= x.shape[1]
    return x if shift == 0 else pltpu.roll(x, shift, 1)


def flat(ref):
    return ref[...].astype(jnp.float32).reshape(-1, ref.shape[-1])


def copied_in(sources, targets, sems):
    copies = [
        pltpu.make_async_copy(source, target, sems.at[k])
        for k, (source, target) in enumerate(zip(sources, targets))
    ]
    for copy in copies:
        copy.start()
    return [copy.wait for copy in copies]


def edge_kernel(dm, left_hbm, right_hbm, *refs):
    *outs, flat_left_ref, flat_right_ref, left_ref, right_ref, sems = refs
    for wait in copied_in((left_hbm, right_hbm), (left_ref, right_ref), sems):
        wait()
    left, right = flat(left_ref), flat(right_ref)
    flat_left_ref[...] = left.astype(flat_left_ref.dtype)
    flat_right_ref[...] = right.astype(flat_right_ref.dtype)
    width = outs[0].shape[1]
    count = dm.hops[0]
    lane = lane_iota((dm.own_rows, width))
    last = rolled(widen(right, width), count - dm.strip)
    edge = rolled(widen(left, width), count + 3 - dm.strip)
    up = jnp.where(lane < count, last, edge)
    down = jnp.where(lane < 3, widen(right, width), rolled(widen(left, width), 3))
    even = lax.axis_index("col") % 2 == 0
    outs[0][...] = jnp.where(even, up, down).astype(outs[0].dtype)
    outs[1][...] = jnp.where(even, down, up).astype(outs[1].dtype)
    for out, count in zip(outs[2:], dm.hops[1:]):
        out[...] = rolled(right, count - dm.strip)[:, : out.shape[1]].astype(out.dtype)


def pack_kernel(dm, left_ref, right_ref, pair0_ref, pair1_ref, *refs):
    more, outs, windows_ref = refs[: len(dm.hops) - 1], refs[len(dm.hops) - 1 : -1], refs[-1]
    left, right = flat(left_ref), flat(right_ref)
    pair0, pair1 = flat(pair0_ref), flat(pair1_ref)
    even = lax.axis_index("col") % 2 == 0
    up = jnp.where(even, pair1, pair0)
    down = jnp.where(even, pair0, pair1)[:, :LANES]
    ext = max(round_up(dm.tail + dm.strip + 3, LANES), dm.lw2, up.shape[1])
    lane = lane_iota((dm.own_rows, ext))
    row = rolled(widen(right, ext), dm.tail)
    row = jnp.where(lane < dm.tail + dm.strip, row, rolled(widen(down, ext), dm.tail + dm.strip))
    pieces = [up] + [flat(ref) for ref in more]
    for k, count in enumerate(dm.hops):
        start = dm.tail - sum(dm.hops[: k + 1])
        piece = rolled(widen(pieces[k], ext), start)
        row = jnp.where((lane >= start) & (lane < start + count), piece, row)
    lext = max(round_up(dm.strip + 6, LANES), dm.lw2, up.shape[1])
    lane_l = lane_iota((dm.own_rows, lext))
    lrow = rolled(widen(left, lext), 3)
    lrow = jnp.where(lane_l < 3, rolled(widen(up, lext), -dm.hops[0]), lrow)
    lrow = jnp.where(lane_l >= dm.strip + 3, rolled(widen(down, lext), dm.strip), lrow)
    lane_o = lane_iota((dm.own_rows, dm.lw2))
    for q in range(dm.chips):
        a = rolled(row, -2 * dm.bw * q)[:, : dm.lw2]
        b = rolled(lrow, dm.lo2 - 2 * dm.bw * q)[:, : dm.lw2]
        windows_ref[q] = jnp.where(lane_o < dm.lo2, a, b).astype(windows_ref.dtype)
    chip = lax.axis_index("disp") // 2
    for m, out in enumerate(outs):
        out[...] = windows_ref[chip ^ m]


def split_kernel(dm, *refs):
    *windows, keep_ref, give_ref = refs
    first_core = lax.axis_index("disp") % 2 == 0
    for m, ref in enumerate(windows):
        x = flat(ref)
        lane = lane_iota((dm.own_rows, dm.lw))
        parts = []
        for core in range(2):
            a = rolled(x, -core * dm.bw)[:, : dm.lw]
            b = rolled(x, dm.lo - dm.lo2 - core * dm.bw)[:, : dm.lw]
            parts.append(jnp.where(lane < dm.lo, a, b))
        keep_ref[m] = jnp.where(first_core, parts[0], parts[1]).astype(keep_ref.dtype)
        give_ref[m] = jnp.where(first_core, parts[1], parts[0]).astype(give_ref.dtype)


def prep_kernel(dm, *refs):
    outs, targets, sems = refs[4:8], refs[8:12], refs[12]
    waits = copied_in(refs[:4], targets, sems)
    w1_ref, w2_ref, w3_ref, head_ref = targets
    o1_ref, o2_ref, o3_ref, column_ref = outs
    chip, core = lax.axis_index("disp") // 2, lax.axis_index("disp") % 2
    for layer, (w_ref, o_ref) in enumerate(((w1_ref, o1_ref), (w2_ref, o2_ref), (w3_ref, o3_ref))):
        inputs = w_ref.shape[2]
        per_a = dm.h * inputs
        waits[layer]()
        shape = (inputs, 3 * per_a)
        i = lax.broadcasted_iota(jnp.int32, shape, 0)
        if layer == 0 and dm.split:
            per_device = inputs // dm.n
            device = i // per_device
            side = (device % 2) ^ core
            i = ((device // 2) ^ chip) * per_device + i % per_device
            rest = 2 * dm.full + side * (dm.kept - dm.full) + i - dm.full
            i = jnp.where(i < dm.full, side * dm.full + i, rest)
        elif layer == 0:
            per_chip = inputs // dm.chips
            i = ((i // per_chip) ^ chip) * per_chip + i % per_chip
        col = lane_iota(shape)
        total = None
        for a in range(3):
            for hi in range(dm.h):
                if layer == 0:
                    pos = jnp.zeros(shape, jnp.int32)
                    first = 0
                    for count in dm.chunks:
                        here = first * dm.h + hi * count + (i - first)
                        pos = jnp.where(i >= first, here, pos)
                        first += count
                else:
                    pos = hi * inputs + i
                place = jnp.where(col == a * per_a + pos, 1.0, 0.0).astype(jnp.bfloat16)
                blocks = []
                for e in range(3):
                    for ho in range(dm.h):
                        b = hi - ho + 1
                        if 0 <= b <= 2:
                            blocks.append(w_ref[(a * 3 + b) * 3 + e])
                        else:
                            blocks.append(jnp.zeros((dm.f, inputs), jnp.bfloat16))
                term = jnp.dot(
                    jnp.concatenate(blocks, axis=0), place, preferred_element_type=jnp.float32
                )
                total = term if total is None else total + term
        o_ref[...] = total.astype(o_ref.dtype)
    waits[3]()
    square = (dm.f, dm.f)
    eye = lane_iota(square) == lax.broadcasted_iota(jnp.int32, square, 0)
    column = jnp.sum(jnp.where(eye, head_ref[...], 0.0), axis=1, keepdims=True)
    column = jnp.broadcast_to(column, (dm.f, dm.d))
    column_ref[...] = jnp.concatenate([column] * dm.h, axis=0)


def correlator(dm, chunks, x_of, lt_ref, lhs_ref, pc_ref):
    keeps = []
    for count in chunks:
        r, q = count * dm.h, count * CG * dm.h
        lane = lane_iota((r, q))
        sub = lax.broadcasted_iota(jnp.int32, (r, q), 0)
        keeps.append((lane % dm.h == sub // count) & (lane // (CG * dm.h) == sub % count))

    def run(m0, m1):
        first = 0
        for k, count in enumerate(chunks):
            r, q = count * dm.h, count * CG * dm.h
            for m in range(m0, m1):
                at = dm.lo - dm.lb + m
                line = jnp.broadcast_to(lt_ref[at : at + 1, first : first + q], (r, q))
                line = jnp.where(keeps[k], line, 0.0).astype(jnp.bfloat16)
                lhs_ref[k, m * r : (m + 1) * r, :q] = line
            pc_ref[k, m0 * r : m1 * r] = jnp.dot(
                lhs_ref[k, m0 * r : m1 * r, :q], x_of(k), preferred_element_type=jnp.float32
            )
            first += q

    return run


def shifts(v, lanes):
    if v.shape not in lanes:
        lanes[v.shape] = lane_iota(v.shape)
    lane, zero = lanes[v.shape], jnp.zeros_like(v)
    last = v.shape[1] - 1
    return (
        jnp.where(lane < last, rolled(v, -1), zero),
        v,
        jnp.where(lane > 0, rolled(v, 1), zero),
    )


def column_of(dm, chunks, pc_ref, m):
    parts = []
    for k, count in enumerate(chunks):
        r = count * dm.h
        parts.append(pc_ref[k, m * r : (m + 1) * r].astype(jnp.bfloat16))
    return rolled(jnp.concatenate(parts, axis=0), -m)[:, : dm.d]


def left_columns(dm, x):
    return jnp.transpose(x[:, dm.lb :].astype(jnp.float32)) * (1.0 / CG)


def pipeline(stages):
    done = [0] * len(stages)
    while done[-1] < stages[-1][1]:
        before = list(done)
        for k in range(len(stages)):
            run, count, beyond = stages[k]
            ready = count if k == 0 else min(count, before[k - 1] - beyond)
            size = ready - done[k] if ready == count else (ready - done[k]) // TILE * TILE
            size = min(size, TILE)
            if size > 0:
                run(done[k], done[k] + size)
                done[k] += size


def early_kernel(dm, keep_ref, part_ref, lt_ref, lhs_ref, pc_ref):
    chunks = dm.chunks[: dm.early]
    x = keep_ref[...].reshape(-1, dm.lw)
    rows = KROWS * dm.early
    lt_ref[...] = left_columns(dm, x[:rows])
    lanes = {}

    def volume(m0, m1):
        for m in range(m0, m1):
            for a, v in enumerate(shifts(column_of(dm, chunks, pc_ref, m), lanes)):
                part_ref[a, :, m * dm.d : (m + 1) * dm.d] = v

    x_of = lambda k: x[k * KROWS : (k + 1) * KROWS]
    pipeline([(correlator(dm, chunks, x_of, lt_ref, lhs_ref, pc_ref), dm.mw, 0), (volume, dm.mw, 0)])


def main_kernel(dm, keep_ref, got_ref, *refs):
    part_ref, refs = (refs[0], refs[1:]) if dm.split else (None, refs)
    w1_ref, w2_ref, w3_ref, head_ref, same_ref, other_ref, x_ref, lt_ref, lhs_ref, pc_ref = refs[:10]
    a1_ref, a2_ref, a3_ref, p1_ref, p2_ref, p3_ref, s_ref = refs[10:]
    d, mw, h, f, bf = dm.d, dm.mw, dm.h, dm.f, jnp.bfloat16
    core = lax.axis_index("disp") % 2
    base = lax.axis_index("col") * dm.strip + lax.axis_index("disp") * dm.bw
    total = dm.strips * dm.strip
    chunks = dm.chunks[dm.early :]

    if dm.split:
        half, early = dm.rows // 2, KROWS * dm.early
        halves = [ref[...].reshape(half, dm.lw) for ref in (keep_ref, got_ref)]
        sources = [halves[1][k * KROWS : (k + 1) * KROWS] for k in range(dm.early)]
        if early < half:
            sources.append(jnp.concatenate([x[early:] for x in halves], axis=0))
        at = 0
        for x in sources:
            lt_ref[:, at : at + x.shape[0]] = left_columns(dm, x)
            at += x.shape[0]
        x_of = lambda k: sources[k]
    else:
        rows = 2 * dm.own_rows
        for m in range(dm.chips):
            kept, got = flat(keep_ref.at[m]), flat(got_ref.at[m])
            both = [jnp.where(core == 0, kept, got), jnp.where(core == 0, got, kept)]
            both = jnp.concatenate(both, axis=0)
            x_ref[m * rows : (m + 1) * rows] = both.astype(bf)
            lt_ref[:, m * rows : (m + 1) * rows] = left_columns(dm, both)
        x_of = lambda k: x_ref[k * KROWS : k * KROWS + chunks[k] * CG * h]

    lanes = {}

    def spread(ref, m, v, first=0):
        rows = first + v.shape[0]
        for a, shifted in enumerate(shifts(v, lanes)):
            ref[a * rows + first : (a + 1) * rows, m * d : (m + 1) * d] = shifted

    def volume(m0, m1):
        for m in range(m0, m1):
            spread(a1_ref, m, column_of(dm, chunks, pc_ref, m), dm.early_rows)
            if dm.split:
                at = slice(m * d, (m + 1) * d)
                for a in range(3):
                    first = a * h * dm.g
                    a1_ref[first : first + dm.early_rows, at] = part_ref[a, :, at]

    def product(w_ref, a_ref, p_ref):
        def run(m0, m1):
            at = slice(m0 * d, m1 * d)
            p_ref[:, at] = jnp.dot(w_ref[...], a_ref[:, at], preferred_element_type=jnp.float32)

        return run

    def taken(p_ref, emit):
        fh = f * h

        def run(m0, m1):
            for m in range(m0, m1):
                z = p_ref[:fh, m * d : (m + 1) * d]
                z = z + p_ref[fh : 2 * fh, (m + 1) * d : (m + 2) * d]
                z = z + p_ref[2 * fh :, (m + 2) * d : (m + 3) * d]
                emit(m, jnp.maximum(z, 0.0))

        return run

    def activity(a_ref, margin):
        def emit(m, z):
            column = m + margin
            if not 3 <= column < mw - 3:
                at = base - 3 + column
                z = jnp.where((at >= 0) & (at < total), z, 0.0)
            spread(a_ref, m, z.astype(bf))

        return emit

    head = head_ref[...]

    def score(m, z):
        z = z * head
        for row in range(h):
            s_ref[row, m : m + 1, :] = jnp.sum(z[row * f : (row + 1) * f], axis=0, keepdims=True)

    stages = [
        (correlator(dm, chunks, x_of, lt_ref, lhs_ref, pc_ref), mw, 0),
        (volume, mw, 0),
        (product(w1_ref, a1_ref, p1_ref), mw, 0),
        (taken(p1_ref, activity(a2_ref, 1)), mw - 2, 2),
        (product(w2_ref, a2_ref, p2_ref), mw - 2, 0),
        (taken(p2_ref, activity(a3_ref, 2)), mw - 4, 2),
        (product(w3_ref, a3_ref, p3_ref), mw - 4, 0),
        (taken(p3_ref, score), mw - 6, 2),
    ]
    pipeline(stages)

    disp = (d - 1) - lane_iota((dm.bw, d))
    column = base + lax.broadcasted_iota(jnp.int32, (dm.bw, d), 0)
    valid = column >= disp
    disp_f = disp.astype(jnp.float32)
    bands, disparity = [], []
    for row in range(h):
        s = jnp.where(valid, s_ref[row], masked_value)
        top = jnp.max(s, axis=1, keepdims=True)
        weighting = jnp.where(valid, jnp.exp(s - top), 0.0)
        denominator = jnp.sum(weighting, axis=1, keepdims=True)
        disp_sum = jnp.sum(weighting * disp_f, axis=1, keepdims=True)
        disparity.append(disp_sum / denominator / d)
        band = widen(weighting / denominator, dm.lw)
        band = pltpu.roll(band, 3, 1, stride=1, stride_axis=0)
        bands += [band] * dm.lg
    band = jnp.concatenate(bands, axis=0)
    band = band.astype(bf)
    sums = [
        lax.dot_general(x, band, (((1,), (1,)), ((), ())), preferred_element_type=jnp.float32)
        for x in (halves if dm.split else [x_ref[...]])
    ]
    sums = jnp.concatenate(sums, axis=0)
    row = lax.broadcasted_iota(jnp.int32, (dm.rows, LANES), 0) % h
    warped = sums[:, :LANES]
    for k in range(1, h):
        warped = jnp.where(row == k, sums[:, k * LANES : (k + 1) * LANES], warped)

    eye = lane_iota((dm.bw, LANES)) % dm.bw == lax.broadcasted_iota(jnp.int32, (dm.bw, LANES), 0)
    rest = [jnp.sum(jnp.where(eye, v, 0.0), axis=0, keepdims=True) for v in disparity]
    lines = []
    for _ in range(TERMS):
        terms = [v.astype(bf).astype(jnp.float32) for v in rest]
        rest = [v - t for v, t in zip(rest, terms)]
        lines += terms
    lines.append(jnp.zeros((dm.lg * dm.rg - dm.own_rows - len(lines), LANES), jnp.float32))
    lines = jnp.concatenate(lines, axis=0)
    group = lane_iota((dm.rg, LANES)) // dm.bw
    blocks = []
    for j in range(dm.n):
        mine = jnp.concatenate([warped[j * dm.own_rows : (j + 1) * dm.own_rows], lines], axis=0)
        packed = mine[: dm.rg]
        for g in range(1, dm.lg):
            packed = jnp.where(group == g, mine[g * dm.rg : (g + 1) * dm.rg], packed)
        blocks.append(packed)
    for m in range(dm.chips):
        if dm.split:
            same, other = blocks[m], blocks[dm.chips + m]
        else:
            pair = blocks[2 * m : 2 * m + 2]
            same = jnp.where(core == 0, pair[0], pair[1])
            other = jnp.where(core == 0, pair[1], pair[0])
        same_ref[m] = same.astype(same_ref.dtype)
        other_ref[m] = other.astype(other_ref.dtype)


def join_kernel(dm, same_ref, theirs_ref, *outs):
    for m, out in enumerate(outs, 1):
        out[0] = same_ref[m]
        out[1] = theirs_ref[m]


def unpack_kernel(dm, same_ref, theirs_ref, *refs):
    *others, warped_ref, disparity_ref, y_ref = refs
    chip, core = lax.axis_index("disp") // 2, lax.axis_index("disp") % 2
    y_ref[chip * 2 + core] = same_ref[0].astype(jnp.float32)
    y_ref[chip * 2 + 1 - core] = theirs_ref[0].astype(jnp.float32)
    for m, ref in enumerate(others, 1):
        y_ref[(chip ^ m) * 2 + core] = ref[0].astype(jnp.float32)
        y_ref[(chip ^ m) * 2 + 1 - core] = ref[1].astype(jnp.float32)
    per = LANES // dm.bw
    lane = lane_iota((dm.rg, LANES))
    tiles = []
    for t in range(dm.n // per):
        groups = []
        for g in range(dm.lg):
            total = None
            for p in range(per):
                piece = rolled(y_ref[t * per + p], (p - g) * dm.bw)
                keep = (lane >= p * dm.bw) & (lane < (p + 1) * dm.bw)
                total = piece if total is None else jnp.where(keep, piece, total)
            groups.append(total)
        tiles.append(jnp.concatenate(groups, axis=0))
    full = jnp.concatenate(tiles, axis=1)
    warped_ref[...] = full[: dm.own_rows].reshape(warped_ref.shape).astype(warped_ref.dtype)
    total = None
    for k in reversed(range(TERMS)):
        at = dm.own_rows + k * dm.h
        term = full[at : at + dm.h]
        total = term if total is None else term + total
    disparity_ref[...] = total


def shards(left_feat, right_feat, conv1_w, conv2_w, conv3_w, head_w):
    n, strips = lax.axis_size("disp"), lax.axis_size("col")
    dm = Dims(left_feat.shape, conv1_w.shape, conv2_w.shape, n, strips)
    bf, f32 = jnp.bfloat16, jnp.float32

    def call(kernel, out_shape, operands, mib=8, in_hbm=False, **options):
        spec = VMEM
        if in_hbm:
            spec = pl.BlockSpec(memory_space=pltpu.HBM)
            operands = [pltpu.with_memory_space_constraint(v, pltpu.HBM) for v in operands]
        return pl.pallas_call(
            functools.partial(kernel, dm),
            out_shape=out_shape,
            in_specs=[spec] * len(operands),
            out_specs=jax.tree.map(lambda _: VMEM, out_shape),
            compiler_params=pltpu.CompilerParams(vmem_limit_bytes=mib << 20),
            **options,
        )(*operands)

    wide = max(round_up(dm.hops[0] + 3, LANES), dm.strip)
    widths = [wide, wide] + [round_up(c, LANES) for c in dm.hops[1:]]
    *edges, left, right = call(
        edge_kernel,
        [jax.ShapeDtypeStruct((dm.own_rows, w), bf) for w in widths + [dm.strip] * 2],
        [left_feat, right_feat],
        in_hbm=True,
        scratch_shapes=[
            pltpu.VMEM(left_feat.shape, bf),
            pltpu.VMEM(left_feat.shape, bf),
            pltpu.SemaphoreType.DMA((2,)),
        ],
    )
    arrived = []
    for first in range(2):
        pairs = [(s, s + 1) for s in range(first, strips - 1, 2)]
        pairs += [(b, a) for a, b in pairs]
        arrived.append(lax.ppermute(edges[first], "col", pairs))
    for k, e in enumerate(edges[2:], 2):
        arrived.append(lax.ppermute(e, "col", [(s, s + k) for s in range(strips - k)]))

    kernels = [w.transpose(2, 3, 4, 0, 1).reshape(27, w.shape[0], w.shape[1]) for w in (conv1_w, conv2_w, conv3_w)]
    arrived, kernels = lax.optimization_barrier((arrived, kernels))
    m3 = 3 * dm.h * dm.f
    depths = [3 * dm.h * w.shape[2] for w in kernels]
    w1, w2, w3, head = call(
        prep_kernel,
        [jax.ShapeDtypeStruct((m3, k), bf) for k in depths]
        + [jax.ShapeDtypeStruct((dm.h * dm.f, dm.d), f32)],
        kernels + [head_w[None]],
        in_hbm=True,
        scratch_shapes=[pltpu.VMEM(w.shape, bf) for w in kernels]
        + [pltpu.VMEM((1, dm.f), f32), pltpu.SemaphoreType.DMA((4,))],
    )

    own_window, *sent = call(
        pack_kernel,
        [jax.ShapeDtypeStruct((dm.own_rows, dm.lw2), bf)] * dm.chips,
        [left, right] + arrived,
        scratch_shapes=[pltpu.VMEM((dm.chips, dm.own_rows, dm.lw2), bf)],
    )
    windows = [own_window]
    for m in range(1, dm.chips):
        pairs = [(i, i ^ (2 * m)) for i in range(n)]
        windows.append(lax.ppermute(sent[m - 1], "disp", pairs))
    windows, (w1, w2, w3, head) = lax.optimization_barrier((windows, (w1, w2, w3, head)))
    half = jax.ShapeDtypeStruct((dm.chips, dm.own_rows, dm.lw), bf)
    keep, give = call(split_kernel, [half, half], windows)
    got = lax.ppermute(give, "disp", [(i, i ^ 1) for i in range(n)])

    def stage(chunks):
        r = max(chunks) * dm.h
        return [
            pltpu.VMEM((dm.lw - dm.lb, sum(chunks) * CG * dm.h), f32),
            pltpu.VMEM((len(chunks), dm.mw * r, KROWS), bf),
            pltpu.VMEM((len(chunks), dm.mw * r, dm.lw), f32),
        ]

    columns = [dm.mw, dm.mw - 2, dm.mw - 4]
    operands = [keep, got]
    if dm.split:
        operands.append(
            call(
                early_kernel,
                jax.ShapeDtypeStruct((3, dm.early_rows, dm.mw * dm.d), bf),
                [keep],
                mib=16,
                scratch_shapes=stage(dm.chunks[: dm.early]),
            )
        )
    blocks = jax.ShapeDtypeStruct((dm.chips, dm.rg, LANES), bf)
    same, other = call(
        main_kernel,
        [blocks, blocks],
        operands + [w1, w2, w3, head],
        mib=32,
        scratch_shapes=[
            pltpu.VMEM((dm.rows, dm.lw), bf),
            *stage(dm.chunks[dm.early :]),
            *[pltpu.VMEM((k, c * dm.d), bf) for k, c in zip(depths, columns)],
            *[pltpu.VMEM((m3, c * dm.d), f32) for c in columns],
            pltpu.VMEM((dm.h, dm.bw, dm.d), f32),
        ],
    )
    theirs = lax.ppermute(other, "disp", [(i, i ^ 1) for i in range(n)])
    joined = call(
        join_kernel,
        [jax.ShapeDtypeStruct((2, dm.rg, LANES), bf)] * (dm.chips - 1),
        [same, theirs],
    )
    back = []
    for m in range(1, dm.chips):
        pairs = [(i, i ^ (2 * m)) for i in range(n)]
        back.append(lax.ppermute(joined[m - 1], "disp", pairs))
    return tuple(
        call(
            unpack_kernel,
            [
                jax.ShapeDtypeStruct(left_feat.shape, bf),
                jax.ShapeDtypeStruct((dm.h, dm.strip), f32),
            ],
            [same, theirs] + back,
            scratch_shapes=[pltpu.VMEM((n, dm.rg, LANES), f32)],
        )
    )


def solution(mesh):
    return jax.shard_map(
        shards,
        mesh=mesh,
        in_specs=(P("disp", None, "col"), P("disp", None, "col"), P(), P(), P(), P()),
        out_specs=(P("disp", None, "col"), P(None, "col")),
        check_vma=False,
    )
```

```python
import functools

import jax
import jax.numpy as jnp
from jax import lax
from jax.experimental import pallas as pl
from jax.experimental.pallas import tpu as pltpu
from jax.sharding import PartitionSpec as P


DG = 16
CG = 8
LANES = 128
KROWS = 256
TILE = 8
TERMS = 3
VMEM = pl.BlockSpec(memory_space=pltpu.VMEM)

masked_value = -1e30


def round_up(value, unit):
    return -(-value // unit) * unit


class Dims:
    def __init__(self, left, conv1, conv2, groups_disp, strips):
        own, self.h, self.strip = left
        self.n = groups_disp
        self.strips = strips
        self.own_rows = own * self.h
        self.rows = self.own_rows * self.n
        self.d = DG * self.n
        self.bw = self.strip // self.n
        self.mw = self.bw + 6
        self.tail = self.d + 2
        self.g = conv1[1]
        self.f = conv2[0]
        self.lo = round_up(self.mw + self.d - 1, 8)
        self.lb = self.lo // LANES * LANES
        self.lw = round_up(self.lo + self.mw, LANES)
        self.hops = []
        left_over = self.tail
        while left_over > 0:
            self.hops.append(min(left_over, self.strip))
            left_over -= self.strip
        self.chips = self.n // 2
        self.lo2 = round_up(self.mw + self.bw + self.d - 1, 8)
        self.lw2 = round_up(self.lo2 + self.mw + self.bw, LANES)
        per = KROWS // (CG * self.h)
        self.kept = self.g // 2
        self.full = self.kept // per * per
        rest = 2 * (self.kept - self.full)
        self.split = own % CG == 0 and self.full > 0 and rest <= per and rest * self.h % 16 == 0
        if self.split:
            self.chunks = [per] * (2 * self.full // per) + ([rest] if rest else [])
            self.early = self.full // per
        else:
            self.chunks = [min(per, self.g - k) for k in range(0, self.g, per)]
            self.early = 0
        self.early_rows = sum(self.chunks[: self.early]) * self.h
        self.lg = LANES // self.bw
        self.rg = round_up(-(-(self.own_rows + TERMS * self.h) // self.lg), 8)


def lane_iota(shape):
    return lax.broadcasted_iota(jnp.int32, shape, 1)


def widen(x, lanes):
    have = x.shape[1]
    if have == lanes:
        return x
    return jnp.concatenate([x, jnp.zeros((x.shape[0], lanes - have), x.dtype)], axis=1)


def rolled(x, shift):
    shift %= x.shape[1]
    return x if shift == 0 else pltpu.roll(x, shift, 1)


def flat(ref):
    return ref[...].astype(jnp.float32).reshape(-1, ref.shape[-1])


def copied_in(sources, targets, sems):
    copies = [
        pltpu.make_async_copy(source, target, sems.at[k])
        for k, (source, target) in enumerate(zip(sources, targets))
    ]
    for copy in copies:
        copy.start()
    return [copy.wait for copy in copies]


def edge_kernel(dm, left_hbm, right_hbm, *refs):
    *outs, left_ref, right_ref, sems = refs
    for wait in copied_in((left_hbm, right_hbm), (left_ref, right_ref), sems):
        wait()
    left, right = flat(left_ref), flat(right_ref)
    width = outs[0].shape[1]
    count = dm.hops[0]
    lane = lane_iota((dm.own_rows, width))
    last = rolled(widen(right, width), count - dm.strip)
    edge = rolled(widen(left, width), count + 3 - dm.strip)
    up = jnp.where(lane < count, last, edge)
    down = jnp.where(lane < 3, widen(right, width), rolled(widen(left, width), 3))
    even = lax.axis_index("col") % 2 == 0
    outs[0][...] = jnp.where(even, up, down).astype(outs[0].dtype)
    outs[1][...] = jnp.where(even, down, up).astype(outs[1].dtype)
    for out, count in zip(outs[2:], dm.hops[1:]):
        out[...] = rolled(right, count - dm.strip)[:, : out.shape[1]].astype(out.dtype)


def flat_kernel(dm, left_hbm, right_hbm, *refs):
    *outs, left_ref, right_ref, sems = refs
    sources = (left_ref, right_ref)
    for wait, out, ref in zip(copied_in((left_hbm, right_hbm), sources, sems), outs, sources):
        wait()
        out[...] = flat(ref).astype(out.dtype)


def pack_kernel(dm, left_ref, right_ref, pair0_ref, pair1_ref, *refs):
    more, outs, windows_ref = refs[: len(dm.hops) - 1], refs[len(dm.hops) - 1 : -1], refs[-1]
    left, right = flat(left_ref), flat(right_ref)
    pair0, pair1 = flat(pair0_ref), flat(pair1_ref)
    even = lax.axis_index("col") % 2 == 0
    up = jnp.where(even, pair1, pair0)
    down = jnp.where(even, pair0, pair1)[:, :LANES]
    ext = max(round_up(dm.tail + dm.strip + 3, LANES), dm.lw2, up.shape[1])
    lane = lane_iota((dm.own_rows, ext))
    row = rolled(widen(right, ext), dm.tail)
    row = jnp.where(lane < dm.tail + dm.strip, row, rolled(widen(down, ext), dm.tail + dm.strip))
    pieces = [up] + [flat(ref) for ref in more]
    for k, count in enumerate(dm.hops):
        start = dm.tail - sum(dm.hops[: k + 1])
        piece = rolled(widen(pieces[k], ext), start)
        row = jnp.where((lane >= start) & (lane < start + count), piece, row)
    lext = max(round_up(dm.strip + 6, LANES), dm.lw2, up.shape[1])
    lane_l = lane_iota((dm.own_rows, lext))
    lrow = rolled(widen(left, lext), 3)
    lrow = jnp.where(lane_l < 3, rolled(widen(up, lext), -dm.hops[0]), lrow)
    lrow = jnp.where(lane_l >= dm.strip + 3, rolled(widen(down, lext), dm.strip), lrow)
    lane_o = lane_iota((dm.own_rows, dm.lw2))
    for q in range(dm.chips):
        a = rolled(row, -2 * dm.bw * q)[:, : dm.lw2]
        b = rolled(lrow, dm.lo2 - 2 * dm.bw * q)[:, : dm.lw2]
        windows_ref[q] = jnp.where(lane_o < dm.lo2, a, b).astype(windows_ref.dtype)
    chip = lax.axis_index("disp") // 2
    for m, out in enumerate(outs):
        out[...] = windows_ref[chip ^ m]


def split_kernel(dm, *refs):
    *windows, keep_ref, give_ref = refs
    first_core = lax.axis_index("disp") % 2 == 0
    for m, ref in enumerate(windows):
        x = flat(ref)
        lane = lane_iota((dm.own_rows, dm.lw))
        parts = []
        for core in range(2):
            a = rolled(x, -core * dm.bw)[:, : dm.lw]
            b = rolled(x, dm.lo - dm.lo2 - core * dm.bw)[:, : dm.lw]
            parts.append(jnp.where(lane < dm.lo, a, b))
        keep_ref[m] = jnp.where(first_core, parts[0], parts[1]).astype(keep_ref.dtype)
        give_ref[m] = jnp.where(first_core, parts[1], parts[0]).astype(give_ref.dtype)


def prep_kernel(dm, *refs):
    outs, targets, sems = refs[4:8], refs[8:12], refs[12]
    waits = copied_in(refs[:4], targets, sems)
    w1_ref, w2_ref, w3_ref, head_ref = targets
    o1_ref, o2_ref, o3_ref, column_ref = outs
    chip, core = lax.axis_index("disp") // 2, lax.axis_index("disp") % 2
    for layer, (w_ref, o_ref) in enumerate(((w1_ref, o1_ref), (w2_ref, o2_ref), (w3_ref, o3_ref))):
        inputs = w_ref.shape[2]
        per_a = dm.h * inputs
        waits[layer]()
        shape = (inputs, 3 * per_a)
        i = lax.broadcasted_iota(jnp.int32, shape, 0)
        if layer == 0 and dm.split:
            per_device = inputs // dm.n
            device = i // per_device
            side = (device % 2) ^ core
            i = ((device // 2) ^ chip) * per_device + i % per_device
            rest = 2 * dm.full + side * (dm.kept - dm.full) + i - dm.full
            i = jnp.where(i < dm.full, side * dm.full + i, rest)
        elif layer == 0:
            per_chip = inputs // dm.chips
            i = ((i // per_chip) ^ chip) * per_chip + i % per_chip
        col = lane_iota(shape)
        total = None
        for a in range(3):
            for hi in range(dm.h):
                if layer == 0:
                    pos = jnp.zeros(shape, jnp.int32)
                    first = 0
                    for count in dm.chunks:
                        here = first * dm.h + hi * count + (i - first)
                        pos = jnp.where(i >= first, here, pos)
                        first += count
                else:
                    pos = hi * inputs + i
                place = jnp.where(col == a * per_a + pos, 1.0, 0.0).astype(jnp.bfloat16)
                blocks = []
                for e in range(3):
                    for ho in range(dm.h):
                        b = hi - ho + 1
                        if 0 <= b <= 2:
                            blocks.append(w_ref[(a * 3 + b) * 3 + e])
                        else:
                            blocks.append(jnp.zeros((dm.f, inputs), jnp.bfloat16))
                term = jnp.dot(
                    jnp.concatenate(blocks, axis=0), place, preferred_element_type=jnp.float32
                )
                total = term if total is None else total + term
        o_ref[...] = total.astype(o_ref.dtype)
    waits[3]()
    square = (dm.f, dm.f)
    eye = lane_iota(square) == lax.broadcasted_iota(jnp.int32, square, 0)
    column = jnp.sum(jnp.where(eye, head_ref[...], 0.0), axis=1, keepdims=True)
    column = jnp.broadcast_to(column, (dm.f, dm.d))
    column_ref[...] = jnp.concatenate([column] * dm.h, axis=0)


def correlator(dm, chunks, x_of, lt_ref, lhs_ref, pc_ref):
    keeps = []
    for count in chunks:
        r, q = count * dm.h, count * CG * dm.h
        lane = lane_iota((r, q))
        sub = lax.broadcasted_iota(jnp.int32, (r, q), 0)
        keeps.append((lane % dm.h == sub // count) & (lane // (CG * dm.h) == sub % count))

    def run(m0, m1):
        first = 0
        for k, count in enumerate(chunks):
            r, q = count * dm.h, count * CG * dm.h
            for m in range(m0, m1):
                at = dm.lo - dm.lb + m
                line = jnp.broadcast_to(lt_ref[at : at + 1, first : first + q], (r, q))
                line = jnp.where(keeps[k], line, 0.0).astype(jnp.bfloat16)
                lhs_ref[k, m * r : (m + 1) * r, :q] = line
            pc_ref[k, m0 * r : m1 * r] = jnp.dot(
                lhs_ref[k, m0 * r : m1 * r, :q], x_of(k), preferred_element_type=jnp.float32
            )
            first += q

    return run


def shifts(v, lanes):
    if v.shape not in lanes:
        lanes[v.shape] = lane_iota(v.shape)
    lane, zero = lanes[v.shape], jnp.zeros_like(v)
    last = v.shape[1] - 1
    return (
        jnp.where(lane < last, rolled(v, -1), zero),
        v,
        jnp.where(lane > 0, rolled(v, 1), zero),
    )


def column_of(dm, chunks, pc_ref, m):
    parts = []
    for k, count in enumerate(chunks):
        r = count * dm.h
        parts.append(pc_ref[k, m * r : (m + 1) * r].astype(jnp.bfloat16))
    return rolled(jnp.concatenate(parts, axis=0), -m)[:, : dm.d]


def left_columns(dm, x):
    return jnp.transpose(x[:, dm.lb :].astype(jnp.float32)) * (1.0 / CG)


def pipeline(stages):
    done = [0] * len(stages)
    while done[-1] < stages[-1][1]:
        before = list(done)
        for k in range(len(stages)):
            run, count, beyond = stages[k]
            ready = count if k == 0 else min(count, before[k - 1] - beyond)
            size = ready - done[k] if ready == count else (ready - done[k]) // TILE * TILE
            size = min(size, TILE)
            if size > 0:
                run(done[k], done[k] + size)
                done[k] += size


def early_kernel(dm, keep_ref, part_ref, lt_ref, lhs_ref, pc_ref):
    chunks = dm.chunks[: dm.early]
    x = keep_ref[...].reshape(-1, dm.lw)
    rows = KROWS * dm.early
    lt_ref[...] = left_columns(dm, x[:rows])
    lanes = {}

    def volume(m0, m1):
        for m in range(m0, m1):
            for a, v in enumerate(shifts(column_of(dm, chunks, pc_ref, m), lanes)):
                part_ref[a, :, m * dm.d : (m + 1) * dm.d] = v

    x_of = lambda k: x[k * KROWS : (k + 1) * KROWS]
    pipeline([(correlator(dm, chunks, x_of, lt_ref, lhs_ref, pc_ref), dm.mw, 0), (volume, dm.mw, 0)])


def main_kernel(dm, keep_ref, got_ref, *refs):
    part_ref, refs = (refs[0], refs[1:]) if dm.split else (None, refs)
    w1_ref, w2_ref, w3_ref, head_ref, same_ref, other_ref, x_ref, lt_ref, lhs_ref, pc_ref = refs[:10]
    a1_ref, a2_ref, a3_ref, p1_ref, p2_ref, p3_ref, s_ref = refs[10:]
    d, mw, h, f, bf = dm.d, dm.mw, dm.h, dm.f, jnp.bfloat16
    core = lax.axis_index("disp") % 2
    base = lax.axis_index("col") * dm.strip + lax.axis_index("disp") * dm.bw
    total = dm.strips * dm.strip
    chunks = dm.chunks[dm.early :]

    if dm.split:
        half, early = dm.rows // 2, KROWS * dm.early
        halves = [ref[...].reshape(half, dm.lw) for ref in (keep_ref, got_ref)]
        sources = [halves[1][k * KROWS : (k + 1) * KROWS] for k in range(dm.early)]
        if early < half:
            sources.append(jnp.concatenate([x[early:] for x in halves], axis=0))
        at = 0
        for x in sources:
            lt_ref[:, at : at + x.shape[0]] = left_columns(dm, x)
            at += x.shape[0]
        x_of = lambda k: sources[k]
    else:
        rows = 2 * dm.own_rows
        for m in range(dm.chips):
            kept, got = flat(keep_ref.at[m]), flat(got_ref.at[m])
            both = [jnp.where(core == 0, kept, got), jnp.where(core == 0, got, kept)]
            both = jnp.concatenate(both, axis=0)
            x_ref[m * rows : (m + 1) * rows] = both.astype(bf)
            lt_ref[:, m * rows : (m + 1) * rows] = left_columns(dm, both)
        x_of = lambda k: x_ref[k * KROWS : k * KROWS + chunks[k] * CG * h]

    lanes = {}

    def spread(ref, m, v, first=0):
        rows = first + v.shape[0]
        for a, shifted in enumerate(shifts(v, lanes)):
            ref[a * rows + first : (a + 1) * rows, m * d : (m + 1) * d] = shifted

    def volume(m0, m1):
        for m in range(m0, m1):
            spread(a1_ref, m, column_of(dm, chunks, pc_ref, m), dm.early_rows)
            if dm.split:
                at = slice(m * d, (m + 1) * d)
                for a in range(3):
                    first = a * h * dm.g
                    a1_ref[first : first + dm.early_rows, at] = part_ref[a, :, at]

    def product(w_ref, a_ref, p_ref):
        def run(m0, m1):
            at = slice(m0 * d, m1 * d)
            p_ref[:, at] = jnp.dot(w_ref[...], a_ref[:, at], preferred_element_type=jnp.float32)

        return run

    def taken(p_ref, emit):
        fh = f * h

        def run(m0, m1):
            for m in range(m0, m1):
                z = p_ref[:fh, m * d : (m + 1) * d]
                z = z + p_ref[fh : 2 * fh, (m + 1) * d : (m + 2) * d]
                z = z + p_ref[2 * fh :, (m + 2) * d : (m + 3) * d]
                emit(m, jnp.maximum(z, 0.0))

        return run

    def activity(a_ref, margin):
        def emit(m, z):
            column = m + margin
            if not 3 <= column < mw - 3:
                at = base - 3 + column
                z = jnp.where((at >= 0) & (at < total), z, 0.0)
            spread(a_ref, m, z.astype(bf))

        return emit

    head = head_ref[...]

    def score(m, z):
        z = z * head
        for row in range(h):
            s_ref[row, m : m + 1, :] = jnp.sum(z[row * f : (row + 1) * f], axis=0, keepdims=True)

    stages = [
        (correlator(dm, chunks, x_of, lt_ref, lhs_ref, pc_ref), mw, 0),
        (volume, mw, 0),
        (product(w1_ref, a1_ref, p1_ref), mw, 0),
        (taken(p1_ref, activity(a2_ref, 1)), mw - 2, 2),
        (product(w2_ref, a2_ref, p2_ref), mw - 2, 0),
        (taken(p2_ref, activity(a3_ref, 2)), mw - 4, 2),
        (product(w3_ref, a3_ref, p3_ref), mw - 4, 0),
        (taken(p3_ref, score), mw - 6, 2),
    ]
    pipeline(stages)

    disp = (d - 1) - lane_iota((dm.bw, d))
    column = base + lax.broadcasted_iota(jnp.int32, (dm.bw, d), 0)
    valid = column >= disp
    disp_f = disp.astype(jnp.float32)
    bands, disparity = [], []
    for row in range(h):
        s = jnp.where(valid, s_ref[row], masked_value)
        top = jnp.max(s, axis=1, keepdims=True)
        weighting = jnp.where(valid, jnp.exp(s - top), 0.0)
        denominator = jnp.sum(weighting, axis=1, keepdims=True)
        disp_sum = jnp.sum(weighting * disp_f, axis=1, keepdims=True)
        disparity.append(disp_sum / denominator / d)
        band = widen(weighting / denominator, dm.lw)
        band = pltpu.roll(band, 3, 1, stride=1, stride_axis=0)
        bands += [band] * dm.lg
    band = jnp.concatenate(bands, axis=0)
    band = band.astype(bf)
    sums = [
        lax.dot_general(x, band, (((1,), (1,)), ((), ())), preferred_element_type=jnp.float32)
        for x in (halves if dm.split else [x_ref[...]])
    ]
    sums = jnp.concatenate(sums, axis=0)
    row = lax.broadcasted_iota(jnp.int32, (dm.rows, LANES), 0) % h
    warped = sums[:, :LANES]
    for k in range(1, h):
        warped = jnp.where(row == k, sums[:, k * LANES : (k + 1) * LANES], warped)

    eye = lane_iota((dm.bw, LANES)) % dm.bw == lax.broadcasted_iota(jnp.int32, (dm.bw, LANES), 0)
    rest = [jnp.sum(jnp.where(eye, v, 0.0), axis=0, keepdims=True) for v in disparity]
    lines = []
    for _ in range(TERMS):
        terms = [v.astype(bf).astype(jnp.float32) for v in rest]
        rest = [v - t for v, t in zip(rest, terms)]
        lines += terms
    lines.append(jnp.zeros((dm.lg * dm.rg - dm.own_rows - len(lines), LANES), jnp.float32))
    lines = jnp.concatenate(lines, axis=0)
    group = lane_iota((dm.rg, LANES)) // dm.bw
    blocks = []
    for j in range(dm.n):
        mine = jnp.concatenate([warped[j * dm.own_rows : (j + 1) * dm.own_rows], lines], axis=0)
        packed = mine[: dm.rg]
        for g in range(1, dm.lg):
            packed = jnp.where(group == g, mine[g * dm.rg : (g + 1) * dm.rg], packed)
        blocks.append(packed)
    for m in range(dm.chips):
        if dm.split:
            same, other = blocks[m], blocks[dm.chips + m]
        else:
            pair = blocks[2 * m : 2 * m + 2]
            same = jnp.where(core == 0, pair[0], pair[1])
            other = jnp.where(core == 0, pair[1], pair[0])
        same_ref[m] = same.astype(same_ref.dtype)
        other_ref[m] = other.astype(other_ref.dtype)


def join_kernel(dm, same_ref, theirs_ref, *outs):
    for m, out in enumerate(outs, 1):
        out[0] = same_ref[m]
        out[1] = theirs_ref[m]


def unpack_kernel(dm, same_ref, theirs_ref, *refs):
    *others, warped_ref, disparity_ref, y_ref = refs
    chip, core = lax.axis_index("disp") // 2, lax.axis_index("disp") % 2
    y_ref[chip * 2 + core] = same_ref[0].astype(jnp.float32)
    y_ref[chip * 2 + 1 - core] = theirs_ref[0].astype(jnp.float32)
    for m, ref in enumerate(others, 1):
        y_ref[(chip ^ m) * 2 + core] = ref[0].astype(jnp.float32)
        y_ref[(chip ^ m) * 2 + 1 - core] = ref[1].astype(jnp.float32)
    per = LANES // dm.bw
    lane = lane_iota((dm.rg, LANES))
    tiles = []
    for t in range(dm.n // per):
        groups = []
        for g in range(dm.lg):
            total = None
            for p in range(per):
                piece = rolled(y_ref[t * per + p], (p - g) * dm.bw)
                keep = (lane >= p * dm.bw) & (lane < (p + 1) * dm.bw)
                total = piece if total is None else jnp.where(keep, piece, total)
            groups.append(total)
        tiles.append(jnp.concatenate(groups, axis=0))
    full = jnp.concatenate(tiles, axis=1)
    warped_ref[...] = full[: dm.own_rows].reshape(warped_ref.shape).astype(warped_ref.dtype)
    total = None
    for k in reversed(range(TERMS)):
        at = dm.own_rows + k * dm.h
        term = full[at : at + dm.h]
        total = term if total is None else term + total
    disparity_ref[...] = total


def shards(left_feat, right_feat, conv1_w, conv2_w, conv3_w, head_w):
    n, strips = lax.axis_size("disp"), lax.axis_size("col")
    dm = Dims(left_feat.shape, conv1_w.shape, conv2_w.shape, n, strips)
    bf, f32 = jnp.bfloat16, jnp.float32

    def call(kernel, out_shape, operands, mib=8, in_hbm=False, **options):
        spec = VMEM
        if in_hbm:
            spec = pl.BlockSpec(memory_space=pltpu.HBM)
            operands = [pltpu.with_memory_space_constraint(v, pltpu.HBM) for v in operands]
        return pl.pallas_call(
            functools.partial(kernel, dm),
            out_shape=out_shape,
            in_specs=[spec] * len(operands),
            out_specs=jax.tree.map(lambda _: VMEM, out_shape),
            compiler_params=pltpu.CompilerParams(vmem_limit_bytes=mib << 20),
            **options,
        )(*operands)

    wide = max(round_up(dm.hops[0] + 3, LANES), dm.strip)
    widths = [wide, wide] + [round_up(c, LANES) for c in dm.hops[1:]]
    landing = [
        pltpu.VMEM(left_feat.shape, bf),
        pltpu.VMEM(left_feat.shape, bf),
        pltpu.SemaphoreType.DMA((2,)),
    ]
    features = [left_feat, right_feat]
    shapes = [jax.ShapeDtypeStruct((dm.own_rows, w), bf) for w in widths]
    edges = call(edge_kernel, shapes, features, in_hbm=True, scratch_shapes=landing)
    shapes = [jax.ShapeDtypeStruct((dm.own_rows, dm.strip), bf)] * 2
    left, right = call(flat_kernel, shapes, features, in_hbm=True, scratch_shapes=landing)
    arrived = []
    for first in range(2):
        pairs = [(s, s + 1) for s in range(first, strips - 1, 2)]
        pairs += [(b, a) for a, b in pairs]
        arrived.append(lax.ppermute(edges[first], "col", pairs))
    for k, e in enumerate(edges[2:], 2):
        arrived.append(lax.ppermute(e, "col", [(s, s + k) for s in range(strips - k)]))

    kernels = [w.transpose(2, 3, 4, 0, 1).reshape(27, w.shape[0], w.shape[1]) for w in (conv1_w, conv2_w, conv3_w)]
    arrived, kernels = lax.optimization_barrier((arrived, kernels))
    m3 = 3 * dm.h * dm.f
    depths = [3 * dm.h * w.shape[2] for w in kernels]
    w1, w2, w3, head = call(
        prep_kernel,
        [jax.ShapeDtypeStruct((m3, k), bf) for k in depths]
        + [jax.ShapeDtypeStruct((dm.h * dm.f, dm.d), f32)],
        kernels + [head_w[None]],
        in_hbm=True,
        scratch_shapes=[pltpu.VMEM(w.shape, bf) for w in kernels]
        + [pltpu.VMEM((1, dm.f), f32), pltpu.SemaphoreType.DMA((4,))],
    )

    own_window, *sent = call(
        pack_kernel,
        [jax.ShapeDtypeStruct((dm.own_rows, dm.lw2), bf)] * dm.chips,
        [left, right] + arrived,
        scratch_shapes=[pltpu.VMEM((dm.chips, dm.own_rows, dm.lw2), bf)],
    )
    windows = [own_window]
    for m in range(1, dm.chips):
        pairs = [(i, i ^ (2 * m)) for i in range(n)]
        windows.append(lax.ppermute(sent[m - 1], "disp", pairs))
    windows, (w1, w2, w3, head) = lax.optimization_barrier((windows, (w1, w2, w3, head)))
    half = jax.ShapeDtypeStruct((dm.chips, dm.own_rows, dm.lw), bf)
    keep, give = call(split_kernel, [half, half], windows)
    got = lax.ppermute(give, "disp", [(i, i ^ 1) for i in range(n)])

    def stage(chunks):
        r = max(chunks) * dm.h
        return [
            pltpu.VMEM((dm.lw - dm.lb, sum(chunks) * CG * dm.h), f32),
            pltpu.VMEM((len(chunks), dm.mw * r, KROWS), bf),
            pltpu.VMEM((len(chunks), dm.mw * r, dm.lw), f32),
        ]

    columns = [dm.mw, dm.mw - 2, dm.mw - 4]
    operands = [keep, got]
    if dm.split:
        operands.append(
            call(
                early_kernel,
                jax.ShapeDtypeStruct((3, dm.early_rows, dm.mw * dm.d), bf),
                [keep],
                mib=16,
                scratch_shapes=stage(dm.chunks[: dm.early]),
            )
        )
    blocks = jax.ShapeDtypeStruct((dm.chips, dm.rg, LANES), bf)
    same, other = call(
        main_kernel,
        [blocks, blocks],
        operands + [w1, w2, w3, head],
        mib=32,
        scratch_shapes=[
            pltpu.VMEM((dm.rows, dm.lw), bf),
            *stage(dm.chunks[dm.early :]),
            *[pltpu.VMEM((k, c * dm.d), bf) for k, c in zip(depths, columns)],
            *[pltpu.VMEM((m3, c * dm.d), f32) for c in columns],
            pltpu.VMEM((dm.h, dm.bw, dm.d), f32),
        ],
    )
    theirs = lax.ppermute(other, "disp", [(i, i ^ 1) for i in range(n)])
    joined = call(
        join_kernel,
        [jax.ShapeDtypeStruct((2, dm.rg, LANES), bf)] * (dm.chips - 1),
        [same, theirs],
    )
    back = []
    for m in range(1, dm.chips):
        pairs = [(i, i ^ (2 * m)) for i in range(n)]
        back.append(lax.ppermute(joined[m - 1], "disp", pairs))
    return tuple(
        call(
            unpack_kernel,
            [
                jax.ShapeDtypeStruct(left_feat.shape, bf),
                jax.ShapeDtypeStruct((dm.h, dm.strip), f32),
            ],
            [same, theirs] + back,
            scratch_shapes=[pltpu.VMEM((n, dm.rg, LANES), f32)],
        )
    )


def solution(mesh):
    return jax.shard_map(
        shards,
        mesh=mesh,
        in_specs=(P("disp", None, "col"), P("disp", None, "col"), P(), P(), P(), P()),
        out_specs=(P("disp", None, "col"), P(None, "col")),
        check_vma=False,
    )
```
